256 devices in a mesh: group: 16 (over z, core), inner: 16 (over y, x).
Axes of the slice: x: 4, y: 4, z: 8, core: 2. Of those that a mesh axis runs over, the one named last changes fastest.
Arguments:
- leaf_blocks: float32 [65536, 256], P(('group', 'inner')), may hold values from -3 to 3, as said below
- bases: float32 [65536, 512], P(('group', 'inner')), may hold values from -2 to 2
- targets: float32 [65536, 128], P(('group', 'inner')), may hold values from -30 to 30
- coupling: float32 [8, 64], replicated, may hold values from 0.01 to 1
Outputs:
- solution: float32 [65536, 128], P(('group', 'inner'))
The draws below stay inside these ranges and needn't reach their ends.
Inputs may be any that keep to these rules, and one draw needn't show every extreme that they name: Each leaf block of leaf_blocks is symmetric with all eigenvalues at least 0.4.
All inputs are finite; a program needn't handle non-finite values.
Results may differ from the reference program's by a relative error of at most 0.00014.
Values sent between devices are 32-bit elements; how exact they have to be, the bound alone decides.
No kernel may reach another device: no remote copies, remote signals or barrier semaphores. Data moves between devices by JAX's collectives and lax.ppermute only.
A program may use at most 64 MiB of HBM per device.

```python
import math
import jax
import jax.numpy as jnp
from jax import lax

M = 256
R = 64
NRHS = 128
LEVELS = 8
BLOCKS = 256
NPTS = 65536


def shared_draw(key):
    scale_key = jax.random.fold_in(key, 101)
    basis_key = jax.random.fold_in(key, 202)
    noise_key = jax.random.fold_in(key, 303)
    latent_key = jax.random.fold_in(key, 404)
    scales = jnp.exp(jax.random.uniform(scale_key, (BLOCKS, 1, LEVELS, 1), jnp.float32, math.log(0.5), math.log(2.0)))
    entries = jnp.clip(jax.random.normal(basis_key, (BLOCKS, M, LEVELS, R), jnp.float32), -5.0, 5.0)
    level_bases = jnp.clip(entries * scales / math.sqrt(M), -2.0, 2.0)
    bases_out = level_bases.reshape(NPTS, LEVELS * R)
    targets_out = jnp.clip(jax.random.normal(noise_key, (NPTS, NRHS), jnp.float32), -6.0, 6.0)
    for current in range(LEVELS):
        node_count = BLOCKS // 2 ** (current + 1)
        level_basis = level_bases[:, :, current, :].reshape(node_count, -1, R)
        latent = 2.0 * jnp.clip(jax.random.normal(jax.random.fold_in(latent_key, current), (node_count, R, NRHS), jnp.float32), -5.0, 5.0)
        targets_out = targets_out + jnp.einsum('nsr,nrc->nsc', level_basis, latent).reshape(NPTS, NRHS)
    return (bases_out, jnp.clip(targets_out, -30.0, 30.0))


def draw_bases(key, part):
    return shared_draw(key)[0]


def draw_targets(key, part):
    return shared_draw(key)[1]


def draw_leaf_blocks(key, part):
    sym_key = jax.random.fold_in(key, 505)
    diag_key = jax.random.fold_in(key, 606)
    raw_part = jnp.clip(jax.random.normal(sym_key, (BLOCKS, M, M), jnp.float32), -5.0, 5.0)
    diagonal = jax.random.uniform(diag_key, (BLOCKS, M), jnp.float32, 1.5, 2.5)
    symmetric = (raw_part + jnp.swapaxes(raw_part, 1, 2)) * (0.35 / math.sqrt(M))
    identity = jnp.eye(M, dtype=jnp.float32)
    return (symmetric + diagonal[:, :, None] * identity).reshape(NPTS, M)


def setup_inputs(seed: int = 0) -> dict:
    splits = jax.random.split(jax.random.key(seed), 5)
    return {
        "leaf_blocks": draw_leaf_blocks(jax.random.fold_in(splits[4], 71), 0),
        "bases": draw_bases(jax.random.fold_in(splits[4], 71), 0),
        "targets": draw_targets(jax.random.fold_in(splits[4], 71), 0),
        "coupling": jnp.clip(jnp.exp(jax.random.uniform(splits[3], (LEVELS, R), jnp.float32, math.log(0.01), math.log(1.0))), 0.01, 1.0),
    }


def chol_solve(factor, rhs_cols):
    forward = lax.linalg.triangular_solve(factor, rhs_cols, left_side=True, lower=True)
    return lax.linalg.triangular_solve(factor, forward, left_side=True, lower=True, transpose_a=True)

def coefficients(gram_part, weights, projected):
    capacity = gram_part + jnp.diag(1.0 / weights)
    capacity = 0.5 * (capacity + capacity.T)
    return chol_solve(jnp.linalg.cholesky(capacity), projected)

def leaf_solve(item_pair):
    block_rows, rhs_cols = item_pair
    return chol_solve(jnp.linalg.cholesky(block_rows), rhs_cols)

def reference(leaf_blocks, bases, targets, coupling):
    blocks = leaf_blocks.reshape(BLOCKS, M, M)
    columns = jnp.concatenate([bases, targets], axis=1).reshape(BLOCKS, M, LEVELS * R + NRHS)
    solved = lax.map(leaf_solve, (blocks, columns)).reshape(NPTS, LEVELS * R + NRHS)
    for current in range(LEVELS):
        node_count = BLOCKS // 2 ** (current + 1)
        width_now = solved.shape[1]
        level_basis = bases[:, current * R:(current + 1) * R].reshape(node_count, -1, R)
        grouped = solved.reshape(node_count, -1, width_now)
        node_sum = jnp.einsum('nsr,nsc->nrc', level_basis, grouped, precision=lax.Precision.HIGHEST)
        solve_coef = jax.vmap(coefficients, in_axes=(0, None, 0))(node_sum[:, :, :R], coupling[current], node_sum[:, :, R:])
        remaining = grouped[:, :, R:] - jnp.einsum('nsr,nrc->nsc', grouped[:, :, :R], solve_coef, precision=lax.Precision.HIGHEST)
        solved = remaining.reshape(NPTS, width_now - R)
    return solved
```

```python
import jax
import jax.numpy as jnp
from jax import lax
from jax.experimental import pallas as pl
from jax.experimental.pallas import tpu as pltpu
from jax.sharding import PartitionSpec as P

M = 256
R = 64
LEVELS = 8
NRHS = 128
WIDTH = LEVELS * R + NRHS
F32 = jnp.float32
HI = lax.Precision.HIGHEST


def start_of(level):
    return 128 * ((level - 1) // 2)


def width_of(level):
    return WIDTH - start_of(level)


def offsets(first):
    out, at = {}, 0
    for level in range(first, LEVELS + 1):
        out[level] = at
        at += width_of(level)
    return out, at


def mm(a, b):
    return lax.dot_general(a, b, (((1,), (0,)), ((), ())), precision=HI, preferred_element_type=F32)


def mm_t(a, b):
    return lax.dot_general(a, b, (((0,), (0,)), ((), ())), precision=HI, preferred_element_type=F32)


def chol_inverse(sym):
    row_ids = lax.broadcasted_iota(jnp.int32, (8, 128), 0)
    lane_ids = lax.broadcasted_iota(jnp.int32, (8, 128), 1)
    tiles = []
    for t in range(8):
        eye = jnp.where(lane_ids == row_ids + (R + 8 * t), 1.0, 0.0)[:, R:]
        tiles.append(jnp.concatenate([sym[8 * t : 8 * t + 8, :], eye], axis=1))
    for i in range(R):
        ti, s = i // 8, i % 8
        head = tiles[ti]
        col = jnp.broadcast_to(head[:, i : i + 1], (8, 128))
        scale = lax.rsqrt(jnp.broadcast_to(col[s : s + 1, :], (8, 128)))
        row = jnp.broadcast_to(head[s : s + 1, :], (8, 128)) * scale
        below = jnp.where(row_ids > s, col, 0.0) * scale
        tiles[ti] = jnp.where(row_ids == s, row, head - below * row)
        for t in range(ti + 1, 8):
            col_t = jnp.broadcast_to(tiles[t][:, i : i + 1], (8, 128))
            tiles[t] = tiles[t] - (col_t * scale) * row
    return jnp.concatenate([tile[:, R:] for tile in tiles], axis=0)


def leaf_kernel(d_ref, b_ref, t_ref, y_ref, z_ref, m_ref, aug):
    aug[:, :M] = d_ref[...]
    aug[:, M : M + LEVELS * R] = b_ref[...]
    aug[:, M + LEVELS * R :] = t_ref[...]
    for j in range(4):
        r0 = R * j
        a0 = 128 * (r0 // 128)
        minv = chol_inverse(aug[r0 : r0 + R, r0 : r0 + R])
        m_ref[r0 : r0 + R, :] = minv
        panel = mm(minv, aug[r0 : r0 + R, a0:])
        z_ref[r0 : r0 + R, :] = jnp.zeros((R, M), F32)
        z_ref[r0 : r0 + R, a0:] = panel[:, : M - a0]
        y_ref[r0 : r0 + R, :] = panel[:, M - a0 :]
        for i in range(j + 1, 4):
            c0 = R * i
            s0 = 128 * (c0 // 128)
            aug[c0 : c0 + R, s0:] -= mm_t(panel[:, c0 - a0 : c0 - a0 + R], panel[:, s0 - a0 :])


def back_kernel(y_ref, z_ref, m_ref, w_ref):
    for j in range(3, -1, -1):
        r0 = R * j
        rhs = y_ref[r0 : r0 + R, :]
        if j < 3:
            rhs = rhs - mm(z_ref[r0 : r0 + R, r0 + R :], w_ref[r0 + R :, :])
        w_ref[r0 : r0 + R, :] = mm_t(m_ref[r0 : r0 + R, :], rhs)


def gram_into(y, out_ref, base=None):
    offs, _ = offsets(1)
    for pair in range(4):
        st = 128 * pair
        g = mm_t(y[:, st : st + 128], y[:, st:])
        for h in range(2):
            level = 2 * pair + 1 + h
            o = offs[level]
            piece = g[R * h : R * h + R, :]
            if base is not None:
                piece = piece + base[:, o : o + width_of(level)]
            out_ref[:, o : o + width_of(level)] = piece


def gram_kernel(y_ref, g_ref):
    gram_into(y_ref[...], g_ref)


def reduce_level(k, coupling_ref, rows, p_ref, m_ref):
    o = R * ((k - 1) % 2)
    cap = rows[:, o : o + R]
    ids0 = lax.broadcasted_iota(jnp.int32, (R, R), 0)
    ids1 = lax.broadcasted_iota(jnp.int32, (R, R), 1)
    weights = 1.0 / coupling_ref[k - 1 : k, :]
    cap = cap + jnp.where(ids0 == ids1, jnp.broadcast_to(weights, (R, R)), 0.0)
    cap = 0.5 * (cap + cap.T)
    minv = chol_inverse(cap)
    m_ref[...] = minv
    p = mm(minv, rows)
    p_ref[...] = p
    return p


def next_level(k, p, trailing, n_ref):
    offs, _ = offsets(k + 1)
    sk = start_of(k)
    for pair in range(k // 2, 4):
        st = 128 * pair
        g = mm_t(p[:, st - sk : st - sk + 128], p[:, st - sk :])
        for h in range(2):
            level = 2 * pair + 1 + h
            if level > k:
                o = offs[level]
                n_ref[:, o : o + width_of(level)] = trailing(level) - g[R * h : R * h + R, :]


def first_level_kernel(c_ref, g_ref, y_ref, p_ref, m_ref, n_ref, sums):
    gram_into(y_ref[...], sums, g_ref)
    offs, _ = offsets(1)
    p = reduce_level(1, c_ref, sums[:, : width_of(1)], p_ref, m_ref)
    next_level(1, p, lambda level: sums[:, offs[level] : offs[level] + width_of(level)], n_ref)


def level_kernel(k, c_ref, own_ref, got_ref, p_ref, m_ref, n_ref):
    offs, _ = offsets(k)

    def part(level):
        o = offs[level]
        return own_ref[:, o : o + width_of(level)] + got_ref[:, o : o + width_of(level)]

    p = reduce_level(k, c_ref, part(k), p_ref, m_ref)
    next_level(k, p, part, n_ref)


def apply_level(k, w, p, minv):
    o = R * ((k - 1) % 2)
    cut = (start_of(k + 1) if k < LEVELS else LEVELS * R) - start_of(k)
    coef = mm_t(minv, p[:, cut:])
    return w[:, cut:] - mm(w[:, o : o + R], coef)


def apply_kernel(k, w_ref, p_ref, m_ref, o_ref):
    o_ref[...] = apply_level(k, w_ref[...], p_ref[...], m_ref[...])


def last_kernel(k, c_ref, own_ref, got_ref, w_ref, o_ref, p_ref, m_ref):
    rows = own_ref[...] + got_ref[...]
    p = reduce_level(k, c_ref, rows, p_ref, m_ref)
    o_ref[...] = apply_level(k, w_ref[...], p, m_ref[...])


def call(kernel, outs, *args, scratch=(), flops=10_000_000, name=None):
    vm = pl.BlockSpec(memory_space=pltpu.VMEM)
    shapes = [jax.ShapeDtypeStruct(s, F32) for s in outs]
    return pl.pallas_call(
        kernel,
        out_shape=shapes,
        in_specs=[vm] * len(args),
        out_specs=[vm] * len(shapes),
        scratch_shapes=[pltpu.VMEM(s, F32) for s in scratch],
        cost_estimate=pl.CostEstimate(flops=flops, bytes_accessed=1_000_000, transcendentals=0),
        name=name,
    )(*args)


def exchange(value, level, inner_bits):
    if level <= inner_bits:
        axis, masks = "inner", {1: 1, 2: 2, 3: 4, 4: 8}
        mask = masks[level]
    else:
        axis, masks = "group", {5: 1, 6: 2, 7: 4, 8: 14}
        mask = masks[level]
    return lax.ppermute(value, axis, [(s, s ^ mask) for s in range(lax.axis_size(axis))])


def per_device(leaf_blocks, bases, targets, coupling):
    inner_bits = lax.axis_size("inner").bit_length() - 1
    y, z, m = call(
        leaf_kernel, [(M, WIDTH), (M, M), (M, R)], leaf_blocks, bases, targets,
        scratch=[(M, M + WIDTH)], name="leaf",
    )
    got = exchange(y, 1, inner_bits)
    (own,) = call(gram_kernel, [(R, offsets(1)[1])], y, name="gram")
    (w,) = call(back_kernel, [(M, WIDTH)], y, z, m, name="back")
    for k in range(1, LEVELS):
        outs = [(R, width_of(k)), (R, R), (R, offsets(k + 1)[1])]
        if k == 1:
            p, minv, nxt = call(
                first_level_kernel, outs, coupling, own, got, scratch=[(R, offsets(1)[1])], name="level1"
            )
        else:
            kernel = lambda *refs, k=k: level_kernel(k, *refs)
            p, minv, nxt = call(kernel, outs, coupling, own, got, name="level%d" % k)
        own = nxt
        got = exchange(own, k + 1, inner_bits)
        kernel = lambda *refs, k=k: apply_kernel(k, *refs)
        (w,) = call(kernel, [(M, width_of(k + 1))], w, p, minv, name="apply%d" % k)
    kernel = lambda *refs: last_kernel(LEVELS, *refs)
    return call(
        kernel, [(M, NRHS)], coupling, own, got, w,
        scratch=[(R, width_of(LEVELS)), (R, R)], name="last",
    )[0]


def solution(mesh):
    in_specs = (
        P(("group", "inner"), None),
        P(("group", "inner"), None),
        P(("group", "inner"), None),
        P(),
    )
    out_specs = P(("group", "inner"), None)
    return jax.shard_map(
        per_device, mesh=mesh, in_specs=in_specs, out_specs=out_specs, check_vma=False
    )
```

```python
import jax
import jax.numpy as jnp
from jax import lax
from jax.experimental import pallas as pl
from jax.experimental.pallas import tpu as pltpu
from jax.sharding import PartitionSpec as P

M = 256
R = 64
LEVELS = 8
NRHS = 128
WIDTH = LEVELS * R + NRHS
NB = 16
F32 = jnp.float32
HI = lax.Precision.HIGHEST


def start_of(level):
    return 128 * ((level - 1) // 2)


def width_of(level):
    return WIDTH - start_of(level)


def offsets(first):
    out, at = {}, 0
    for level in range(first, LEVELS + 1):
        out[level] = at
        at += width_of(level)
    return out, at


def mm(a, b):
    return lax.dot_general(a, b, (((1,), (0,)), ((), ())), precision=HI, preferred_element_type=F32)


def mm_t(a, b):
    return lax.dot_general(a, b, (((0,), (0,)), ((), ())), precision=HI, preferred_element_type=F32)


def chol_inverse(block, at):
    sub = lax.broadcasted_iota(jnp.int32, (8, 128), 0)
    lane = lax.broadcasted_iota(jnp.int32, (8, 128), 1)
    mine = (lane >= at) & (lane < at + R)
    groups = R // 8
    tiles, pivots = [], [None] * groups
    for g in range(groups):
        eye = jnp.where(lane == sub + (8 * g + R - at), 1.0, 0.0)
        tiles.append(jnp.where(mine, block[8 * g : 8 * g + 8, :], eye))

    def spread(tile, s):
        return jnp.broadcast_to(tile[s : s + 1, :], (8, 128))

    for first in range(0, R, NB):
        cols = {}
        for r in range(first, first + NB):
            for g in range(r // 8, groups):
                cols[r, g] = jnp.broadcast_to(tiles[g][:, at + r : at + r + 1], (8, 128))
        for i in range(first, first + NB):
            gi, s = i // 8, i % 8
            pivot = spread(cols[i, gi], s)
            inv = 1.0 / pivot
            pivots[gi] = pivot if s == 0 else jnp.where(sub >= s, pivot, pivots[gi])
            row = spread(tiles[gi], s)
            below = {g: cols[i, g] for g in range(gi, groups)}
            below[gi] = jnp.where(sub > s, below[gi], 0.0)
            for r in range(i + 1, first + NB):
                mult = spread(cols[i, r // 8], r % 8) * inv
                for g in range(r // 8, groups):
                    cols[r, g] = cols[r, g] - below[g] * mult
            scaled = row * inv
            for g in range(gi, groups):
                if g > gi or s < 7:
                    tiles[g] = tiles[g] - below[g] * scaled
    out = [jnp.where(mine, 0.0, tiles[g] * lax.rsqrt(pivots[g])) for g in range(groups)]
    return jnp.concatenate(out, axis=0)


def leaf_kernel(d_ref, b_ref, t_ref, y_ref, z_ref, m_ref, aug):
    aug[:, :M] = d_ref[...]
    aug[:, M : M + LEVELS * R] = b_ref[...]
    aug[:, M + LEVELS * R :] = t_ref[...]
    for j in range(4):
        r0 = R * j
        a0 = 128 * (r0 // 128)
        minv = chol_inverse(aug[r0 : r0 + R, a0 : a0 + 128], r0 - a0)
        m_ref[r0 : r0 + R, :] = minv
        rows = aug[r0 : r0 + R, a0:]
        panel = mm(minv, jnp.concatenate([rows, rows], axis=0))
        z_ref[r0 : r0 + R, :] = jnp.zeros((R, M), F32)
        z_ref[r0 : r0 + R, a0:] = panel[:, : M - a0]
        y_ref[r0 : r0 + R, :] = panel[:, M - a0 :]
        for i in range(j + 1, 4):
            c0 = R * i
            s0 = 128 * (c0 // 128)
            aug[c0 : c0 + R, s0:] -= mm_t(panel[:, c0 - a0 : c0 - a0 + R], panel[:, s0 - a0 :])


def back_kernel(y_ref, z_ref, m_ref, w_ref):
    for j in range(3, -1, -1):
        r0 = R * j
        o = R - r0 % 128
        rhs = y_ref[r0 : r0 + R, :]
        if j < 3:
            rhs = rhs - mm(z_ref[r0 : r0 + R, r0 + R :], w_ref[r0 + R :, :])
        w_ref[r0 : r0 + R, :] = mm_t(m_ref[r0 : r0 + R, :], rhs)[o : o + R, :]


def gram_pair(y, pair):
    st = 128 * pair
    return mm_t(y[:, st : st + 128], y[:, st:])


def gram_kernel(y_ref, g_ref):
    y = y_ref[...]
    offs, _ = offsets(1)
    for pair in range(4):
        g = gram_pair(y, pair)
        for h in range(2):
            level = 2 * pair + 1 + h
            g_ref[:, offs[level] : offs[level] + width_of(level)] = g[R * h : R * h + R, :]


def reduce_level(k, coupling_ref, rows, p_ref, m_ref):
    o = R * ((k - 1) % 2)
    ids0 = lax.broadcasted_iota(jnp.int32, (R, 128), 0)
    ids1 = lax.broadcasted_iota(jnp.int32, (R, 128), 1)
    weights = 1.0 / coupling_ref[k - 1 : k, :]
    weights = jnp.concatenate([weights, weights], axis=1)
    cap = rows[:, :128] + jnp.where(ids0 + o == ids1, jnp.broadcast_to(weights, (R, 128)), 0.0)
    minv = chol_inverse(cap, o)
    m_ref[...] = minv
    p = mm(minv, jnp.concatenate([rows, rows], axis=0))
    p_ref[...] = p
    return p


def next_level(k, p, trailing, n_ref):
    offs, _ = offsets(k + 1)
    sk = start_of(k)
    for pair in range(k // 2, 4):
        st = 128 * pair
        g = mm_t(p[:, st - sk : st - sk + 128], p[:, st - sk :])
        for h in range(2):
            level = 2 * pair + 1 + h
            if level > k:
                o = offs[level]
                n_ref[:, o : o + width_of(level)] = trailing(level) - g[R * h : R * h + R, :]


def first_level_kernel(c_ref, g_ref, got_ref, dep_ref, p_ref, m_ref, n_ref):
    y = got_ref[...]
    offs, _ = offsets(1)
    grams = {0: gram_pair(y, 0)}

    def part(level):
        pair, h = (level - 1) // 2, (level - 1) % 2
        if pair not in grams:
            grams[pair] = gram_pair(y, pair)
        o = offs[level]
        return g_ref[:, o : o + width_of(level)] + grams[pair][R * h : R * h + R, :]

    p = reduce_level(1, c_ref, part(1), p_ref, m_ref)
    next_level(1, p, part, n_ref)


def level_kernel(k, c_ref, own_ref, got_ref, dep_ref, p_ref, m_ref, n_ref):
    offs, _ = offsets(k)

    def part(level):
        o = offs[level]
        return own_ref[:, o : o + width_of(level)] + got_ref[:, o : o + width_of(level)]

    p = reduce_level(k, c_ref, part(k), p_ref, m_ref)
    next_level(k, p, part, n_ref)


def apply_level(k, w, p, minv):
    o = R * ((k - 1) % 2)
    cut = (start_of(k + 1) if k < LEVELS else LEVELS * R) - start_of(k)
    coef = mm_t(minv, p[:, cut:])[R - o : 2 * R - o, :]
    return w[:, cut:] - mm(w[:, o : o + R], coef)


def apply_kernel(k, w_ref, p_ref, m_ref, o_ref):
    o_ref[...] = apply_level(k, w_ref[...], p_ref[...], m_ref[...])


def last_kernel(k, c_ref, own_ref, got_ref, w_ref, o_ref, p_ref, m_ref):
    p = reduce_level(k, c_ref, own_ref[...] + got_ref[...], p_ref, m_ref)
    o_ref[...] = apply_level(k, w_ref[...], p, m_ref[...])


def call(kernel, outs, *args, hbm=(), scratch=(), flops=10_000_000, name=None):
    vm = pl.BlockSpec(memory_space=pltpu.VMEM)
    hb = pl.BlockSpec(memory_space=pl.ANY)
    shapes = [jax.ShapeDtypeStruct(s, F32) for s in outs]
    return pl.pallas_call(
        kernel,
        out_shape=shapes,
        in_specs=[hb if i in hbm else vm for i in range(len(args))],
        out_specs=[vm] * len(shapes),
        scratch_shapes=[pltpu.VMEM(s, F32) for s in scratch],
        compiler_params=pltpu.CompilerParams(vmem_limit_bytes=16 << 20),
        cost_estimate=pl.CostEstimate(flops=flops, bytes_accessed=1_000_000, transcendentals=0),
        name=name,
    )(*args)


def exchange(value, level, inner_bits):
    axis = "inner" if level <= inner_bits else "group"
    mask = {1: 1, 2: 2, 3: 4, 4: 8, 5: 1, 6: 2, 7: 4, 8: 14}[level]
    return lax.ppermute(value, axis, [(s, s ^ mask) for s in range(lax.axis_size(axis))])


def per_device(leaf_blocks, bases, targets, coupling):
    inner_bits = lax.axis_size("inner").bit_length() - 1
    y, z, m = call(
        leaf_kernel, [(M, WIDTH), (M, M), (M, 128)], leaf_blocks, bases, targets,
        scratch=[(M, M + WIDTH)], name="leaf",
    )
    got = exchange(y, 1, inner_bits)
    (own,) = call(gram_kernel, [(R, offsets(1)[1])], y, name="gram")
    (w,) = call(back_kernel, [(M, WIDTH)], y, z, m, name="back")
    for k in range(1, LEVELS):
        outs = [(R, width_of(k)), (R, 128), (R, offsets(k + 1)[1])]
        kernel = first_level_kernel if k == 1 else (lambda *refs, k=k: level_kernel(k, *refs))
        p, minv, own = call(kernel, outs, coupling, own, got, w, hbm=(3,), name="level%d" % k)
        got = exchange(own, k + 1, inner_bits)
        kernel = lambda *refs, k=k: apply_kernel(k, *refs)
        (w,) = call(kernel, [(M, width_of(k + 1))], w, p, minv, name="apply%d" % k)
    kernel = lambda *refs: last_kernel(LEVELS, *refs)
    return call(
        kernel, [(M, NRHS)], coupling, own, got, w,
        scratch=[(R, width_of(LEVELS)), (R, 128)], name="last",
    )[0]


def solution(mesh):
    in_specs = (
        P(("group", "inner"), None),
        P(("group", "inner"), None),
        P(("group", "inner"), None),
        P(),
    )
    out_specs = P(("group", "inner"), None)
    return jax.shard_map(
        per_device, mesh=mesh, in_specs=in_specs, out_specs=out_specs, check_vma=False
    )
```

```python
import jax
import jax.numpy as jnp
from jax import lax
from jax.experimental import pallas as pl
from jax.experimental.pallas import tpu as pltpu
from jax.sharding import PartitionSpec as P

M = 256
R = 64
LEVELS = 8
NRHS = 128
WIDTH = LEVELS * R + NRHS
NB = 16
SPLIT = 4
F32 = jnp.float32
HI = lax.Precision.HIGHEST


def start_of(level):
    return 128 * ((level - 1) // 2)


def width_of(level):
    return WIDTH - start_of(level)


def offsets(first):
    out, at = {}, 0
    for level in range(first, LEVELS + 1):
        out[level] = at
        at += width_of(level)
    return out, at


def mm(a, b):
    return lax.dot_general(a, b, (((1,), (0,)), ((), ())), precision=HI, preferred_element_type=F32)


def mm_t(a, b):
    return lax.dot_general(a, b, (((0,), (0,)), ((), ())), precision=HI, preferred_element_type=F32)


def chol_inverse(block, at):
    sub = lax.broadcasted_iota(jnp.int32, (8, 128), 0)
    lane = lax.broadcasted_iota(jnp.int32, (8, 128), 1)
    mine = (lane >= at) & (lane < at + R)
    groups = R // 8
    tiles, pivots = [], [None] * groups
    for g in range(groups):
        eye = jnp.where(lane == sub + (8 * g + R - at), 1.0, 0.0)
        tiles.append(jnp.where(mine, block[8 * g : 8 * g + 8, :], eye))

    def spread(tile, s):
        return jnp.broadcast_to(tile[s : s + 1, :], (8, 128))

    for first in range(0, R, NB):
        cols = {}
        for r in range(first, first + NB):
            for g in range(r // 8, groups):
                cols[r, g] = jnp.broadcast_to(tiles[g][:, at + r : at + r + 1], (8, 128))
        for i in range(first, first + NB):
            gi, s = i // 8, i % 8
            pivot = spread(cols[i, gi], s)
            inv = 1.0 / pivot
            pivots[gi] = pivot if s == 0 else jnp.where(sub >= s, pivot, pivots[gi])
            row = spread(tiles[gi], s)
            below = {g: cols[i, g] for g in range(gi, groups)}
            below[gi] = jnp.where(sub > s, below[gi], 0.0)
            for r in range(i + 1, first + NB):
                mult = spread(cols[i, r // 8], r % 8) * inv
                for g in range(r // 8, groups):
                    cols[r, g] = cols[r, g] - below[g] * mult
            scaled = row * inv
            for g in range(gi, groups):
                if g > gi or s < 7:
                    tiles[g] = tiles[g] - below[g] * scaled
    out = [jnp.where(mine, 0.0, tiles[g] * lax.rsqrt(pivots[g])) for g in range(groups)]
    return jnp.concatenate(out, axis=0)


def sweep(aug, count, y_ref, z_ref, m_ref, late=()):
    rows = aug.shape[0]
    cols = aug.shape[1] - WIDTH
    for j in range(count):
        r0 = R * j
        a0 = 128 * (r0 // 128)
        minv = chol_inverse(aug[r0 : r0 + R, a0 : a0 + 128], r0 - a0)
        m_ref[r0 : r0 + R, :] = minv
        if j == 0:
            for copy in late:
                copy.wait()
        block = aug[r0 : r0 + R, a0:]
        panel = mm(minv, jnp.concatenate([block, block], axis=0))
        z_ref[r0 : r0 + R, :] = panel[:, : cols - a0]
        y_ref[r0 : r0 + R, :] = panel[:, cols - a0 :]
        for i in range(j + 1, rows // R):
            c0 = R * i
            s0 = 128 * (c0 // 128)
            aug[c0 : c0 + R, s0:] -= mm_t(panel[:, c0 - a0 : c0 - a0 + R], panel[:, s0 - a0 :])


def leaf_kernel(d_any, b_any, t_any, y_ref, z_ref, m_ref, rest_ref, aug, sem):
    at = M + LEVELS * R
    copies = [
        pltpu.make_async_copy(d_any, aug.at[:, :M], sem.at[0]),
        pltpu.make_async_copy(b_any, aug.at[:, M:at], sem.at[1]),
        pltpu.make_async_copy(t_any, aug.at[:, at:], sem.at[2]),
    ]
    for copy in copies:
        copy.start()
    copies[0].wait()
    sweep(aug, 2, y_ref, z_ref, m_ref, copies[1:])
    rest_ref[...] = aug[M // 2 :, M // 2 :]


def leaf2_kernel(rest_ref, y_ref, z_ref, m_ref, aug):
    aug[...] = rest_ref[...]
    sweep(aug, 2, y_ref, z_ref, m_ref)


def back_kernel(ya_ref, za_ref, ma_ref, yb_ref, zb_ref, mb_ref, w_ref):
    for j in range(3, -1, -1):
        y_ref, z_ref, m_ref = (ya_ref, za_ref, ma_ref) if j < 2 else (yb_ref, zb_ref, mb_ref)
        q0 = R * (j % 2)
        rhs = y_ref[q0 : q0 + R, :]
        if j < 3:
            z = z_ref[q0 : q0 + R, q0 + R :]
            rhs = rhs - mm(z, w_ref[R * (j + 1) :, :])
        w_ref[R * j : R * j + R, :] = mm_t(m_ref[q0 : q0 + R, :], rhs)[R - q0 : 2 * R - q0, :]


def gram_pair(y, pair):
    st = 128 * pair
    return mm_t(y[:, st : st + 128], y[:, st:])


def gram_pairs(ya, yb):
    return [gram_pair(ya, pair) + gram_pair(yb, pair) for pair in range(4)]


def gram_kernel(ya_ref, yb_ref, g_ref):
    offs, _ = offsets(1)
    grams = gram_pairs(ya_ref[...], yb_ref[...])
    for level in range(1, LEVELS + 1):
        pair, h = (level - 1) // 2, (level - 1) % 2
        g_ref[:, offs[level] : offs[level] + width_of(level)] = grams[pair][R * h : R * h + R, :]


def reduce_level(k, coupling_ref, rows, p_ref, m_ref):
    o = R * ((k - 1) % 2)
    ids0 = lax.broadcasted_iota(jnp.int32, (R, 128), 0)
    ids1 = lax.broadcasted_iota(jnp.int32, (R, 128), 1)
    weights = 1.0 / coupling_ref[k - 1 : k, :]
    weights = jnp.concatenate([weights, weights], axis=1)
    cap = rows[:, :128] + jnp.where(ids0 + o == ids1, jnp.broadcast_to(weights, (R, 128)), 0.0)
    minv = chol_inverse(cap, o)
    m_ref[...] = minv
    p = mm(minv, jnp.concatenate([rows, rows], axis=0))
    p_ref[...] = p
    return p


def next_level(k, p, trailing, n_ref):
    offs, _ = offsets(k + 1)
    sk = start_of(k)
    for pair in range(k // 2, 4):
        st = 128 * pair
        g = mm_t(p[:, st - sk : st - sk + 128], p[:, st - sk :])
        for h in range(2):
            level = 2 * pair + 1 + h
            if level > k:
                o = offs[level]
                n_ref[:, o : o + width_of(level)] = trailing(level) - g[R * h : R * h + R, :]


def first_level_kernel(c_ref, g_ref, ya_ref, yb_ref, dep_ref, p_ref, m_ref, n_ref):
    offs, _ = offsets(1)
    grams = gram_pairs(ya_ref[...], yb_ref[...])

    def part(level):
        pair, h = (level - 1) // 2, (level - 1) % 2
        o = offs[level]
        return g_ref[:, o : o + width_of(level)] + grams[pair][R * h : R * h + R, :]

    p = reduce_level(1, c_ref, part(1), p_ref, m_ref)
    next_level(1, p, part, n_ref)


def level_kernel(k, c_ref, own_ref, got_ref, dep_ref, p_ref, m_ref, n_ref):
    offs, _ = offsets(k)

    def part(level):
        o = offs[level]
        return own_ref[:, o : o + width_of(level)] + got_ref[:, o : o + width_of(level)]

    p = reduce_level(k, c_ref, part(k), p_ref, m_ref)
    next_level(k, p, part, n_ref)


def coefficient(k, p_ref, m_ref):
    o = R * ((k - 1) % 2)
    cut = (start_of(k + 1) if k < LEVELS else LEVELS * R) - start_of(k)
    return mm_t(m_ref[...], p_ref[:, cut:])[R - o : 2 * R - o, :], o, cut


def stack_kernel(k, *refs):
    *old, p_ref, m_ref, o_ref = refs
    coef, o, cut = coefficient(k, p_ref, m_ref)
    rows = 0
    if old:
        prev = old[0]
        rows = prev.shape[0]
        o_ref[:rows, :] = prev[:, cut:] - mm(prev[:, o : o + R], coef)
    o_ref[rows:, :] = coef


def is_active():
    x = lax.rem(lax.axis_index("inner"), 4)
    core = lax.rem(lax.axis_index("group"), 2)
    middle = (x == 1) | (x == 2)
    return middle == (core == 0)


def fold_kernel(w_ref, own_ref, got_ref, o_ref):
    coef = jnp.where(is_active(), own_ref[...], got_ref[...])
    at = start_of(SPLIT + 1)
    o_ref[...] = w_ref[:, at:] - mm(w_ref[:, :at], coef)


def last_kernel(k, c_ref, own_ref, got_ref, old_ref, dep_ref, z_ref, p_ref, m_ref):
    reduce_level(k, c_ref, own_ref[...] + got_ref[...], p_ref, m_ref)
    stack_kernel(k, old_ref, p_ref, m_ref, z_ref)


def finish_kernel(w_ref, own_ref, got_ref, o_ref):
    z = jnp.where(is_active(), own_ref[...], got_ref[...])
    at = w_ref.shape[1] - NRHS
    o_ref[...] = w_ref[:, at:] - mm(w_ref[:, :at], z)


def call(kernel, outs, *args, hbm=(), scratch=(), sems=0, flops=10_000_000, name=None):
    vm = pl.BlockSpec(memory_space=pltpu.VMEM)
    hb = pl.BlockSpec(memory_space=pl.ANY)
    shapes = [jax.ShapeDtypeStruct(s, F32) for s in outs]
    extra = [pltpu.SemaphoreType.DMA((sems,))] if sems else []
    return pl.pallas_call(
        kernel,
        out_shape=shapes,
        in_specs=[hb if i in hbm else vm for i in range(len(args))],
        out_specs=[vm] * len(shapes),
        scratch_shapes=[pltpu.VMEM(s, F32) for s in scratch] + extra,
        compiler_params=pltpu.CompilerParams(vmem_limit_bytes=16 << 20),
        cost_estimate=pl.CostEstimate(flops=flops, bytes_accessed=1_000_000, transcendentals=0),
        name=name,
    )(*args)


def send(value, move):
    pairs = []
    for group in range(16):
        for inner in range(16):
            to = move(group // 2, group % 2, inner // 4, inner % 4)
            if to is not None:
                z, core, y, x = to
                pairs.append((group * 16 + inner, (z * 2 + core) * 16 + y * 4 + x))
    return lax.ppermute(value, ("group", "inner"), pairs)


def active(core, x):
    return (x in (1, 2)) == (core == 0)


def exchange(value, level):
    moves = {
        2: lambda z, c, y, x: (z, c, y, x ^ 3),
        3: lambda z, c, y, x: (z, c, y ^ 1, x),
        4: lambda z, c, y, x: (z, c, y ^ 3, x),
        5: lambda z, c, y, x: (z, c ^ 1, y, x ^ 1),
        6: lambda z, c, y, x: (z ^ 1, c, y, x),
        7: lambda z, c, y, x: (z ^ 2, c, y, x),
        8: lambda z, c, y, x: (z ^ 7, c, y, x),
    }
    return send(value, lambda z, c, y, x: moves[level](z, c, y, x) if active(c, x) else None)


def to_active(value):
    return send(value, lambda z, c, y, x: None if active(c, x) else (z, c, y, x ^ 1))


def to_passive(value):
    return send(value, lambda z, c, y, x: (z, c, y, x ^ 1) if active(c, x) else None)


def to_other_core(value):
    return send(value, lambda z, c, y, x: (z, c ^ 1, y, x) if active(c, x) else None)


def per_device(leaf_blocks, bases, targets, coupling):
    half = M // 2
    leaf_blocks, bases, targets = (
        pltpu.with_memory_space_constraint(a, pltpu.HBM) for a in (leaf_blocks, bases, targets)
    )
    ya, za, ma, rest = call(
        leaf_kernel, [(half, WIDTH), (half, M), (half, 128), (half, half + WIDTH)], leaf_blocks, bases, targets,
        hbm=(0, 1, 2), scratch=[(M, M + WIDTH)], sems=3, name="leaf",
    )
    got_a = to_active(ya)
    yb, zb, mb = call(
        leaf2_kernel, [(half, WIDTH), (half, half), (half, 128)], rest,
        scratch=[(half, half + WIDTH)], name="leaf2",
    )
    got_b = to_active(yb)
    (own,) = call(gram_kernel, [(R, offsets(1)[1])], ya, yb, name="gram")
    (w,) = call(back_kernel, [(M, WIDTH)], ya, za, ma, yb, zb, mb, name="back")
    dep, stack, folded = w, (), None
    for k in range(1, LEVELS):
        outs = [(R, width_of(k)), (R, 128), (R, offsets(k + 1)[1])]
        if k == 1:
            p, minv, own = call(first_level_kernel, outs, coupling, own, got_a, got_b, dep, hbm=(4,), name="level1")
        else:
            kernel = lambda *refs, k=k: level_kernel(k, *refs)
            p, minv, own = call(kernel, outs, coupling, own, got, dep, hbm=(3,), name="level%d" % k)
        got = exchange(own, k + 1)
        kernel = lambda *refs, k=k: stack_kernel(k, *refs)
        rows = R * k if k <= SPLIT else R * (k - SPLIT)
        stack = call(kernel, [(rows, width_of(k + 1))], *stack, p, minv, name="stack%d" % k)
        dep = stack[0]
        if k == SPLIT:
            lower, stack = stack[0], ()
            lower_got = to_passive(lower)
        if k == SPLIT + 2:
            (folded,) = call(fold_kernel, [(M, width_of(SPLIT + 1))], w, lower, lower_got, name="fold")
            dep = folded
    kernel = lambda *refs: last_kernel(LEVELS, *refs)
    (z,) = call(
        kernel, [(R * (LEVELS - SPLIT), NRHS)], coupling, own, got, stack[0], dep, hbm=(4,),
        scratch=[(R, width_of(LEVELS)), (R, 128)], name="last",
    )
    return call(finish_kernel, [(M, NRHS)], folded, z, to_other_core(z), name="finish")[0]


def solution(mesh):
    in_specs = (
        P(("group", "inner"), None),
        P(("group", "inner"), None),
        P(("group", "inner"), None),
        P(),
    )
    out_specs = P(("group", "inner"), None)
    return jax.shard_map(
        per_device, mesh=mesh, in_specs=in_specs, out_specs=out_specs, check_vma=False
    )
```

```python
import jax
import jax.numpy as jnp
from jax import lax
from jax.experimental import pallas as pl
from jax.experimental.pallas import tpu as pltpu
from jax.sharding import PartitionSpec as P


M = 256
R = 64
LEVELS = 8
NRHS = 128
WIDTH = LEVELS * R + NRHS
NB = 16
SPLIT = 4
F32 = jnp.float32
HI = lax.Precision.HIGHEST


def start_of(level):
    return 128 * ((level - 1) // 2)


def width_of(level):
    return WIDTH - start_of(level)


def offsets(first, last=LEVELS):
    out, at = {}, 0
    for level in range(first, last + 1):
        out[level] = at
        at += width_of(level)
    return out, at


def mm(a, b):
    return lax.dot_general(a, b, (((1,), (0,)), ((), ())), precision=HI, preferred_element_type=F32)


def mm_t(a, b):
    return lax.dot_general(a, b, (((0,), (0,)), ((), ())), precision=HI, preferred_element_type=F32)


def chol_inverse(block, at):
    sub = lax.broadcasted_iota(jnp.int32, (8, 128), 0)
    lane = lax.broadcasted_iota(jnp.int32, (8, 128), 1)
    mine = (lane >= at) & (lane < at + R)
    groups = R // 8
    tiles, pivots = [], [None] * groups
    for g in range(groups):
        eye = jnp.where(lane == sub + (8 * g + R - at), 1.0, 0.0)
        tiles.append(jnp.where(mine, block[8 * g : 8 * g + 8, :], eye))

    def spread(tile, s):
        return jnp.broadcast_to(tile[s : s + 1, :], (8, 128))

    for first in range(0, R, NB):
        cols = {}
        for r in range(first, first + NB):
            for g in range(r // 8, groups):
                cols[r, g] = jnp.broadcast_to(tiles[g][:, at + r : at + r + 1], (8, 128))
        for i in range(first, first + NB):
            gi, s = i // 8, i % 8
            pivot = spread(cols[i, gi], s)
            inv = 1.0 / pivot
            pivots[gi] = pivot if s == 0 else jnp.where(sub >= s, pivot, pivots[gi])
            row = spread(tiles[gi], s)
            below = {g: cols[i, g] for g in range(gi, groups)}
            below[gi] = jnp.where(sub > s, below[gi], 0.0)
            for r in range(i + 1, first + NB):
                mult = spread(cols[i, r // 8], r % 8) * inv
                for g in range(r // 8, groups):
                    cols[r, g] = cols[r, g] - below[g] * mult
            scaled = row * inv
            for g in range(gi, groups):
                if g > gi or s < 7:
                    tiles[g] = tiles[g] - below[g] * scaled
    out = [jnp.where(mine, 0.0, tiles[g] * lax.rsqrt(pivots[g])) for g in range(groups)]
    return jnp.concatenate(out, axis=0)


def sweep(aug, count, y_ref, z_ref, m_ref, late=()):
    rows = aug.shape[0]
    cols = aug.shape[1] - WIDTH
    for j in range(count):
        r0 = R * j
        a0 = 128 * (r0 // 128)
        minv = chol_inverse(aug[r0 : r0 + R, a0 : a0 + 128], r0 - a0)
        m_ref[r0 : r0 + R, :] = minv
        if j == 0:
            for copy in late:
                copy.wait()
        block = aug[r0 : r0 + R, a0:]
        panel = mm(minv, jnp.concatenate([block, block], axis=0))
        z_ref[r0 : r0 + R, :] = panel[:, : cols - a0]
        y_ref[r0 : r0 + R, :] = panel[:, cols - a0 :]
        for i in range(j + 1, rows // R):
            c0 = R * i
            s0 = 128 * (c0 // 128)
            aug[c0 : c0 + R, s0:] -= mm_t(panel[:, c0 - a0 : c0 - a0 + R], panel[:, s0 - a0 :])


def leaf_kernel(d_any, b_any, t_any, y_ref, z_ref, m_ref, rest_ref, aug, sem):
    at = M + LEVELS * R
    copies = [
        pltpu.make_async_copy(d_any, aug.at[:, :M], sem.at[0]),
        pltpu.make_async_copy(b_any, aug.at[:, M:at], sem.at[1]),
        pltpu.make_async_copy(t_any, aug.at[:, at:], sem.at[2]),
    ]
    for copy in copies:
        copy.start()
    copies[0].wait()
    sweep(aug, 2, y_ref, z_ref, m_ref, copies[1:])
    rest_ref[...] = aug[M // 2 :, M // 2 :]


def leaf2_kernel(rest_ref, y_ref, z_ref, m_ref, aug):
    aug[...] = rest_ref[...]
    sweep(aug, 2, y_ref, z_ref, m_ref)


def back_kernel(ya_ref, za_ref, ma_ref, yb_ref, zb_ref, mb_ref, w_ref):
    for j in range(3, -1, -1):
        y_ref, z_ref, m_ref = (ya_ref, za_ref, ma_ref) if j < 2 else (yb_ref, zb_ref, mb_ref)
        q0 = R * (j % 2)
        rhs = y_ref[q0 : q0 + R, :]
        if j < 3:
            z = z_ref[q0 : q0 + R, q0 + R :]
            rhs = rhs - mm(z, w_ref[R * (j + 1) :, :])
        w_ref[R * j : R * j + R, :] = mm_t(m_ref[q0 : q0 + R, :], rhs)[R - q0 : 2 * R - q0, :]


def gram_pair(y, pair):
    st = 128 * pair
    return mm_t(y[:, st : st + 128], y[:, st:])


def last_of(first):
    return SPLIT if first <= SPLIT else LEVELS


def row_block(grams, level):
    h = R * ((level - 1) % 2)
    return grams[(level - 1) // 2][h : h + R, :]


def put(ref, first, level, value):
    o = offsets(first)[0][level]
    ref[:, o : o + width_of(level)] = value


def get(ref, first, level):
    o = offsets(first)[0][level]
    return ref[:, o : o + width_of(level)]


def gram_pairs(ya_ref, yb_ref, pairs):
    y = jnp.concatenate([ya_ref[...], yb_ref[...]], axis=0)
    return {pair: gram_pair(y, pair) for pair in pairs}


def gram_kernel(ya_ref, yb_ref, near_ref, far_ref):
    grams = gram_pairs(ya_ref, yb_ref, range(4))
    for level in range(1, SPLIT + 1):
        put(near_ref, 1, level, row_block(grams, level))
    for level in range(SPLIT + 1, LEVELS + 1):
        put(far_ref, SPLIT + 1, level, row_block(grams, level))


def reduce_level(k, coupling_ref, rows, p_ref, m_ref):
    o = R * ((k - 1) % 2)
    ids0 = lax.broadcasted_iota(jnp.int32, (R, 128), 0)
    ids1 = lax.broadcasted_iota(jnp.int32, (R, 128), 1)
    weights = 1.0 / coupling_ref[k - 1 : k, :]
    weights = jnp.concatenate([weights, weights], axis=1)
    cap = rows[:, :128] + jnp.where(ids0 + o == ids1, jnp.broadcast_to(weights, (R, 128)), 0.0)
    minv = chol_inverse(cap, o)
    m_ref[...] = minv
    p = mm(minv, jnp.concatenate([rows, rows], axis=0))
    p_ref[...] = p
    return p


def schur(k, p, first, last):
    sk = start_of(k)
    grams = {}
    for pair in range((first - 1) // 2, (last + 1) // 2):
        st = 128 * pair
        grams[pair] = mm_t(p[:, st - sk : st - sk + 128], p[:, st - sk :])
    return grams


def next_level(k, p, trailing, n_ref):
    last = last_of(k + 1) if k != SPLIT else SPLIT
    if k < last:
        grams = schur(k, p, k + 1, last)
        for level in range(k + 1, last + 1):
            put(n_ref, k + 1, level, trailing(level) - row_block(grams, level))


def first_level_kernel(c_ref, own_ref, ya_ref, yb_ref, dep_ref, p_ref, m_ref, n_ref):
    grams = gram_pairs(ya_ref, yb_ref, range(SPLIT // 2))

    def part(level):
        return get(own_ref, 1, level) + row_block(grams, level)

    p = reduce_level(1, c_ref, part(1), p_ref, m_ref)
    next_level(1, p, part, n_ref)


def level_kernel(k, c_ref, own_ref, got_ref, dep_ref, dep2_ref, p_ref, m_ref, n_ref=None):
    def part(level):
        return get(own_ref, k, level) + get(got_ref, k, level)

    p = reduce_level(k, c_ref, part(k), p_ref, m_ref)
    next_level(k, p, part, n_ref)


def first_far_kernel(own_ref, ya_ref, yb_ref, p_ref, n_ref):
    grams = gram_pairs(ya_ref, yb_ref, range(SPLIT // 2, LEVELS // 2))
    less = schur(1, p_ref[...], SPLIT + 1, LEVELS)
    for level in range(SPLIT + 1, LEVELS + 1):
        put(n_ref, SPLIT + 1, level, get(own_ref, SPLIT + 1, level) + row_block(grams, level) - row_block(less, level))


def far_kernel(k, own_ref, got_ref, p_ref, n_ref):
    less = schur(k, p_ref[...], SPLIT + 1, LEVELS)
    for level in range(SPLIT + 1, LEVELS + 1):
        both = get(own_ref, SPLIT + 1, level) + get(got_ref, SPLIT + 1, level)
        put(n_ref, SPLIT + 1, level, both - row_block(less, level))


def apply_level(k, w, p, minv):
    o = R * ((k - 1) % 2)
    cut = (start_of(k + 1) if k < LEVELS else LEVELS * R) - start_of(k)
    coef = mm_t(minv, p[:, cut:])[R - o : 2 * R - o, :]
    return w[:, cut:] - mm(w[:, o : o + R], coef)


def apply_kernel(k, w_ref, p_ref, m_ref, o_ref):
    o_ref[...] = apply_level(k, w_ref[...], p_ref[...], m_ref[...])


def apply_two_kernel(w_ref, p_ref, m_ref, p2_ref, m2_ref, o_ref):
    two = 2 * R
    coef = mm_t(m_ref[...], p_ref[...])[R:, :]
    coef2 = mm_t(m2_ref[...], p2_ref[:, two:])[:R, :]
    coef = jnp.concatenate([coef[:, two:] - mm(coef[:, R:two], coef2), coef2], axis=0)
    o_ref[...] = w_ref[:, two:] - mm(w_ref[:, :two], coef)


def last_kernel(k, c_ref, own_ref, got_ref, w_ref, o_ref, p_ref, m_ref):
    p = reduce_level(k, c_ref, own_ref[...] + got_ref[...], p_ref, m_ref)
    o_ref[...] = apply_level(k, w_ref[...], p, m_ref[...])


def call(kernel, outs, *args, hbm=(), scratch=(), sems=0, flops=10_000_000):
    vm = pl.BlockSpec(memory_space=pltpu.VMEM)
    hb = pl.BlockSpec(memory_space=pl.ANY)
    shapes = [jax.ShapeDtypeStruct(s, F32) for s in outs]
    extra = [pltpu.SemaphoreType.DMA((sems,))] if sems else []
    return pl.pallas_call(
        kernel,
        out_shape=shapes,
        in_specs=[hb if i in hbm else vm for i in range(len(args))],
        out_specs=[vm] * len(shapes),
        scratch_shapes=[pltpu.VMEM(s, F32) for s in scratch] + extra,
        compiler_params=pltpu.CompilerParams(vmem_limit_bytes=16 << 20),
        cost_estimate=pl.CostEstimate(flops=flops, bytes_accessed=1_000_000, transcendentals=0),
    )(*args)


def exchange(value, level):
    axis = "inner" if level <= 4 else "group"
    mask = {1: 1, 2: 2, 3: 4, 4: 8, 5: 1, 6: 2, 7: 4, 8: 14}[level]
    return lax.ppermute(value, axis, [(s, s ^ mask) for s in range(lax.axis_size(axis))])


def per_device(leaf_blocks, bases, targets, coupling):
    half = M // 2
    leaf_blocks, bases, targets = (
        pltpu.with_memory_space_constraint(a, pltpu.HBM) for a in (leaf_blocks, bases, targets)
    )
    ya, za, ma, rest = call(
        leaf_kernel, [(half, WIDTH), (half, M), (half, 128), (half, half + WIDTH)], leaf_blocks, bases, targets,
        hbm=(0, 1, 2), scratch=[(M, M + WIDTH)], sems=3,
    )
    got_a = exchange(ya, 1)
    yb, zb, mb = call(
        leaf2_kernel, [(half, WIDTH), (half, half), (half, 128)], rest,
        scratch=[(half, half + WIDTH)],
    )
    got_b = exchange(yb, 1)
    far_shape = (R, offsets(SPLIT + 1)[1])
    near, far = call(gram_kernel, [(R, offsets(1, SPLIT)[1]), far_shape], ya, yb)
    (w,) = call(back_kernel, [(M, WIDTH)], ya, za, ma, yb, zb, mb)
    got = far_got = None
    for k in range(1, LEVELS):
        outs = [(R, width_of(k)), (R, 128)]
        if k != SPLIT:
            outs.append((R, offsets(k + 1, last_of(k + 1))[1]))
        if k == 1:
            p, minv, near = call(first_level_kernel, outs, coupling, near, got_a, got_b, w, hbm=(4,))
        else:
            kernel = lambda *refs, k=k: level_kernel(k, *refs)
            p, minv, *more = call(kernel, outs, coupling, near, got, w, far, hbm=(3, 4))
            near = more[0] if more else None
        if k < SPLIT:
            got = exchange(near, k + 1)
        if k == 1:
            (far,) = call(first_far_kernel, [far_shape], far, got_a, got_b, p)
        elif k <= SPLIT:
            kernel = lambda *refs, k=k: far_kernel(k, *refs)
            (far,) = call(kernel, [far_shape], far, far_got, p)
        if k < SPLIT:
            far_got = exchange(far, k + 1)
        if k == SPLIT:
            near = far
        if k >= SPLIT:
            got = exchange(near, k + 1)
        if k == LEVELS - 1:
            kernel = lambda *refs, k=k: apply_kernel(k, *refs)
            (w,) = call(kernel, [(M, width_of(k + 1))], w, p, minv)
        elif k % 2 == 0:
            (w,) = call(apply_two_kernel, [(M, width_of(k + 1))], w, *before, p, minv)
        before = (p, minv)
    kernel = lambda *refs: last_kernel(LEVELS, *refs)
    return call(
        kernel, [(M, NRHS)], coupling, near, got, w,
        scratch=[(R, width_of(LEVELS)), (R, 128)],
    )[0]


def solution(mesh):
    in_specs = (
        P(("group", "inner"), None),
        P(("group", "inner"), None),
        P(("group", "inner"), None),
        P(),
    )
    out_specs = P(("group", "inner"), None)
    return jax.shard_map(per_device, mesh=mesh, in_specs=in_specs, out_specs=out_specs, check_vma=False)
```

```python
import jax
import jax.numpy as jnp
from jax import lax
from jax.experimental import pallas as pl
from jax.experimental.pallas import tpu as pltpu
from jax.sharding import PartitionSpec as P


M = 256
R = 64
LEVELS = 8
NRHS = 128
WIDTH = LEVELS * R + NRHS
NB = 16
SPLIT = 4
F32 = jnp.float32
HI = lax.Precision.HIGHEST


def start_of(level):
    return 128 * ((level - 1) // 2)


def width_of(level):
    return WIDTH - start_of(level)


def offsets(first, last=LEVELS):
    out, at = {}, 0
    for level in range(first, last + 1):
        out[level] = at
        at += width_of(level)
    return out, at


def mm(a, b):
    return lax.dot_general(a, b, (((1,), (0,)), ((), ())), precision=HI, preferred_element_type=F32)


def mm_t(a, b):
    return lax.dot_general(a, b, (((0,), (0,)), ((), ())), precision=HI, preferred_element_type=F32)


def chol_inverse(block, at):
    sub = lax.broadcasted_iota(jnp.int32, (8, 128), 0)
    lane = lax.broadcasted_iota(jnp.int32, (8, 128), 1)
    mine = (lane >= at) & (lane < at + R)
    groups = R // 8
    tiles, pivots = [], [None] * groups
    for g in range(groups):
        eye = jnp.where(lane == sub + (8 * g + R - at), 1.0, 0.0)
        tiles.append(jnp.where(mine, block[8 * g : 8 * g + 8, :], eye))

    def spread(tile, s):
        return jnp.broadcast_to(tile[s : s + 1, :], (8, 128))

    first = 0
    while first < R:
        last = first + NB
        cols = {}
        for r in range(first, last):
            for g in range(r // 8, groups):
                cols[r, g] = jnp.broadcast_to(tiles[g][:, at + r : at + r + 1], (8, 128))
        for i in range(first, last, 2):
            gi, s = i // 8, i % 8
            a, b = spread(cols[i, gi], s), spread(cols[i, gi], s + 1)
            c = spread(cols[i + 1, gi], s + 1)
            inv_a = 1.0 / a
            inv_c = a * (1.0 / (a * c - b * b))
            ratio = b * inv_a
            low = {g: cols[i, g] for g in range(gi, groups)}
            low2 = {g: cols[i + 1, g] - low[g] * ratio for g in range(gi, groups)}
            for r in range(i + 2, last):
                h = r // 8
                mult = spread(low[h], r % 8) * inv_a
                mult2 = spread(low2[h], r % 8) * inv_c
                for g in range(h, groups):
                    cols[r, g] = (cols[r, g] - low[g] * mult) - low2[g] * mult2
            pair = jnp.where(sub == s, a, c - b * ratio)
            pivots[gi] = pair if s == 0 else jnp.where(sub >= s, pair, pivots[gi])
            row = spread(tiles[gi], s)
            row2 = (spread(tiles[gi], s + 1) - row * ratio) * inv_c
            row = row * inv_a
            low[gi] = jnp.where(sub > s, low[gi], 0.0)
            low2[gi] = jnp.where(sub > s + 1, low2[gi], 0.0)
            for g in range(gi, groups):
                tiles[g] = (tiles[g] - low[g] * row) - low2[g] * row2
        first = last
    out = [jnp.where(mine, 0.0, tiles[g] * lax.rsqrt(pivots[g])) for g in range(groups)]
    return jnp.concatenate(out, axis=0)


def sweep(aug, count, y_ref, z_ref, m_ref, late=()):
    rows = aug.shape[0]
    cols = aug.shape[1] - WIDTH
    for j in range(count):
        r0 = R * j
        a0 = 128 * (r0 // 128)
        minv = chol_inverse(aug[r0 : r0 + R, a0 : a0 + 128], r0 - a0)
        m_ref[r0 : r0 + R, :] = minv
        if j == 0:
            for copy in late:
                copy.wait()
        block = aug[r0 : r0 + R, a0:]
        panel = mm(minv, jnp.concatenate([block, block], axis=0))
        z_ref[r0 : r0 + R, :] = panel[:, : cols - a0]
        y_ref[r0 : r0 + R, :] = panel[:, cols - a0 :]
        for i in range(j + 1, rows // R):
            c0 = R * i
            s0 = 128 * (c0 // 128)
            aug[c0 : c0 + R, s0:] -= mm_t(panel[:, c0 - a0 : c0 - a0 + R], panel[:, s0 - a0 :])


def leaf_kernel(d_any, b_any, t_any, y_ref, z_ref, m_ref, rest_ref, aug, sem):
    at = M + LEVELS * R
    copies = [
        pltpu.make_async_copy(d_any, aug.at[:, :M], sem.at[0]),
        pltpu.make_async_copy(b_any, aug.at[:, M:at], sem.at[1]),
        pltpu.make_async_copy(t_any, aug.at[:, at:], sem.at[2]),
    ]
    for copy in copies:
        copy.start()
    copies[0].wait()
    sweep(aug, 2, y_ref, z_ref, m_ref, copies[1:])
    rest_ref[...] = aug[M // 2 :, M // 2 :]


def leaf2_kernel(rest_ref, y_ref, z_ref, m_ref, aug):
    aug[...] = rest_ref[...]
    sweep(aug, 2, y_ref, z_ref, m_ref)


def back_kernel(ya_ref, za_ref, ma_ref, yb_ref, zb_ref, mb_ref, w_ref):
    for j in range(3, -1, -1):
        y_ref, z_ref, m_ref = (ya_ref, za_ref, ma_ref) if j < 2 else (yb_ref, zb_ref, mb_ref)
        q0 = R * (j % 2)
        rhs = y_ref[q0 : q0 + R, :]
        if j < 3:
            z = z_ref[q0 : q0 + R, q0 + R :]
            rhs = rhs - mm(z, w_ref[R * (j + 1) :, :])
        w_ref[R * j : R * j + R, :] = mm_t(m_ref[q0 : q0 + R, :], rhs)[R - q0 : 2 * R - q0, :]


def gram_pair(y, pair):
    st = 128 * pair
    return mm_t(y[:, st : st + 128], y[:, st:])


def last_of(first):
    return SPLIT if first <= SPLIT else LEVELS


def row_block(grams, level):
    h = R * ((level - 1) % 2)
    return grams[(level - 1) // 2][h : h + R, :]


def put(ref, first, level, value):
    o = offsets(first)[0][level]
    ref[:, o : o + width_of(level)] = value


def get(ref, first, level):
    o = offsets(first)[0][level]
    return ref[:, o : o + width_of(level)]


def gram_pairs(ya_ref, yb_ref, pairs):
    y = jnp.concatenate([ya_ref[...], yb_ref[...]], axis=0)
    return {pair: gram_pair(y, pair) for pair in pairs}


def gram_kernel(ya_ref, yb_ref, near_ref, far_ref):
    grams = gram_pairs(ya_ref, yb_ref, range(4))
    for level in range(1, SPLIT + 1):
        put(near_ref, 1, level, row_block(grams, level))
    for level in range(SPLIT + 1, LEVELS + 1):
        put(far_ref, SPLIT + 1, level, row_block(grams, level))


def reduce_level(k, coupling_ref, rows, p_ref, m_ref):
    o = R * ((k - 1) % 2)
    ids0 = lax.broadcasted_iota(jnp.int32, (R, 128), 0)
    ids1 = lax.broadcasted_iota(jnp.int32, (R, 128), 1)
    weights = 1.0 / coupling_ref[k - 1 : k, :]
    weights = jnp.concatenate([weights, weights], axis=1)
    cap = rows[:, :128] + jnp.where(ids0 + o == ids1, jnp.broadcast_to(weights, (R, 128)), 0.0)
    minv = chol_inverse(cap, o)
    m_ref[...] = minv
    p = mm(minv, jnp.concatenate([rows, rows], axis=0))
    p_ref[...] = p
    return p


def schur(k, p, first, last):
    sk = start_of(k)
    grams = {}
    for pair in range((first - 1) // 2, (last + 1) // 2):
        st = 128 * pair
        grams[pair] = mm_t(p[:, st - sk : st - sk + 128], p[:, st - sk :])
    return grams


def next_level(k, p, trailing, n_ref):
    last = last_of(k + 1) if k != SPLIT else SPLIT
    if k < last:
        grams = schur(k, p, k + 1, last)
        for level in range(k + 1, last + 1):
            put(n_ref, k + 1, level, trailing(level) - row_block(grams, level))


def first_level_kernel(c_ref, own_ref, ya_ref, yb_ref, dep_ref, p_ref, m_ref, n_ref):
    grams = gram_pairs(ya_ref, yb_ref, range(SPLIT // 2))

    def part(level):
        return get(own_ref, 1, level) + row_block(grams, level)

    p = reduce_level(1, c_ref, part(1), p_ref, m_ref)
    next_level(1, p, part, n_ref)


def level_kernel(k, c_ref, own_ref, got_ref, dep_ref, dep2_ref, p_ref, m_ref, n_ref=None):
    def part(level):
        return get(own_ref, k, level) + get(got_ref, k, level)

    p = reduce_level(k, c_ref, part(k), p_ref, m_ref)
    next_level(k, p, part, n_ref)


def first_far_kernel(own_ref, ya_ref, yb_ref, p_ref, n_ref):
    grams = gram_pairs(ya_ref, yb_ref, range(SPLIT // 2, LEVELS // 2))
    less = schur(1, p_ref[...], SPLIT + 1, LEVELS)
    for level in range(SPLIT + 1, LEVELS + 1):
        put(n_ref, SPLIT + 1, level, get(own_ref, SPLIT + 1, level) + row_block(grams, level) - row_block(less, level))


def far_kernel(k, own_ref, got_ref, p_ref, n_ref):
    less = schur(k, p_ref[...], SPLIT + 1, LEVELS)
    for level in range(SPLIT + 1, LEVELS + 1):
        both = get(own_ref, SPLIT + 1, level) + get(got_ref, SPLIT + 1, level)
        put(n_ref, SPLIT + 1, level, both - row_block(less, level))


def apply_level(k, w, p, minv):
    o = R * ((k - 1) % 2)
    cut = (start_of(k + 1) if k < LEVELS else LEVELS * R) - start_of(k)
    coef = mm_t(minv, p[:, cut:])[R - o : 2 * R - o, :]
    return w[:, cut:] - mm(w[:, o : o + R], coef)


def apply_kernel(k, w_ref, p_ref, m_ref, o_ref):
    o_ref[...] = apply_level(k, w_ref[...], p_ref[...], m_ref[...])


def apply_two_kernel(w_ref, p_ref, m_ref, p2_ref, m2_ref, o_ref):
    two = 2 * R
    coef = mm_t(m_ref[...], p_ref[...])[R:, :]
    coef2 = mm_t(m2_ref[...], p2_ref[:, two:])[:R, :]
    coef = jnp.concatenate([coef[:, two:] - mm(coef[:, R:two], coef2), coef2], axis=0)
    o_ref[...] = w_ref[:, two:] - mm(w_ref[:, :two], coef)


def last_kernel(k, c_ref, own_ref, got_ref, w_ref, o_ref, p_ref, m_ref):
    p = reduce_level(k, c_ref, own_ref[...] + got_ref[...], p_ref, m_ref)
    o_ref[...] = apply_level(k, w_ref[...], p, m_ref[...])


def call(kernel, outs, *args, hbm=(), scratch=(), sems=0, flops=10_000_000):
    vm = pl.BlockSpec(memory_space=pltpu.VMEM)
    hb = pl.BlockSpec(memory_space=pl.ANY)
    shapes = [jax.ShapeDtypeStruct(s, F32) for s in outs]
    extra = [pltpu.SemaphoreType.DMA((sems,))] if sems else []
    return pl.pallas_call(
        kernel,
        out_shape=shapes,
        in_specs=[hb if i in hbm else vm for i in range(len(args))],
        out_specs=[vm] * len(shapes),
        scratch_shapes=[pltpu.VMEM(s, F32) for s in scratch] + extra,
        compiler_params=pltpu.CompilerParams(vmem_limit_bytes=16 << 20),
        cost_estimate=pl.CostEstimate(flops=flops, bytes_accessed=1_000_000, transcendentals=0),
    )(*args)


def exchange(value, level):
    axis = "inner" if level <= 4 else "group"
    mask = {1: 1, 2: 3, 3: 4, 4: 12, 5: 1, 6: 2, 7: 4, 8: 14}[level]
    return lax.ppermute(value, axis, [(s, s ^ mask) for s in range(lax.axis_size(axis))])


def per_device(leaf_blocks, bases, targets, coupling):
    half = M // 2
    leaf_blocks, bases, targets = (
        pltpu.with_memory_space_constraint(a, pltpu.HBM) for a in (leaf_blocks, bases, targets)
    )
    ya, za, ma, rest = call(
        leaf_kernel, [(half, WIDTH), (half, M), (half, 128), (half, half + WIDTH)], leaf_blocks, bases, targets,
        hbm=(0, 1, 2), scratch=[(M, M + WIDTH)], sems=3,
    )
    got_a = exchange(ya, 1)
    yb, zb, mb = call(
        leaf2_kernel, [(half, WIDTH), (half, half), (half, 128)], rest,
        scratch=[(half, half + WIDTH)],
    )
    got_b = exchange(yb, 1)
    far_shape = (R, offsets(SPLIT + 1)[1])
    near, far = call(gram_kernel, [(R, offsets(1, SPLIT)[1]), far_shape], ya, yb)
    (w,) = call(back_kernel, [(M, WIDTH)], ya, za, ma, yb, zb, mb)
    got = far_got = None
    for k in range(1, LEVELS):
        outs = [(R, width_of(k)), (R, 128)]
        if k != SPLIT:
            outs.append((R, offsets(k + 1, last_of(k + 1))[1]))
        if k == 1:
            p, minv, near = call(first_level_kernel, outs, coupling, near, got_a, got_b, w, hbm=(4,))
        else:
            kernel = lambda *refs, k=k: level_kernel(k, *refs)
            p, minv, *more = call(kernel, outs, coupling, near, got, w, far, hbm=(3, 4))
            near = more[0] if more else None
        if k < SPLIT:
            got = exchange(near, k + 1)
        if k == 1:
            (far,) = call(first_far_kernel, [far_shape], far, got_a, got_b, p)
        elif k <= SPLIT:
            kernel = lambda *refs, k=k: far_kernel(k, *refs)
            (far,) = call(kernel, [far_shape], far, far_got, p)
        if k < SPLIT:
            far_got = exchange(far, k + 1)
        if k == SPLIT:
            near = far
        if k >= SPLIT:
            got = exchange(near, k + 1)
        if k == LEVELS - 1:
            kernel = lambda *refs, k=k: apply_kernel(k, *refs)
            (w,) = call(kernel, [(M, width_of(k + 1))], w, p, minv)
        elif k % 2 == 0:
            (w,) = call(apply_two_kernel, [(M, width_of(k + 1))], w, *before, p, minv)
        before = (p, minv)
    kernel = lambda *refs: last_kernel(LEVELS, *refs)
    return call(
        kernel, [(M, NRHS)], coupling, near, got, w,
        scratch=[(R, width_of(LEVELS)), (R, 128)],
    )[0]


def solution(mesh):
    in_specs = (
        P(("group", "inner"), None),
        P(("group", "inner"), None),
        P(("group", "inner"), None),
        P(),
    )
    out_specs = P(("group", "inner"), None)
    return jax.shard_map(per_device, mesh=mesh, in_specs=in_specs, out_specs=out_specs, check_vma=False)
```

```python
import jax
import jax.numpy as jnp
from jax import lax
from jax.experimental import pallas as pl
from jax.experimental.pallas import tpu as pltpu
from jax.sharding import PartitionSpec as P


M = 256
R = 64
LEVELS = 8
NRHS = 128
WIDTH = LEVELS * R + NRHS
NB = 16
SPLIT = 4
F32 = jnp.float32
HI = lax.Precision.HIGHEST


def start_of(level):
    return 128 * ((level - 1) // 2)


def width_of(level):
    return WIDTH - start_of(level)


def offsets(first, last=LEVELS):
    out, at = {}, 0
    for level in range(first, last + 1):
        out[level] = at
        at += width_of(level)
    return out, at


def mm(a, b):
    return lax.dot_general(a, b, (((1,), (0,)), ((), ())), precision=HI, preferred_element_type=F32)


def mm_t(a, b):
    return lax.dot_general(a, b, (((0,), (0,)), ((), ())), precision=HI, preferred_element_type=F32)


def chol_inverse(block, at):
    sub = lax.broadcasted_iota(jnp.int32, (8, 128), 0)
    lane = lax.broadcasted_iota(jnp.int32, (8, 128), 1)
    mine = (lane >= at) & (lane < at + R)
    groups = R // 8
    tiles, pivots = [], [None] * groups
    for g in range(groups):
        eye = jnp.where(lane == sub + (8 * g + R - at), 1.0, 0.0)
        tiles.append(jnp.where(mine, block[8 * g : 8 * g + 8, :], eye))

    def spread(tile, s):
        return jnp.broadcast_to(tile[s : s + 1, :], (8, 128))

    first = 0
    while first < R:
        last = first + NB
        cols = {}
        for r in range(first, last):
            for g in range(r // 8, groups):
                cols[r, g] = jnp.broadcast_to(tiles[g][:, at + r : at + r + 1], (8, 128))
        for i in range(first, last, 2):
            gi, s = i // 8, i % 8
            a, b = spread(cols[i, gi], s), spread(cols[i, gi], s + 1)
            c = spread(cols[i + 1, gi], s + 1)
            inv_a = 1.0 / a
            inv_c = a * (1.0 / (a * c - b * b))
            ratio = b * inv_a
            low = {g: cols[i, g] for g in range(gi, groups)}
            low2 = {g: cols[i + 1, g] - low[g] * ratio for g in range(gi, groups)}
            for r in range(i + 2, last):
                h = r // 8
                mult = spread(low[h], r % 8) * inv_a
                mult2 = spread(low2[h], r % 8) * inv_c
                for g in range(h, groups):
                    cols[r, g] = (cols[r, g] - low[g] * mult) - low2[g] * mult2
            pair = jnp.where(sub == s, a, c - b * ratio)
            pivots[gi] = pair if s == 0 else jnp.where(sub >= s, pair, pivots[gi])
            row = spread(tiles[gi], s)
            row2 = (spread(tiles[gi], s + 1) - row * ratio) * inv_c
            row = row * inv_a
            low[gi] = jnp.where(sub > s, low[gi], 0.0)
            low2[gi] = jnp.where(sub > s + 1, low2[gi], 0.0)
            for g in range(gi, groups):
                tiles[g] = (tiles[g] - low[g] * row) - low2[g] * row2
        first = last
    out = [jnp.where(mine, 0.0, tiles[g] * lax.rsqrt(pivots[g])) for g in range(groups)]
    return jnp.concatenate(out, axis=0)


def lanes_from(j):
    return 128 * (R * j // 128)


def sweep(aug, first, count, y_ref, z_ref, m_ref, late=()):
    base = lanes_from(first)
    for j in range(first, first + count):
        r0 = R * (j - first)
        a0 = lanes_from(j) - base
        at = R * j - lanes_from(j)
        split = M - lanes_from(j)
        minv = chol_inverse(aug[r0 : r0 + R, a0 : a0 + 128], at)
        m_ref[r0 : r0 + R, :] = minv
        for copy in late:
            copy.wait()
        late = ()
        block = aug[r0 : r0 + R, a0:]
        panel = mm(minv, jnp.concatenate([block, block], axis=0))
        z_ref[r0 : r0 + R, :] = panel[:, :split]
        y_ref[r0 : r0 + R, :] = panel[:, split:]
        for i in range(j + 1, 4):
            c0 = R * i - lanes_from(j)
            s0 = lanes_from(i) - lanes_from(j)
            q0 = R * (i - first)
            aug[q0 : q0 + R, a0 + s0 :] -= mm_t(panel[:, c0 : c0 + R], panel[:, s0:])


def leaf_kernel(d_any, b_any, t_any, y_ref, z_ref, m_ref, rest_ref, aug, sem):
    at = M + LEVELS * R
    copies = [
        pltpu.make_async_copy(d_any, aug.at[:, :M], sem.at[0]),
        pltpu.make_async_copy(b_any, aug.at[:, M:at], sem.at[1]),
        pltpu.make_async_copy(t_any, aug.at[:, at:], sem.at[2]),
    ]
    for copy in copies:
        copy.start()
    copies[0].wait()
    sweep(aug, 0, 1, y_ref, z_ref, m_ref, copies[1:])
    rest_ref[...] = aug[R:, :]


def leaf2_kernel(aug_ref, y_ref, z_ref, m_ref, rest_ref, aug):
    aug[...] = aug_ref[...]
    sweep(aug, 1, 1, y_ref, z_ref, m_ref)
    rest_ref[...] = aug[R:, 2 * R :]


def leaf3_kernel(aug_ref, y_ref, z_ref, m_ref, aug):
    aug[...] = aug_ref[...]
    sweep(aug, 2, 2, y_ref, z_ref, m_ref)


def back_kernel(*refs):
    ys, zs, ms, w_ref = refs[:3], refs[3:6], refs[6:9], refs[9]
    for j in range(3, -1, -1):
        part, q0 = min(j, 2), R * max(j - 2, 0)
        o = R - (R * j - lanes_from(j))
        rhs = ys[part][q0 : q0 + R, :]
        if j < 3:
            z = zs[part][q0 : q0 + R, R * (j + 1) - lanes_from(j) :]
            rhs = rhs - mm(z, w_ref[R * (j + 1) :, :])
        w_ref[R * j : R * j + R, :] = mm_t(ms[part][q0 : q0 + R, :], rhs)[o : o + R, :]


def gram_pair(y, pair):
    st = 128 * pair
    return mm_t(y[:, st : st + 128], y[:, st:])


def last_of(first):
    return SPLIT if first <= SPLIT else LEVELS


def row_block(grams, level):
    h = R * ((level - 1) % 2)
    return grams[(level - 1) // 2][h : h + R, :]


def put(ref, first, level, value):
    o = offsets(first)[0][level]
    ref[:, o : o + width_of(level)] = value


def get(ref, first, level):
    o = offsets(first)[0][level]
    return ref[:, o : o + width_of(level)]


def gram_pairs(y_refs, pairs):
    y = jnp.concatenate([y_ref[...] for y_ref in y_refs], axis=0)
    return {pair: gram_pair(y, pair) for pair in pairs}


def gram_kernel(ya_ref, yb_ref, yc_ref, near_ref, far_ref):
    grams = gram_pairs((ya_ref, yb_ref, yc_ref), range(4))
    for level in range(1, SPLIT + 1):
        put(near_ref, 1, level, row_block(grams, level))
    for level in range(SPLIT + 1, LEVELS + 1):
        put(far_ref, SPLIT + 1, level, row_block(grams, level))


def reduce_level(k, coupling_ref, rows, p_ref, m_ref):
    o = R * ((k - 1) % 2)
    ids0 = lax.broadcasted_iota(jnp.int32, (R, 128), 0)
    ids1 = lax.broadcasted_iota(jnp.int32, (R, 128), 1)
    weights = 1.0 / coupling_ref[k - 1 : k, :]
    weights = jnp.concatenate([weights, weights], axis=1)
    cap = rows[:, :128] + jnp.where(ids0 + o == ids1, jnp.broadcast_to(weights, (R, 128)), 0.0)
    minv = chol_inverse(cap, o)
    m_ref[...] = minv
    p = mm(minv, jnp.concatenate([rows, rows], axis=0))
    p_ref[...] = p
    return p


def schur(k, p, first, last):
    sk = start_of(k)
    grams = {}
    for pair in range((first - 1) // 2, (last + 1) // 2):
        st = 128 * pair
        grams[pair] = mm_t(p[:, st - sk : st - sk + 128], p[:, st - sk :])
    return grams


def next_level(k, p, trailing, n_ref):
    last = last_of(k + 1) if k != SPLIT else SPLIT
    if k < last:
        grams = schur(k, p, k + 1, last)
        for level in range(k + 1, last + 1):
            put(n_ref, k + 1, level, trailing(level) - row_block(grams, level))


def first_level_kernel(c_ref, own_ref, ya_ref, yb_ref, yc_ref, dep_ref, p_ref, m_ref, n_ref):
    grams = gram_pairs((ya_ref, yb_ref, yc_ref), range(SPLIT // 2))

    def part(level):
        return get(own_ref, 1, level) + row_block(grams, level)

    p = reduce_level(1, c_ref, part(1), p_ref, m_ref)
    next_level(1, p, part, n_ref)


def level_kernel(k, c_ref, own_ref, got_ref, dep_ref, dep2_ref, p_ref, m_ref, n_ref=None):
    def part(level):
        return get(own_ref, k, level) + get(got_ref, k, level)

    p = reduce_level(k, c_ref, part(k), p_ref, m_ref)
    next_level(k, p, part, n_ref)


def first_far_kernel(own_ref, ya_ref, yb_ref, yc_ref, p_ref, n_ref):
    grams = gram_pairs((ya_ref, yb_ref, yc_ref), range(SPLIT // 2, LEVELS // 2))
    less = schur(1, p_ref[...], SPLIT + 1, LEVELS)
    for level in range(SPLIT + 1, LEVELS + 1):
        put(n_ref, SPLIT + 1, level, get(own_ref, SPLIT + 1, level) + row_block(grams, level) - row_block(less, level))


def far_kernel(k, own_ref, got_ref, p_ref, n_ref):
    less = schur(k, p_ref[...], SPLIT + 1, LEVELS)
    for level in range(SPLIT + 1, LEVELS + 1):
        both = get(own_ref, SPLIT + 1, level) + get(got_ref, SPLIT + 1, level)
        put(n_ref, SPLIT + 1, level, both - row_block(less, level))


def apply_level(k, w, p, minv):
    o = R * ((k - 1) % 2)
    cut = (start_of(k + 1) if k < LEVELS else LEVELS * R) - start_of(k)
    coef = mm_t(minv, p[:, cut:])[R - o : 2 * R - o, :]
    return w[:, cut:] - mm(w[:, o : o + R], coef)


def apply_kernel(k, w_ref, p_ref, m_ref, o_ref):
    o_ref[...] = apply_level(k, w_ref[...], p_ref[...], m_ref[...])


def apply_two_kernel(w_ref, p_ref, m_ref, p2_ref, m2_ref, o_ref):
    two = 2 * R
    coef = mm_t(m_ref[...], p_ref[...])[R:, :]
    coef2 = mm_t(m2_ref[...], p2_ref[:, two:])[:R, :]
    coef = jnp.concatenate([coef[:, two:] - mm(coef[:, R:two], coef2), coef2], axis=0)
    o_ref[...] = w_ref[:, two:] - mm(w_ref[:, :two], coef)


def last_kernel(k, c_ref, own_ref, got_ref, w_ref, o_ref, p_ref, m_ref):
    p = reduce_level(k, c_ref, own_ref[...] + got_ref[...], p_ref, m_ref)
    o_ref[...] = apply_level(k, w_ref[...], p, m_ref[...])


def call(kernel, outs, *args, hbm=(), scratch=(), sems=0, flops=10_000_000):
    vm = pl.BlockSpec(memory_space=pltpu.VMEM)
    hb = pl.BlockSpec(memory_space=pl.ANY)
    shapes = [jax.ShapeDtypeStruct(s, F32) for s in outs]
    extra = [pltpu.SemaphoreType.DMA((sems,))] if sems else []
    return pl.pallas_call(
        kernel,
        out_shape=shapes,
        in_specs=[hb if i in hbm else vm for i in range(len(args))],
        out_specs=[vm] * len(shapes),
        scratch_shapes=[pltpu.VMEM(s, F32) for s in scratch] + extra,
        compiler_params=pltpu.CompilerParams(vmem_limit_bytes=16 << 20),
        cost_estimate=pl.CostEstimate(flops=flops, bytes_accessed=1_000_000, transcendentals=0),
    )(*args)


def exchange(value, level):
    axis = "inner" if level <= 4 else "group"
    mask = {1: 1, 2: 3, 3: 4, 4: 12, 5: 1, 6: 2, 7: 4, 8: 14}[level]
    return lax.ppermute(value, axis, [(s, s ^ mask) for s in range(lax.axis_size(axis))])


def per_device(leaf_blocks, bases, targets, coupling):
    half = M // 2
    leaf_blocks, bases, targets = (
        pltpu.with_memory_space_constraint(a, pltpu.HBM) for a in (leaf_blocks, bases, targets)
    )
    ya, za, ma, rest = call(
        leaf_kernel, [(R, WIDTH), (R, M), (R, 128), (3 * R, M + WIDTH)], leaf_blocks, bases, targets,
        hbm=(0, 1, 2), scratch=[(M, M + WIDTH)], sems=3,
    )
    got_a = exchange(ya, 1)
    yb, zb, mb, rest = call(
        leaf2_kernel, [(R, WIDTH), (R, M), (R, 128), (half, half + WIDTH)], rest,
        scratch=[(3 * R, M + WIDTH)],
    )
    got_b = exchange(yb, 1)
    yc, zc, mc = call(
        leaf3_kernel, [(half, WIDTH), (half, half), (half, 128)], rest,
        scratch=[(half, half + WIDTH)],
    )
    got_y = (got_a, got_b, exchange(yc, 1))
    far_shape = (R, offsets(SPLIT + 1)[1])
    near, far = call(gram_kernel, [(R, offsets(1, SPLIT)[1]), far_shape], ya, yb, yc)
    (w,) = call(back_kernel, [(M, WIDTH)], ya, yb, yc, za, zb, zc, ma, mb, mc)
    got = far_got = None
    dep = w
    for k in range(1, LEVELS):
        outs = [(R, width_of(k)), (R, 128)]
        if k != SPLIT:
            outs.append((R, offsets(k + 1, last_of(k + 1))[1]))
        if k == 1:
            p, minv, near = call(first_level_kernel, outs, coupling, near, *got_y, w, hbm=(5,))
        else:
            kernel = lambda *refs, k=k: level_kernel(k, *refs)
            p, minv, *more = call(kernel, outs, coupling, near, got, dep, far, hbm=(3, 4))
            near = more[0] if more else None
        if k < SPLIT:
            got = exchange(near, k + 1)
        if k == 1:
            (far,) = call(first_far_kernel, [far_shape], far, *got_y, p)
        elif k <= SPLIT:
            kernel = lambda *refs, k=k: far_kernel(k, *refs)
            (far,) = call(kernel, [far_shape], far, far_got, p)
        if k < SPLIT:
            far_got = exchange(far, k + 1)
        if k == SPLIT:
            near = far
        if k >= SPLIT:
            got = exchange(near, k + 1)
        if k == LEVELS - 1:
            kernel = lambda *refs, k=k: apply_kernel(k, *refs)
            (w,) = call(kernel, [(M, width_of(k + 1))], w, p, minv)
        elif k % 2 == 0:
            (w,) = call(apply_two_kernel, [(M, width_of(k + 1))], w, *before, p, minv)
        before = (p, minv)
        if k != SPLIT:
            dep = w
    kernel = lambda *refs: last_kernel(LEVELS, *refs)
    return call(
        kernel, [(M, NRHS)], coupling, near, got, w,
        scratch=[(R, width_of(LEVELS)), (R, 128)],
    )[0]


def solution(mesh):
    in_specs = (
        P(("group", "inner"), None),
        P(("group", "inner"), None),
        P(("group", "inner"), None),
        P(),
    )
    out_specs = P(("group", "inner"), None)
    return jax.shard_map(per_device, mesh=mesh, in_specs=in_specs, out_specs=out_specs, check_vma=False)
```

```python
import jax
import jax.numpy as jnp
from jax import lax
from jax.experimental import pallas as pl
from jax.experimental.pallas import tpu as pltpu
from jax.sharding import PartitionSpec as P


M = 256
R = 64
LEVELS = 8
NRHS = 128
WIDTH = LEVELS * R + NRHS
NB = 16
SPLIT = 4
HALVED = (6, 7)
F32 = jnp.float32
HI = lax.Precision.HIGHEST


def start_of(level):
    return 128 * ((level - 1) // 2)


def width_of(level):
    return WIDTH - start_of(level)


def shared(first):
    return {2: (2, 4), 5: (6, 8), 6: (6, 8)}.get(first, (0, 0))


def last_of(first):
    return SPLIT if first <= SPLIT else LEVELS


def offsets(first):
    out, at = {}, 0
    for level in range(first, last_of(first) + 1):
        out[level] = at
        at += width_in(first, level)
    return out, at


def width_in(first, level):
    return width_of(level) - (128 if level == shared(first)[1] else 0)


def mm(a, b):
    return lax.dot_general(a, b, (((1,), (0,)), ((), ())), precision=HI, preferred_element_type=F32)


def mm_t(a, b):
    return lax.dot_general(a, b, (((0,), (0,)), ((), ())), precision=HI, preferred_element_type=F32)


def chol_inverse(block, at):
    sub = lax.broadcasted_iota(jnp.int32, (8, 128), 0)
    lane = lax.broadcasted_iota(jnp.int32, (8, 128), 1)
    mine = (lane >= at) & (lane < at + R)
    groups = R // 8
    tiles, pivots = [], [None] * groups
    for g in range(groups):
        eye = jnp.where(lane == sub + (8 * g + R - at), 1.0, 0.0)
        tiles.append(jnp.where(mine, block[8 * g : 8 * g + 8, :], eye))

    def spread(tile, s):
        return jnp.broadcast_to(tile[s : s + 1, :], (8, 128))

    first = 0
    while first < R:
        last = first + NB
        cols = {}
        for r in range(first, last):
            for g in range(r // 8, groups):
                cols[r, g] = jnp.broadcast_to(tiles[g][:, at + r : at + r + 1], (8, 128))
        for i in range(first, last, 2):
            gi, s = i // 8, i % 8
            a, b = spread(cols[i, gi], s), spread(cols[i, gi], s + 1)
            c = spread(cols[i + 1, gi], s + 1)
            inv_a = 1.0 / a
            inv_c = a * (1.0 / (a * c - b * b))
            ratio = b * inv_a
            low = {g: cols[i, g] for g in range(gi, groups)}
            low2 = {g: cols[i + 1, g] - low[g] * ratio for g in range(gi, groups)}
            for r in range(i + 2, last):
                h = r // 8
                mult = spread(low[h], r % 8) * inv_a
                mult2 = spread(low2[h], r % 8) * inv_c
                for g in range(h, groups):
                    cols[r, g] = (cols[r, g] - low[g] * mult) - low2[g] * mult2
            pair = jnp.where(sub == s, a, c - b * ratio)
            pivots[gi] = pair if s == 0 else jnp.where(sub >= s, pair, pivots[gi])
            row = spread(tiles[gi], s)
            row2 = (spread(tiles[gi], s + 1) - row * ratio) * inv_c
            row = row * inv_a
            low[gi] = jnp.where(sub > s, low[gi], 0.0)
            low2[gi] = jnp.where(sub > s + 1, low2[gi], 0.0)
            for g in range(gi, groups):
                tiles[g] = (tiles[g] - low[g] * row) - low2[g] * row2
        first = last
    out = [jnp.where(mine, 0.0, tiles[g] * lax.rsqrt(pivots[g])) for g in range(groups)]
    return jnp.concatenate(out, axis=0)


def lanes_from(j):
    return 128 * (R * j // 128)


def sweep(aug, first, count, y_ref, z_ref, m_ref, late=()):
    base = lanes_from(first)
    for j in range(first, first + count):
        r0 = R * (j - first)
        a0 = lanes_from(j) - base
        at = R * j - lanes_from(j)
        split = M - lanes_from(j)
        minv = chol_inverse(aug[r0 : r0 + R, a0 : a0 + 128], at)
        m_ref[r0 : r0 + R, :] = minv
        for copy in late:
            copy.wait()
        late = ()
        block = aug[r0 : r0 + R, a0:]
        panel = mm(minv, jnp.concatenate([block, block], axis=0))
        z_ref[r0 : r0 + R, :] = panel[:, :split]
        y_ref[r0 : r0 + R, :] = panel[:, split:]
        for i in range(j + 1, 4):
            c0 = R * i - lanes_from(j)
            s0 = lanes_from(i) - lanes_from(j)
            q0 = R * (i - first)
            aug[q0 : q0 + R, a0 + s0 :] -= mm_t(panel[:, c0 : c0 + R], panel[:, s0:])


def leaf_kernel(d_any, b_any, t_any, y_ref, z_ref, m_ref, rest_ref, aug, sem):
    at = M + LEVELS * R
    copies = [
        pltpu.make_async_copy(d_any, aug.at[:, :M], sem.at[0]),
        pltpu.make_async_copy(b_any, aug.at[:, M:at], sem.at[1]),
        pltpu.make_async_copy(t_any, aug.at[:, at:], sem.at[2]),
    ]
    for copy in copies:
        copy.start()
    copies[0].wait()
    sweep(aug, 0, 1, y_ref, z_ref, m_ref, copies[1:])
    rest_ref[...] = aug[R:, :]


def leaf2_kernel(aug_ref, y_ref, z_ref, m_ref, rest_ref, aug):
    aug[...] = aug_ref[...]
    sweep(aug, 1, 1, y_ref, z_ref, m_ref)
    rest_ref[...] = aug[R:, 2 * R :]


def leaf3_kernel(aug_ref, y_ref, z_ref, m_ref, aug):
    aug[...] = aug_ref[...]
    sweep(aug, 2, 2, y_ref, z_ref, m_ref)


def back_kernel(*refs):
    ys, zs, ms, w_ref = refs[:3], refs[3:6], refs[6:9], refs[9]
    for j in range(3, -1, -1):
        part, q0 = min(j, 2), R * max(j - 2, 0)
        o = R - (R * j - lanes_from(j))
        rhs = ys[part][q0 : q0 + R, :]
        if j < 3:
            z = zs[part][q0 : q0 + R, R * (j + 1) - lanes_from(j) :]
            rhs = rhs - mm(z, w_ref[R * (j + 1) :, :])
        w_ref[R * j : R * j + R, :] = mm_t(ms[part][q0 : q0 + R, :], rhs)[o : o + R, :]


def gram_pair(y, pair):
    st = 128 * pair
    return mm_t(y[:, st : st + 128], y[:, st:])


def row_block(grams, level):
    h = R * ((level - 1) % 2)
    return grams[(level - 1) // 2][h : h + R, :]


def pack(first, blocks):
    host, guest = shared(first)
    out = dict(blocks)
    if host:
        lane = lax.broadcasted_iota(jnp.int32, (R, 128), 1)
        moved = pltpu.roll(blocks[guest][:, :128], R, 1)
        tile = jnp.where(lane < R, moved, blocks[host][:, :128])
        out[host] = jnp.concatenate([tile, blocks[host][:, 128:]], axis=1)
        out[guest] = blocks[guest][:, 128:]
    return out


def packed(first, value, level):
    o = offsets(first)[0][level]
    return value[:, o : o + width_in(first, level)]


def unpack(first, value, level):
    host, guest = shared(first)
    if level != guest:
        return value(level)
    return jnp.concatenate([pltpu.roll(value(host)[:, :128], R, 1), value(level)], axis=1)


def put(ref, first, level, value):
    o = offsets(first)[0][level]
    ref[:, o : o + width_in(first, level)] = value


def gram_pairs(y_refs, pairs):
    y = jnp.concatenate([y_ref[...] for y_ref in y_refs], axis=0)
    return {pair: gram_pair(y, pair) for pair in pairs}


def gram_kernel(ya_ref, yb_ref, yc_ref, near_ref, far_ref):
    grams = gram_pairs((ya_ref, yb_ref, yc_ref), range(4))
    for level in range(1, SPLIT + 1):
        put(near_ref, 1, level, row_block(grams, level))
    first = SPLIT + 1
    blocks = pack(first, {level: row_block(grams, level) for level in range(first, LEVELS + 1)})
    for level, value in blocks.items():
        put(far_ref, first, level, value)


def reduce_level(k, coupling_ref, rows, p_ref, m_ref):
    o = R * ((k - 1) % 2)
    ids0 = lax.broadcasted_iota(jnp.int32, (R, 128), 0)
    ids1 = lax.broadcasted_iota(jnp.int32, (R, 128), 1)
    weights = 1.0 / coupling_ref[k - 1 : k, :]
    weights = jnp.concatenate([weights, weights], axis=1)
    cap = rows[:, :128] + jnp.where(ids0 + o == ids1, jnp.broadcast_to(weights, (R, 128)), 0.0)
    minv = chol_inverse(cap, o)
    m_ref[...] = minv
    p = mm(minv, jnp.concatenate([rows, rows], axis=0))
    p_ref[...] = p
    return p


def schur(k, p, first, last):
    sk = start_of(k)
    grams = {}
    for pair in range((first - 1) // 2, (last + 1) // 2):
        st = 128 * pair
        grams[pair] = mm_t(p[:, st - sk : st - sk + 128], p[:, st - sk :])
    return grams


def next_level(k, p, trailing, n_ref):
    first, last = k + 1, last_of(k)
    if k >= last:
        return
    grams = schur(k, p, first, last)
    less = {level: row_block(grams, level) for level in range(first, last + 1)}
    if shared(first)[0] and shared(first) == shared(k):
        less = pack(first, less)
        blocks = {level: trailing(level) - less[level] for level in less}
    else:
        blocks = pack(first, {level: unpack(k, trailing, level) - less[level] for level in less})
    for level, value in blocks.items():
        put(n_ref, first, level, value)


def on_core0():
    return lax.rem(lax.axis_index("group"), 2) == 0


def next_half(n_ref, h_ref):
    h_ref[...] = jnp.where(on_core0(), n_ref[: R // 2, :], n_ref[R // 2 :, :])


def first_level_kernel(c_ref, own_ref, ya_ref, yb_ref, yc_ref, dep_ref, p_ref, m_ref, n_ref):
    grams = gram_pairs((ya_ref, yb_ref, yc_ref), range(SPLIT // 2))

    def part(level):
        return packed(1, own_ref, level) + row_block(grams, level)

    p = reduce_level(1, c_ref, part(1), p_ref, m_ref)
    next_level(1, p, part, n_ref)


def level_kernel(k, c_ref, own_ref, got_ref, dep_ref, dep2_ref, p_ref, m_ref, n_ref=None, h_ref=None):
    def part(level):
        return packed(k, own_ref, level) + packed(k, got_ref, level)

    p = reduce_level(k, c_ref, part(k), p_ref, m_ref)
    next_level(k, p, part, n_ref)
    if h_ref is not None:
        next_half(n_ref, h_ref)


def halves_level_kernel(k, c_ref, own_ref, got_ref, other_ref, dep_ref, p_ref, m_ref, n_ref, h_ref=None):
    core0 = on_core0()

    def part(level):
        mine, theirs = packed(k, got_ref, level), packed(k, other_ref, level)
        got = [jnp.where(core0, mine, theirs), jnp.where(core0, theirs, mine)]
        return packed(k, own_ref, level) + jnp.concatenate(got, axis=0)

    p = reduce_level(k, c_ref, part(k), p_ref, m_ref)
    next_level(k, p, part, n_ref)
    if h_ref is not None:
        next_half(n_ref, h_ref)


def first_far_kernel(own_ref, ya_ref, yb_ref, yc_ref, p_ref, n_ref):
    first = SPLIT + 1
    grams = gram_pairs((ya_ref, yb_ref, yc_ref), range(SPLIT // 2, LEVELS // 2))
    less = schur(1, p_ref[...], first, LEVELS)
    more = {level: row_block(grams, level) - row_block(less, level) for level in range(first, LEVELS + 1)}
    for level, value in pack(first, more).items():
        put(n_ref, first, level, packed(first, own_ref, level) + value)


def far_kernel(k, own_ref, got_ref, p_ref, n_ref):
    first = SPLIT + 1
    less = schur(k, p_ref[...], first, LEVELS)
    for level, value in pack(first, {level: row_block(less, level) for level in range(first, LEVELS + 1)}).items():
        both = packed(first, own_ref, level) + packed(first, got_ref, level)
        put(n_ref, first, level, both - value)


def apply_level(k, w, p, minv):
    o = R * ((k - 1) % 2)
    cut = (start_of(k + 1) if k < LEVELS else LEVELS * R) - start_of(k)
    coef = mm_t(minv, p[:, cut:])[R - o : 2 * R - o, :]
    return w[:, cut:] - mm(w[:, o : o + R], coef)


def apply_kernel(k, w_ref, p_ref, m_ref, o_ref):
    o_ref[...] = apply_level(k, w_ref[...], p_ref[...], m_ref[...])


def apply_two_kernel(w_ref, p_ref, m_ref, p2_ref, m2_ref, o_ref):
    two = 2 * R
    coef = mm_t(m_ref[...], p_ref[...])[R:, :]
    coef2 = mm_t(m2_ref[...], p2_ref[:, two:])[:R, :]
    coef = jnp.concatenate([coef[:, two:] - mm(coef[:, R:two], coef2), coef2], axis=0)
    o_ref[...] = w_ref[:, two:] - mm(w_ref[:, :two], coef)


def last_kernel(k, c_ref, own_ref, got_ref, w_ref, o_ref, p_ref, m_ref):
    p = reduce_level(k, c_ref, own_ref[...] + got_ref[...], p_ref, m_ref)
    o_ref[...] = apply_level(k, w_ref[...], p, m_ref[...])


def call(kernel, outs, *args, hbm=(), scratch=(), sems=0, flops=10_000_000):
    vm = pl.BlockSpec(memory_space=pltpu.VMEM)
    hb = pl.BlockSpec(memory_space=pl.ANY)
    shapes = [jax.ShapeDtypeStruct(s, F32) for s in outs]
    extra = [pltpu.SemaphoreType.DMA((sems,))] if sems else []
    return pl.pallas_call(
        kernel,
        out_shape=shapes,
        in_specs=[hb if i in hbm else vm for i in range(len(args))],
        out_specs=[vm] * len(shapes),
        scratch_shapes=[pltpu.VMEM(s, F32) for s in scratch] + extra,
        compiler_params=pltpu.CompilerParams(vmem_limit_bytes=16 << 20),
        cost_estimate=pl.CostEstimate(flops=flops, bytes_accessed=1_000_000, transcendentals=0),
    )(*args)


def exchange(value, level):
    axis = "inner" if level <= 4 else "group"
    mask = {1: 1, 2: 3, 3: 4, 4: 12, 5: 1, 6: 2, 7: 4, 8: 14}[level]
    return lax.ppermute(value, axis, [(s, s ^ mask) for s in range(lax.axis_size(axis))])


def per_device(leaf_blocks, bases, targets, coupling):
    half = M // 2
    leaf_blocks, bases, targets = (
        pltpu.with_memory_space_constraint(a, pltpu.HBM) for a in (leaf_blocks, bases, targets)
    )
    ya, za, ma, rest = call(
        leaf_kernel, [(R, WIDTH), (R, M), (R, 128), (3 * R, M + WIDTH)], leaf_blocks, bases, targets,
        hbm=(0, 1, 2), scratch=[(M, M + WIDTH)], sems=3,
    )
    got_a = exchange(ya, 1)
    yb, zb, mb, rest = call(
        leaf2_kernel, [(R, WIDTH), (R, M), (R, 128), (half, half + WIDTH)], rest,
        scratch=[(3 * R, M + WIDTH)],
    )
    got_b = exchange(yb, 1)
    yc, zc, mc = call(
        leaf3_kernel, [(half, WIDTH), (half, half), (half, 128)], rest,
        scratch=[(half, half + WIDTH)],
    )
    got_y = (got_a, got_b, exchange(yc, 1))
    far_shape = (R, offsets(SPLIT + 1)[1])
    near, far = call(gram_kernel, [(R, offsets(1)[1]), far_shape], ya, yb, yc)
    (w,) = call(back_kernel, [(M, WIDTH)], ya, yb, yc, za, zb, zc, ma, mb, mc)
    got = far_got = None
    dep = w
    for k in range(1, LEVELS):
        outs = [(R, width_of(k)), (R, 128)]
        if k != SPLIT:
            outs.append((R, offsets(k + 1)[1]))
        if k + 1 in HALVED:
            outs.append((R // 2, offsets(k + 1)[1]))
        if k == 1:
            p, minv, near = call(first_level_kernel, outs, coupling, near, *got_y, dep, hbm=(5,))
            more = [near]
        elif k in HALVED:
            kernel = lambda *refs, k=k: halves_level_kernel(k, *refs)
            p, minv, *more = call(kernel, outs, coupling, near, got, other, dep, hbm=(4,))
        else:
            kernel = lambda *refs, k=k: level_kernel(k, *refs)
            p, minv, *more = call(kernel, outs, coupling, near, got, dep, far, hbm=(3, 4))
        near = more[0] if more else None
        if k < SPLIT:
            got = exchange(near, k + 1)
        if k == 1:
            (far,) = call(first_far_kernel, [far_shape], far, *got_y, p)
        elif k <= SPLIT:
            kernel = lambda *refs, k=k: far_kernel(k, *refs)
            (far,) = call(kernel, [far_shape], far, far_got, p)
        if k < SPLIT:
            far_got = exchange(far, k + 1)
        if k == SPLIT:
            near = far
        if k + 1 in HALVED:
            got = exchange(more[1], k + 1)
            other = exchange(got, SPLIT + 1)
        elif k >= SPLIT:
            got = exchange(near, k + 1)
        if k == LEVELS - 1:
            kernel = lambda *refs, k=k: apply_kernel(k, *refs)
            (w,) = call(kernel, [(M, width_of(k + 1))], w, p, minv)
        elif k % 2 == 0:
            (w,) = call(apply_two_kernel, [(M, width_of(k + 1))], w, *before, p, minv)
        before = (p, minv)
        if k != SPLIT:
            dep = w
    kernel = lambda *refs: last_kernel(LEVELS, *refs)
    return call(
        kernel, [(M, NRHS)], coupling, near, got, w,
        scratch=[(R, width_of(LEVELS)), (R, 128)],
    )[0]


def solution(mesh):
    in_specs = (
        P(("group", "inner"), None),
        P(("group", "inner"), None),
        P(("group", "inner"), None),
        P(),
    )
    out_specs = P(("group", "inner"), None)
    return jax.shard_map(per_device, mesh=mesh, in_specs=in_specs, out_specs=out_specs, check_vma=False)
```

```python
import jax
import jax.numpy as jnp
from jax import lax
from jax.experimental import pallas as pl
from jax.experimental.pallas import tpu as pltpu
from jax.sharding import PartitionSpec as P


M = 256
R = 64
LEVELS = 8
NRHS = 128
WIDTH = LEVELS * R + NRHS
NB = 16
SPLIT = 4
HALVED = (6, 7)
F32 = jnp.float32
HI = lax.Precision.HIGHEST


def start_of(level):
    return 128 * ((level - 1) // 2)


def width_of(level):
    return WIDTH - start_of(level)


def shared(first):
    return {2: (2, 4), 5: (6, 8), 6: (6, 8)}.get(first, (0, 0))


def last_of(first):
    return SPLIT if first <= SPLIT else LEVELS


def offsets(first):
    out, at = {}, 0
    for level in range(first, last_of(first) + 1):
        out[level] = at
        at += width_in(first, level)
    return out, at


def width_in(first, level):
    return width_of(level) - (128 if level == shared(first)[1] else 0)


def mm(a, b):
    return lax.dot_general(a, b, (((1,), (0,)), ((), ())), precision=HI, preferred_element_type=F32)


def mm_t(a, b):
    return lax.dot_general(a, b, (((0,), (0,)), ((), ())), precision=HI, preferred_element_type=F32)


def chol_inverse(block, at):
    sub = lax.broadcasted_iota(jnp.int32, (8, 128), 0)
    lane = lax.broadcasted_iota(jnp.int32, (8, 128), 1)
    mine = (lane >= at) & (lane < at + R)
    groups = R // 8
    tiles, pivots = [], [None] * groups
    for g in range(groups):
        eye = jnp.where(lane == sub + (8 * g + R - at), 1.0, 0.0)
        tiles.append(jnp.where(mine, block[8 * g : 8 * g + 8, :], eye))

    def spread(tile, s):
        return jnp.broadcast_to(tile[s : s + 1, :], (8, 128))

    first = 0
    while first < R:
        last = first + NB
        cols = {}
        for r in range(first, last):
            for g in range(r // 8, groups):
                cols[r, g] = jnp.broadcast_to(tiles[g][:, at + r : at + r + 1], (8, 128))
        for i in range(first, last, 2):
            gi, s = i // 8, i % 8
            a, b = spread(cols[i, gi], s), spread(cols[i, gi], s + 1)
            c = spread(cols[i + 1, gi], s + 1)
            inv_a = 1.0 / a
            inv_c = a * (1.0 / (a * c - b * b))
            ratio = b * inv_a
            low = {g: cols[i, g] for g in range(gi, groups)}
            low2 = {g: cols[i + 1, g] - low[g] * ratio for g in range(gi, groups)}
            for r in range(i + 2, last):
                h = r // 8
                mult = spread(low[h], r % 8) * inv_a
                mult2 = spread(low2[h], r % 8) * inv_c
                for g in range(h, groups):
                    cols[r, g] = (cols[r, g] - low[g] * mult) - low2[g] * mult2
            pair = jnp.where(sub == s, a, c - b * ratio)
            pivots[gi] = pair if s == 0 else jnp.where(sub >= s, pair, pivots[gi])
            row = spread(tiles[gi], s)
            row2 = (spread(tiles[gi], s + 1) - row * ratio) * inv_c
            row = row * inv_a
            low[gi] = jnp.where(sub > s, low[gi], 0.0)
            low2[gi] = jnp.where(sub > s + 1, low2[gi], 0.0)
            for g in range(gi, groups):
                tiles[g] = (tiles[g] - low[g] * row) - low2[g] * row2
        first = last
    out = [jnp.where(mine, 0.0, tiles[g] * lax.rsqrt(pivots[g])) for g in range(groups)]
    return jnp.concatenate(out, axis=0)


def lanes_from(j):
    return 128 * (R * j // 128)


def panel_out(rows, j, y_ref, z_ref, m_ref):
    split = M - lanes_from(j)
    minv = chol_inverse(rows[:, :128], R * j - lanes_from(j))
    m_ref[...] = minv
    panel = mm(minv, jnp.concatenate([rows, rows], axis=0))
    z_ref[...] = panel[:, :split]
    y_ref[...] = panel[:, split:]


def leaf_kernel(d_any, b_any, t_any, y_ref, z_ref, m_ref, rest_ref, head, sem):
    at = M + LEVELS * R
    parts = ((d_any, 0, M), (b_any, M, at), (t_any, at, M + WIDTH))
    copies = []
    for n, (rows, dest) in enumerate((((0, R), head), ((R, M), rest_ref))):
        for i, (src, lo, hi) in enumerate(parts):
            copies.append(
                pltpu.make_async_copy(src.at[rows[0] : rows[1], :], dest.at[:, lo:hi], sem.at[3 * n + i])
            )
    for copy in copies:
        copy.start()
    for copy in copies[:3]:
        copy.wait()
    panel_out(head[...], 0, y_ref, z_ref, m_ref)
    for copy in copies[3:]:
        copy.wait()


def leaf_next_kernel(j, rest_ref, *refs):
    ys, zs, outs = refs[:j], refs[j : 2 * j], refs[2 * j :]
    base = lanes_from(j)
    before = jnp.concatenate(
        [jnp.concatenate([zs[i][:, base - lanes_from(i) :], ys[i][...]], axis=1) for i in range(j)], axis=0
    )
    c0 = R * j - base
    rows = rest_ref[R * (j - 1) : R * j, base:] - mm_t(before[:, c0 : c0 + R], before)
    panel_out(rows, j, *outs)


def back_kernel(*refs):
    ys, zs, ms, w_ref = refs[:4], refs[4:8], refs[8:12], refs[12]
    for j in range(3, -1, -1):
        o = R - (R * j - lanes_from(j))
        rhs = ys[j][...]
        if j < 3:
            z = zs[j][:, R * (j + 1) - lanes_from(j) :]
            rhs = rhs - mm(z, w_ref[R * (j + 1) :, :])
        w_ref[R * j : R * j + R, :] = mm_t(ms[j][...], rhs)[o : o + R, :]


def gram_pair(y, pair):
    st = 128 * pair
    return mm_t(y[:, st : st + 128], y[:, st:])


def row_block(grams, level):
    h = R * ((level - 1) % 2)
    return grams[(level - 1) // 2][h : h + R, :]


def pack(first, blocks):
    host, guest = shared(first)
    out = dict(blocks)
    if host:
        lane = lax.broadcasted_iota(jnp.int32, (R, 128), 1)
        moved = pltpu.roll(blocks[guest][:, :128], R, 1)
        tile = jnp.where(lane < R, moved, blocks[host][:, :128])
        out[host] = jnp.concatenate([tile, blocks[host][:, 128:]], axis=1)
        out[guest] = blocks[guest][:, 128:]
    return out


def packed(first, value, level):
    o = offsets(first)[0][level]
    return value[:, o : o + width_in(first, level)]


def unpack(first, value, level):
    host, guest = shared(first)
    if level != guest:
        return value(level)
    return jnp.concatenate([pltpu.roll(value(host)[:, :128], R, 1), value(level)], axis=1)


def put(ref, first, level, value):
    o = offsets(first)[0][level]
    ref[:, o : o + width_in(first, level)] = value


def gram_pairs(y_refs, pairs):
    y = jnp.concatenate([y_ref[...] for y_ref in y_refs], axis=0)
    return {pair: gram_pair(y, pair) for pair in pairs}


def gram_kernel(*refs):
    *y_refs, near_ref, far_ref = refs
    grams = gram_pairs(y_refs, range(4))
    for level in range(1, SPLIT + 1):
        put(near_ref, 1, level, row_block(grams, level))
    first = SPLIT + 1
    blocks = pack(first, {level: row_block(grams, level) for level in range(first, LEVELS + 1)})
    for level, value in blocks.items():
        put(far_ref, first, level, value)


def reduce_level(k, coupling_ref, rows, p_ref, m_ref):
    o = R * ((k - 1) % 2)
    ids0 = lax.broadcasted_iota(jnp.int32, (R, 128), 0)
    ids1 = lax.broadcasted_iota(jnp.int32, (R, 128), 1)
    weights = 1.0 / coupling_ref[k - 1 : k, :]
    weights = jnp.concatenate([weights, weights], axis=1)
    cap = rows[:, :128] + jnp.where(ids0 + o == ids1, jnp.broadcast_to(weights, (R, 128)), 0.0)
    minv = chol_inverse(cap, o)
    m_ref[...] = minv
    p = mm(minv, jnp.concatenate([rows, rows], axis=0))
    p_ref[...] = p
    return p


def schur(k, p, first, last):
    sk = start_of(k)
    grams = {}
    for pair in range((first - 1) // 2, (last + 1) // 2):
        st = 128 * pair
        grams[pair] = mm_t(p[:, st - sk : st - sk + 128], p[:, st - sk :])
    return grams


def next_level(k, p, trailing, n_ref):
    first, last = k + 1, last_of(k)
    if k >= last:
        return
    grams = schur(k, p, first, last)
    less = {level: row_block(grams, level) for level in range(first, last + 1)}
    if shared(first)[0] and shared(first) == shared(k):
        less = pack(first, less)
        blocks = {level: trailing(level) - less[level] for level in less}
    else:
        blocks = pack(first, {level: unpack(k, trailing, level) - less[level] for level in less})
    for level, value in blocks.items():
        put(n_ref, first, level, value)


def on_core0():
    return lax.rem(lax.axis_index("group"), 2) == 0


def next_half(n_ref, h_ref):
    h_ref[...] = jnp.where(on_core0(), n_ref[: R // 2, :], n_ref[R // 2 :, :])


def first_level_kernel(c_ref, own_ref, *refs):
    *y_refs, dep_ref, p_ref, m_ref, n_ref = refs
    grams = gram_pairs(y_refs, range(SPLIT // 2))

    def part(level):
        return packed(1, own_ref, level) + row_block(grams, level)

    p = reduce_level(1, c_ref, part(1), p_ref, m_ref)
    next_level(1, p, part, n_ref)


def level_kernel(k, c_ref, own_ref, got_ref, dep_ref, dep2_ref, p_ref, m_ref, n_ref=None, h_ref=None):
    def part(level):
        return packed(k, own_ref, level) + packed(k, got_ref, level)

    p = reduce_level(k, c_ref, part(k), p_ref, m_ref)
    next_level(k, p, part, n_ref)
    if h_ref is not None:
        next_half(n_ref, h_ref)


def halves_level_kernel(k, c_ref, own_ref, got_ref, other_ref, dep_ref, p_ref, m_ref, n_ref, h_ref=None):
    core0 = on_core0()

    def part(level):
        mine, theirs = packed(k, got_ref, level), packed(k, other_ref, level)
        got = [jnp.where(core0, mine, theirs), jnp.where(core0, theirs, mine)]
        return packed(k, own_ref, level) + jnp.concatenate(got, axis=0)

    p = reduce_level(k, c_ref, part(k), p_ref, m_ref)
    next_level(k, p, part, n_ref)
    if h_ref is not None:
        next_half(n_ref, h_ref)


def first_far_kernel(own_ref, *refs):
    *y_refs, p_ref, n_ref = refs
    first = SPLIT + 1
    grams = gram_pairs(y_refs, range(SPLIT // 2, LEVELS // 2))
    less = schur(1, p_ref[...], first, LEVELS)
    more = {level: row_block(grams, level) - row_block(less, level) for level in range(first, LEVELS + 1)}
    for level, value in pack(first, more).items():
        put(n_ref, first, level, packed(first, own_ref, level) + value)


def far_kernel(k, own_ref, got_ref, p_ref, n_ref):
    first = SPLIT + 1
    less = schur(k, p_ref[...], first, LEVELS)
    for level, value in pack(first, {level: row_block(less, level) for level in range(first, LEVELS + 1)}).items():
        both = packed(first, own_ref, level) + packed(first, got_ref, level)
        put(n_ref, first, level, both - value)


def apply_level(k, w, p, minv):
    o = R * ((k - 1) % 2)
    cut = (start_of(k + 1) if k < LEVELS else LEVELS * R) - start_of(k)
    coef = mm_t(minv, p[:, cut:])[R - o : 2 * R - o, :]
    return w[:, cut:] - mm(w[:, o : o + R], coef)


def apply_kernel(k, w_ref, p_ref, m_ref, o_ref):
    o_ref[...] = apply_level(k, w_ref[...], p_ref[...], m_ref[...])


def apply_two_kernel(w_ref, p_ref, m_ref, p2_ref, m2_ref, o_ref):
    two = 2 * R
    coef = mm_t(m_ref[...], p_ref[...])[R:, :]
    coef2 = mm_t(m2_ref[...], p2_ref[:, two:])[:R, :]
    coef = jnp.concatenate([coef[:, two:] - mm(coef[:, R:two], coef2), coef2], axis=0)
    o_ref[...] = w_ref[:, two:] - mm(w_ref[:, :two], coef)


def last_kernel(k, c_ref, own_ref, got_ref, w_ref, o_ref, p_ref, m_ref):
    p = reduce_level(k, c_ref, own_ref[...] + got_ref[...], p_ref, m_ref)
    o_ref[...] = apply_level(k, w_ref[...], p, m_ref[...])


def call(kernel, outs, *args, hbm=(), scratch=(), sems=0, flops=10_000_000):
    vm = pl.BlockSpec(memory_space=pltpu.VMEM)
    hb = pl.BlockSpec(memory_space=pl.ANY)
    shapes = [jax.ShapeDtypeStruct(s, F32) for s in outs]
    extra = [pltpu.SemaphoreType.DMA((sems,))] if sems else []
    return pl.pallas_call(
        kernel,
        out_shape=shapes,
        in_specs=[hb if i in hbm else vm for i in range(len(args))],
        out_specs=[vm] * len(shapes),
        scratch_shapes=[pltpu.VMEM(s, F32) for s in scratch] + extra,
        compiler_params=pltpu.CompilerParams(vmem_limit_bytes=16 << 20),
        cost_estimate=pl.CostEstimate(flops=flops, bytes_accessed=1_000_000, transcendentals=0),
    )(*args)


def exchange(value, level):
    axis = "inner" if level <= 4 else "group"
    mask = {1: 1, 2: 3, 3: 4, 4: 12, 5: 1, 6: 2, 7: 4, 8: 12}[level]
    return lax.ppermute(value, axis, [(s, s ^ mask) for s in range(lax.axis_size(axis))])


def per_device(leaf_blocks, bases, targets, coupling):
    leaf_blocks, bases, targets = (
        pltpu.with_memory_space_constraint(a, pltpu.HBM) for a in (leaf_blocks, bases, targets)
    )
    ys, zs, ms, got_y = [], [], [], []
    for j in range(4):
        outs = [(R, WIDTH), (R, M - lanes_from(j)), (R, 128)]
        if j == 0:
            y, z, m, rest = call(
                leaf_kernel, outs + [(M - R, M + WIDTH)], leaf_blocks, bases, targets,
                hbm=(0, 1, 2), scratch=[(R, M + WIDTH)], sems=6,
            )
        else:
            kernel = lambda *refs, j=j: leaf_next_kernel(j, *refs)
            y, z, m = call(kernel, outs, rest, *ys, *zs)
        ys.append(y)
        zs.append(z)
        ms.append(m)
        got_y.append(exchange(y, 1))
    far_shape = (R, offsets(SPLIT + 1)[1])
    near, far = call(gram_kernel, [(R, offsets(1)[1]), far_shape], *ys)
    (w,) = call(back_kernel, [(M, WIDTH)], *ys, *zs, *ms)
    got = far_got = None
    dep = w
    for k in range(1, LEVELS):
        outs = [(R, width_of(k)), (R, 128)]
        if k != SPLIT:
            outs.append((R, offsets(k + 1)[1]))
        if k + 1 in HALVED:
            outs.append((R // 2, offsets(k + 1)[1]))
        if k == 1:
            p, minv, near = call(first_level_kernel, outs, coupling, near, *got_y, dep, hbm=(6,))
            more = [near]
        elif k in HALVED:
            kernel = lambda *refs, k=k: halves_level_kernel(k, *refs)
            p, minv, *more = call(kernel, outs, coupling, near, got, other, dep, hbm=(4,))
        else:
            kernel = lambda *refs, k=k: level_kernel(k, *refs)
            p, minv, *more = call(kernel, outs, coupling, near, got, dep, far, hbm=(3, 4))
        near = more[0] if more else None
        if k < SPLIT:
            got = exchange(near, k + 1)
        if k == 1:
            (far,) = call(first_far_kernel, [far_shape], far, *got_y, p)
        elif k <= SPLIT:
            kernel = lambda *refs, k=k: far_kernel(k, *refs)
            (far,) = call(kernel, [far_shape], far, far_got, p)
        if k < SPLIT:
            far_got = exchange(far, k + 1)
        if k == SPLIT:
            near = far
        if k + 1 in HALVED:
            got = exchange(more[1], k + 1)
            other = exchange(got, SPLIT + 1)
        elif k >= SPLIT:
            got = exchange(near, k + 1)
        if k == LEVELS - 1:
            kernel = lambda *refs, k=k: apply_kernel(k, *refs)
            (w,) = call(kernel, [(M, width_of(k + 1))], w, p, minv)
        elif k % 2 == 0:
            (w,) = call(apply_two_kernel, [(M, width_of(k + 1))], w, *before, p, minv)
        before = (p, minv)
        if k != SPLIT:
            dep = w
    kernel = lambda *refs: last_kernel(LEVELS, *refs)
    return call(
        kernel, [(M, NRHS)], coupling, near, got, w,
        scratch=[(R, width_of(LEVELS)), (R, 128)],
    )[0]


def solution(mesh):
    in_specs = (
        P(("group", "inner"), None),
        P(("group", "inner"), None),
        P(("group", "inner"), None),
        P(),
    )
    out_specs = P(("group", "inner"), None)
    return jax.shard_map(per_device, mesh=mesh, in_specs=in_specs, out_specs=out_specs, check_vma=False)
```

```python
import jax
import jax.numpy as jnp
from jax import lax
from jax.experimental import pallas as pl
from jax.experimental.pallas import tpu as pltpu
from jax.sharding import PartitionSpec as P


M = 256
R = 64
LEVELS = 8
NRHS = 128
WIDTH = LEVELS * R + NRHS
BLOCKS = (8, 8, 16, 16, 16)
SPLIT = 4
HALVED = (6, 7)
F32 = jnp.float32
HI = lax.Precision.HIGHEST


def start_of(level):
    return 128 * ((level - 1) // 2)


def width_of(level):
    return WIDTH - start_of(level)


def shared(first):
    return {2: (2, 4), 5: (6, 8), 6: (6, 8)}.get(first, (0, 0))


def last_of(first):
    return SPLIT if first <= SPLIT else LEVELS


def offsets(first):
    out, at = {}, 0
    for level in range(first, last_of(first) + 1):
        out[level] = at
        at += width_in(first, level)
    return out, at


def width_in(first, level):
    return width_of(level) - (128 if level == shared(first)[1] else 0)


def mm(a, b):
    return lax.dot_general(a, b, (((1,), (0,)), ((), ())), precision=HI, preferred_element_type=F32)


def mm_t(a, b):
    return lax.dot_general(a, b, (((0,), (0,)), ((), ())), precision=HI, preferred_element_type=F32)


def chol_inverse(block, at):
    sub = lax.broadcasted_iota(jnp.int32, (8, 128), 0)
    lane = lax.broadcasted_iota(jnp.int32, (8, 128), 1)
    mine = (lane >= at) & (lane < at + R)
    groups = R // 8
    tiles, pivots = [], [None] * groups
    for g in range(groups):
        eye = jnp.where(lane == sub + (8 * g + R - at), 1.0, 0.0)
        tiles.append(jnp.where(mine, block[8 * g : 8 * g + 8, :], eye))

    def spread(tile, s):
        return jnp.broadcast_to(tile[s : s + 1, :], (8, 128))

    first = 0
    for size in BLOCKS:
        last = first + size
        cols = {}
        for r in range(first, last):
            for g in range(r // 8, groups):
                cols[r, g] = jnp.take_along_axis(tiles[g], jnp.full((8, 128), at + r, jnp.int32), axis=1)
        for i in range(first, last, 2):
            gi, s = i // 8, i % 8
            a, b = spread(cols[i, gi], s), spread(cols[i, gi], s + 1)
            c = spread(cols[i + 1, gi], s + 1)
            inv_a = 1.0 / a
            inv_c = a * (1.0 / (a * c - b * b))
            ratio = b * inv_a
            low = {g: cols[i, g] for g in range(gi, groups)}
            low2 = {g: cols[i + 1, g] - low[g] * ratio for g in range(gi, groups)}
            for r in range(i + 2, last):
                h = r // 8
                mult = spread(low[h], r % 8) * inv_a
                mult2 = spread(low2[h], r % 8) * inv_c
                for g in range(h, groups):
                    cols[r, g] = (cols[r, g] - low[g] * mult) - low2[g] * mult2
            pair = jnp.where(sub == s, a, c - b * ratio)
            pivots[gi] = pair if s == 0 else jnp.where(sub >= s, pair, pivots[gi])
            row = spread(tiles[gi], s)
            row2 = (spread(tiles[gi], s + 1) - row * ratio) * inv_c
            row = row * inv_a
            low[gi] = jnp.where(sub > s, low[gi], 0.0)
            low2[gi] = jnp.where(sub > s + 1, low2[gi], 0.0)
            for g in range(gi, groups):
                tiles[g] = (tiles[g] - low[g] * row) - low2[g] * row2
        first = last
    out = [jnp.where(mine, 0.0, tiles[g] * lax.rsqrt(pivots[g])) for g in range(groups)]
    return jnp.concatenate(out, axis=0)


def lanes_from(j):
    return 128 * (R * j // 128)


def panel_out(rows, j, y_ref, z_ref, m_ref):
    split = M - lanes_from(j)
    minv = chol_inverse(rows[:, :128], R * j - lanes_from(j))
    m_ref[...] = minv
    panel = mm(minv, jnp.concatenate([rows, rows], axis=0))
    z_ref[...] = panel[:, :split]
    y_ref[...] = panel[:, split:]


def leaf_kernel(d_any, b_any, t_any, y_ref, z_ref, m_ref, rest_ref, head, sem):
    at = M + LEVELS * R
    parts = ((d_any, 0, M), (b_any, M, at), (t_any, at, M + WIDTH))
    copies = []
    for n, (rows, dest) in enumerate((((0, R), head), ((R, M), rest_ref))):
        for i, (src, lo, hi) in enumerate(parts):
            copies.append(
                pltpu.make_async_copy(src.at[rows[0] : rows[1], :], dest.at[:, lo:hi], sem.at[3 * n + i])
            )
    for copy in copies:
        copy.start()
    for copy in copies[:3]:
        copy.wait()
    panel_out(head[...], 0, y_ref, z_ref, m_ref)
    for copy in copies[3:]:
        copy.wait()


def leaf_next_kernel(j, rest_ref, *refs):
    ys, zs, outs = refs[:j], refs[j : 2 * j], refs[2 * j :]
    base = lanes_from(j)
    before = jnp.concatenate(
        [jnp.concatenate([zs[i][:, base - lanes_from(i) :], ys[i][...]], axis=1) for i in range(j)], axis=0
    )
    c0 = R * j - base
    rows = rest_ref[R * (j - 1) : R * j, base:] - mm_t(before[:, c0 : c0 + R], before)
    panel_out(rows, j, *outs)


def back_kernel(*refs):
    ys, zs, ms, w_ref = refs[:4], refs[4:8], refs[8:12], refs[12]
    for j in range(3, -1, -1):
        o = R - (R * j - lanes_from(j))
        rhs = ys[j][...]
        if j < 3:
            z = zs[j][:, R * (j + 1) - lanes_from(j) :]
            rhs = rhs - mm(z, w_ref[R * (j + 1) :, :])
        w_ref[R * j : R * j + R, :] = mm_t(ms[j][...], rhs)[o : o + R, :]


def gram_pair(y, pair):
    st = 128 * pair
    return mm_t(y[:, st : st + 128], y[:, st:])


def row_block(grams, level):
    h = R * ((level - 1) % 2)
    return grams[(level - 1) // 2][h : h + R, :]


def pack(first, blocks):
    host, guest = shared(first)
    out = dict(blocks)
    if host:
        lane = lax.broadcasted_iota(jnp.int32, (R, 128), 1)
        moved = pltpu.roll(blocks[guest][:, :128], R, 1)
        tile = jnp.where(lane < R, moved, blocks[host][:, :128])
        out[host] = jnp.concatenate([tile, blocks[host][:, 128:]], axis=1)
        out[guest] = blocks[guest][:, 128:]
    return out


def packed(first, value, level):
    o = offsets(first)[0][level]
    return value[:, o : o + width_in(first, level)]


def unpack(first, value, level):
    host, guest = shared(first)
    if level != guest:
        return value(level)
    return jnp.concatenate([pltpu.roll(value(host)[:, :128], R, 1), value(level)], axis=1)


def put(ref, first, level, value):
    o = offsets(first)[0][level]
    ref[:, o : o + width_in(first, level)] = value


def gram_pairs(y_refs, pairs):
    y = jnp.concatenate([y_ref[...] for y_ref in y_refs], axis=0)
    return {pair: gram_pair(y, pair) for pair in pairs}


def gram_kernel(*refs):
    *y_refs, near_ref, far_ref = refs
    grams = gram_pairs(y_refs, range(4))
    for level in range(1, SPLIT + 1):
        put(near_ref, 1, level, row_block(grams, level))
    first = SPLIT + 1
    blocks = pack(first, {level: row_block(grams, level) for level in range(first, LEVELS + 1)})
    for level, value in blocks.items():
        put(far_ref, first, level, value)


def factor(k, coupling_ref, rows):
    o = R * ((k - 1) % 2)
    ids0 = lax.broadcasted_iota(jnp.int32, (R, 128), 0)
    ids1 = lax.broadcasted_iota(jnp.int32, (R, 128), 1)
    weights = 1.0 / coupling_ref[k - 1 : k, :]
    weights = jnp.concatenate([weights, weights], axis=1)
    cap = rows[:, :128] + jnp.where(ids0 + o == ids1, jnp.broadcast_to(weights, (R, 128)), 0.0)
    return chol_inverse(cap, o)


def reduce_level(k, coupling_ref, rows, p_ref, m_ref):
    minv = factor(k, coupling_ref, rows)
    m_ref[...] = minv
    p = mm(minv, jnp.concatenate([rows, rows], axis=0))
    p_ref[...] = p
    return p


def schur(k, p, first, last):
    sk = start_of(k)
    grams = {}
    for pair in range((first - 1) // 2, (last + 1) // 2):
        st = 128 * pair
        grams[pair] = mm_t(p[:, st - sk : st - sk + 128], p[:, st - sk :])
    return grams


def next_level(k, p, trailing, n_ref):
    first, last = k + 1, last_of(k)
    if k >= last:
        return
    grams = schur(k, p, first, last)
    less = {level: row_block(grams, level) for level in range(first, last + 1)}
    if shared(first)[0] and shared(first) == shared(k):
        less = pack(first, less)
        blocks = {level: trailing(level) - less[level] for level in less}
    else:
        blocks = pack(first, {level: unpack(k, trailing, level) - less[level] for level in less})
    for level, value in blocks.items():
        put(n_ref, first, level, value)


def on_core0():
    return lax.rem(lax.axis_index("group"), 2) == 0


def next_half(n_ref, h_ref):
    h_ref[...] = jnp.where(on_core0(), n_ref[: R // 2, :], n_ref[R // 2 :, :])


def first_level_kernel(c_ref, own_ref, *refs):
    *y_refs, dep_ref, p_ref, m_ref, n_ref = refs
    grams = gram_pairs(y_refs, range(SPLIT // 2))

    def part(level):
        return packed(1, own_ref, level) + row_block(grams, level)

    p = reduce_level(1, c_ref, part(1), p_ref, m_ref)
    next_level(1, p, part, n_ref)


def level_kernel(k, c_ref, own_ref, got_ref, dep_ref, dep2_ref, p_ref, m_ref, n_ref=None, h_ref=None):
    def part(level):
        return packed(k, own_ref, level) + packed(k, got_ref, level)

    p = reduce_level(k, c_ref, part(k), p_ref, m_ref)
    next_level(k, p, part, n_ref)
    if h_ref is not None:
        next_half(n_ref, h_ref)


def halves_level_kernel(k, c_ref, own_ref, got_ref, other_ref, dep_ref, p_ref, m_ref, n_ref, h_ref=None):
    core0 = on_core0()

    def part(level):
        mine, theirs = packed(k, got_ref, level), packed(k, other_ref, level)
        got = [jnp.where(core0, mine, theirs), jnp.where(core0, theirs, mine)]
        return packed(k, own_ref, level) + jnp.concatenate(got, axis=0)

    p = reduce_level(k, c_ref, part(k), p_ref, m_ref)
    next_level(k, p, part, n_ref)
    if h_ref is not None:
        next_half(n_ref, h_ref)


def first_far_kernel(own_ref, *refs):
    *y_refs, p_ref, n_ref = refs
    first = SPLIT + 1
    grams = gram_pairs(y_refs, range(SPLIT // 2, LEVELS // 2))
    less = schur(1, p_ref[...], first, LEVELS)
    more = {level: row_block(grams, level) - row_block(less, level) for level in range(first, LEVELS + 1)}
    for level, value in pack(first, more).items():
        put(n_ref, first, level, packed(first, own_ref, level) + value)


def far_kernel(k, own_ref, got_ref, p_ref, n_ref):
    first = SPLIT + 1
    less = schur(k, p_ref[...], first, LEVELS)
    for level, value in pack(first, {level: row_block(less, level) for level in range(first, LEVELS + 1)}).items():
        both = packed(first, own_ref, level) + packed(first, got_ref, level)
        put(n_ref, first, level, both - value)


def apply_level(k, w, p, minv):
    o = R * ((k - 1) % 2)
    cut = (start_of(k + 1) if k < LEVELS else LEVELS * R) - start_of(k)
    coef = mm_t(minv, p[:, cut:])[R - o : 2 * R - o, :]
    return w[:, cut:] - mm(w[:, o : o + R], coef)


def apply_kernel(k, w_ref, p_ref, m_ref, o_ref):
    o_ref[...] = apply_level(k, w_ref[...], p_ref[...], m_ref[...])


def apply_two_kernel(w_ref, p_ref, m_ref, p2_ref, m2_ref, o_ref):
    two = 2 * R
    coef = mm_t(m_ref[...], p_ref[...])[R:, :]
    coef2 = mm_t(m2_ref[...], p2_ref[:, two:])[:R, :]
    coef = jnp.concatenate([coef[:, two:] - mm(coef[:, R:two], coef2), coef2], axis=0)
    o_ref[...] = w_ref[:, two:] - mm(w_ref[:, :two], coef)


def last_kernel(k, c_ref, own_ref, got_ref, w_ref, o_ref):
    o = R * ((k - 1) % 2)
    rows = own_ref[...] + got_ref[...]
    minv = factor(k, c_ref, rows)[:, R - o : 2 * R - o]
    left = lax.dot_general(
        w_ref[:, o : o + R], minv, (((1,), (1,)), ((), ())), precision=HI, preferred_element_type=F32
    )
    o_ref[...] = w_ref[:, 128:] - mm(left, mm(minv, rows[:, 128:]))


def call(kernel, outs, *args, hbm=(), scratch=(), sems=0, flops=10_000_000):
    vm = pl.BlockSpec(memory_space=pltpu.VMEM)
    hb = pl.BlockSpec(memory_space=pl.ANY)
    shapes = [jax.ShapeDtypeStruct(s, F32) for s in outs]
    extra = [pltpu.SemaphoreType.DMA((sems,))] if sems else []
    return pl.pallas_call(
        kernel,
        out_shape=shapes,
        in_specs=[hb if i in hbm else vm for i in range(len(args))],
        out_specs=[vm] * len(shapes),
        scratch_shapes=[pltpu.VMEM(s, F32) for s in scratch] + extra,
        compiler_params=pltpu.CompilerParams(vmem_limit_bytes=16 << 20),
        cost_estimate=pl.CostEstimate(flops=flops, bytes_accessed=1_000_000, transcendentals=0),
    )(*args)


def exchange(value, level):
    axis = "inner" if level <= 4 else "group"
    mask = {1: 1, 2: 3, 3: 4, 4: 12, 5: 1, 6: 2, 7: 4, 8: 12}[level]
    return lax.ppermute(value, axis, [(s, s ^ mask) for s in range(lax.axis_size(axis))])


def per_device(leaf_blocks, bases, targets, coupling):
    leaf_blocks, bases, targets = (
        pltpu.with_memory_space_constraint(a, pltpu.HBM) for a in (leaf_blocks, bases, targets)
    )
    ys, zs, ms, got_y = [], [], [], []
    for j in range(4):
        outs = [(R, WIDTH), (R, M - lanes_from(j)), (R, 128)]
        if j == 0:
            y, z, m, rest = call(
                leaf_kernel, outs + [(M - R, M + WIDTH)], leaf_blocks, bases, targets,
                hbm=(0, 1, 2), scratch=[(R, M + WIDTH)], sems=6,
            )
        else:
            kernel = lambda *refs, j=j: leaf_next_kernel(j, *refs)
            y, z, m = call(kernel, outs, rest, *ys, *zs)
        ys.append(y)
        zs.append(z)
        ms.append(m)
        got_y.append(exchange(y, 1))
    far_shape = (R, offsets(SPLIT + 1)[1])
    near, far = call(gram_kernel, [(R, offsets(1)[1]), far_shape], *ys, *got_y[:3])
    (w,) = call(back_kernel, [(M, WIDTH)], *ys, *zs, *ms)
    got = far_got = None
    dep = w
    for k in range(1, LEVELS):
        outs = [(R, width_of(k)), (R, 128)]
        if k != SPLIT:
            outs.append((R, offsets(k + 1)[1]))
        if k + 1 in HALVED:
            outs.append((R // 2, offsets(k + 1)[1]))
        if k == 1:
            p, minv, near = call(first_level_kernel, outs, coupling, near, *got_y[3:], dep, hbm=(3,))
            more = [near]
        elif k in HALVED:
            kernel = lambda *refs, k=k: halves_level_kernel(k, *refs)
            p, minv, *more = call(kernel, outs, coupling, near, got, other, dep, hbm=(4,))
        else:
            kernel = lambda *refs, k=k: level_kernel(k, *refs)
            p, minv, *more = call(kernel, outs, coupling, near, got, dep, far, hbm=(3, 4))
        near = more[0] if more else None
        if k < SPLIT:
            got = exchange(near, k + 1)
        if k == 1:
            (far,) = call(first_far_kernel, [far_shape], far, *got_y[3:], p)
        elif k <= SPLIT:
            kernel = lambda *refs, k=k: far_kernel(k, *refs)
            (far,) = call(kernel, [far_shape], far, far_got, p)
        if k < SPLIT:
            far_got = exchange(far, k + 1)
        if k == SPLIT:
            near = far
        if k + 1 in HALVED:
            got = exchange(more[1], k + 1)
            other = exchange(got, SPLIT + 1)
        elif k >= SPLIT:
            got = exchange(near, k + 1)
        if k == LEVELS - 1:
            kernel = lambda *refs, k=k: apply_kernel(k, *refs)
            (w,) = call(kernel, [(M, width_of(k + 1))], w, p, minv)
        elif k % 2 == 0:
            (w,) = call(apply_two_kernel, [(M, width_of(k + 1))], w, *before, p, minv)
        before = (p, minv)
        if k != SPLIT:
            dep = w
    kernel = lambda *refs: last_kernel(LEVELS, *refs)
    return call(kernel, [(M, NRHS)], coupling, near, got, w)[0]


def solution(mesh):
    in_specs = (
        P(("group", "inner"), None),
        P(("group", "inner"), None),
        P(("group", "inner"), None),
        P(),
    )
    out_specs = P(("group", "inner"), None)
    return jax.shard_map(per_device, mesh=mesh, in_specs=in_specs, out_specs=out_specs, check_vma=False)
```

```python
import jax
import jax.numpy as jnp
from jax import lax
from jax.experimental import pallas as pl
from jax.experimental.pallas import tpu as pltpu
from jax.sharding import PartitionSpec as P


M = 256
R = 64
LEVELS = 8
NRHS = 128
WIDTH = LEVELS * R + NRHS
BLOCKS = (8, 8, 16, 16, 16)
SPLIT = 4
HALVED = (6, 7)
F32 = jnp.float32
HI = lax.Precision.HIGHEST


def start_of(level):
    return 128 * ((level - 1) // 2)


def width_of(level):
    return WIDTH - start_of(level)


def shared(first):
    return {2: (2, 4), 5: (6, 8), 6: (6, 8)}.get(first, (0, 0))


def last_of(first):
    return SPLIT if first <= SPLIT else LEVELS


def offsets(first):
    out, at = {}, 0
    for level in range(first, last_of(first) + 1):
        out[level] = at
        at += width_in(first, level)
    return out, at


def width_in(first, level):
    return width_of(level) - (128 if level == shared(first)[1] else 0)


def mm(a, b):
    return lax.dot_general(a, b, (((1,), (0,)), ((), ())), precision=HI, preferred_element_type=F32)


def mm_t(a, b):
    return lax.dot_general(a, b, (((0,), (0,)), ((), ())), precision=HI, preferred_element_type=F32)


def chol_inverse(block, at):
    sub = lax.broadcasted_iota(jnp.int32, (8, 128), 0)
    lane = lax.broadcasted_iota(jnp.int32, (8, 128), 1)
    mine = (lane >= at) & (lane < at + R)
    groups = R // 8
    tiles, pivots = [], [None] * groups
    for g in range(groups):
        eye = jnp.where(lane == sub + (8 * g + R - at), 1.0, 0.0)
        tiles.append(jnp.where(mine, block[8 * g : 8 * g + 8, :], eye))

    def spread(tile, s):
        return jnp.broadcast_to(tile[s : s + 1, :], (8, 128))

    first = 0
    for size in BLOCKS:
        last = first + size
        cols = {}
        for r in range(first, last):
            for g in range(r // 8, groups):
                cols[r, g] = jnp.take_along_axis(tiles[g], jnp.full((8, 128), at + r, jnp.int32), axis=1)
        for i in range(first, last, 2):
            gi, s = i // 8, i % 8
            a, b = spread(cols[i, gi], s), spread(cols[i, gi], s + 1)
            c = spread(cols[i + 1, gi], s + 1)
            inv_a = 1.0 / a
            inv_c = a * (1.0 / (a * c - b * b))
            ratio = b * inv_a
            low = {g: cols[i, g] for g in range(gi, groups)}
            low2 = {g: cols[i + 1, g] - low[g] * ratio for g in range(gi, groups)}
            for r in range(i + 2, last):
                h = r // 8
                mult = spread(low[h], r % 8) * inv_a
                mult2 = spread(low2[h], r % 8) * inv_c
                for g in range(h, groups):
                    cols[r, g] = (cols[r, g] - low[g] * mult) - low2[g] * mult2
            pair = jnp.where(sub == s, a, c - b * ratio)
            pivots[gi] = pair if s == 0 else jnp.where(sub >= s, pair, pivots[gi])
            row = spread(tiles[gi], s)
            row2 = (spread(tiles[gi], s + 1) - row * ratio) * inv_c
            row = row * inv_a
            low[gi] = jnp.where(sub > s, low[gi], 0.0)
            low2[gi] = jnp.where(sub > s + 1, low2[gi], 0.0)
            for g in range(gi, groups):
                tiles[g] = (tiles[g] - low[g] * row) - low2[g] * row2
        first = last
    out = [jnp.where(mine, 0.0, tiles[g] * lax.rsqrt(pivots[g])) for g in range(groups)]
    return jnp.concatenate(out, axis=0)


def lanes_from(j):
    return 128 * (R * j // 128)


def panel_out(rows, j, y_ref, z_ref, m_ref):
    split = M - lanes_from(j)
    minv = chol_inverse(rows[:, :128], R * j - lanes_from(j))
    m_ref[...] = minv
    panel = mm(minv, jnp.concatenate([rows, rows], axis=0))
    z_ref[...] = panel[:, :split]
    y_ref[...] = panel[:, split:]


def leaf_kernel(d_any, b_any, t_any, y_ref, z_ref, m_ref, rest_ref, head, sem):
    at = M + LEVELS * R
    parts = ((d_any, 0, M), (b_any, M, at), (t_any, at, M + WIDTH))
    copies = []
    for n, (rows, dest) in enumerate((((0, R), head), ((R, M), rest_ref))):
        for i, (src, lo, hi) in enumerate(parts):
            copies.append(
                pltpu.make_async_copy(src.at[rows[0] : rows[1], :], dest.at[:, lo:hi], sem.at[3 * n + i])
            )
    for copy in copies:
        copy.start()
    for copy in copies[:3]:
        copy.wait()
    panel_out(head[...], 0, y_ref, z_ref, m_ref)
    for copy in copies[3:]:
        copy.wait()


def leaf_next_kernel(j, rest_ref, *refs):
    ys, zs, outs = refs[:j], refs[j : 2 * j], refs[2 * j :]
    base = lanes_from(j)
    before = jnp.concatenate(
        [jnp.concatenate([zs[i][:, base - lanes_from(i) :], ys[i][...]], axis=1) for i in range(j)], axis=0
    )
    c0 = R * j - base
    rows = rest_ref[R * (j - 1) : R * j, base:] - mm_t(before[:, c0 : c0 + R], before)
    panel_out(rows, j, *outs)


def back_kernel(*refs):
    ys, zs, ms, w_ref = refs[:4], refs[4:8], refs[8:12], refs[12]
    for j in range(3, -1, -1):
        o = R - (R * j - lanes_from(j))
        rhs = ys[j][...]
        if j < 3:
            z = zs[j][:, R * (j + 1) - lanes_from(j) :]
            rhs = rhs - mm(z, w_ref[R * (j + 1) :, :])
        w_ref[R * j : R * j + R, :] = mm_t(ms[j][...], rhs)[o : o + R, :]


def gram_pair(y, pair):
    st = 128 * pair
    return mm_t(y[:, st : st + 128], y[:, st:])


def row_block(grams, level):
    h = R * ((level - 1) % 2)
    return grams[(level - 1) // 2][h : h + R, :]


def pack(first, blocks):
    host, guest = shared(first)
    out = dict(blocks)
    if host:
        lane = lax.broadcasted_iota(jnp.int32, (R, 128), 1)
        moved = pltpu.roll(blocks[guest][:, :128], R, 1)
        tile = jnp.where(lane < R, moved, blocks[host][:, :128])
        out[host] = jnp.concatenate([tile, blocks[host][:, 128:]], axis=1)
        out[guest] = blocks[guest][:, 128:]
    return out


def packed(first, value, level):
    o = offsets(first)[0][level]
    return value[:, o : o + width_in(first, level)]


def unpack(first, value, level):
    host, guest = shared(first)
    if level != guest:
        return value(level)
    return jnp.concatenate([pltpu.roll(value(host)[:, :128], R, 1), value(level)], axis=1)


def put(ref, first, level, value):
    o = offsets(first)[0][level]
    ref[:, o : o + width_in(first, level)] = value


def gram_pairs(y_refs, pairs):
    y = jnp.concatenate([y_ref[...] for y_ref in y_refs], axis=0)
    return {pair: gram_pair(y, pair) for pair in pairs}


def gram_kernel(*refs):
    *y_refs, near_ref, far_ref = refs
    grams = gram_pairs(y_refs, range(4))
    for level in range(1, SPLIT + 1):
        put(near_ref, 1, level, row_block(grams, level))
    first = SPLIT + 1
    blocks = pack(first, {level: row_block(grams, level) for level in range(first, LEVELS + 1)})
    for level, value in blocks.items():
        put(far_ref, first, level, value)


def factor(k, coupling_ref, rows):
    o = R * ((k - 1) % 2)
    ids0 = lax.broadcasted_iota(jnp.int32, (R, 128), 0)
    ids1 = lax.broadcasted_iota(jnp.int32, (R, 128), 1)
    weights = 1.0 / coupling_ref[k - 1 : k, :]
    weights = jnp.concatenate([weights, weights], axis=1)
    cap = rows[:, :128] + jnp.where(ids0 + o == ids1, jnp.broadcast_to(weights, (R, 128)), 0.0)
    return chol_inverse(cap, o)


def reduce_level(k, coupling_ref, rows, p_ref, m_ref):
    minv = factor(k, coupling_ref, rows)
    m_ref[...] = minv
    p = mm(minv, jnp.concatenate([rows, rows], axis=0))
    p_ref[...] = p
    return p


def schur(k, p, first, last):
    sk = start_of(k)
    grams = {}
    for pair in range((first - 1) // 2, (last + 1) // 2):
        st = 128 * pair
        grams[pair] = mm_t(p[:, st - sk : st - sk + 128], p[:, st - sk :])
    return grams


def next_level(k, p, trailing, n_ref):
    first, last = k + 1, last_of(k)
    if k >= last:
        return
    grams = schur(k, p, first, last)
    less = {level: row_block(grams, level) for level in range(first, last + 1)}
    if shared(first)[0] and shared(first) == shared(k):
        less = pack(first, less)
        blocks = {level: trailing(level) - less[level] for level in less}
    else:
        blocks = pack(first, {level: unpack(k, trailing, level) - less[level] for level in less})
    for level, value in blocks.items():
        put(n_ref, first, level, value)


def on_core0():
    return lax.rem(lax.axis_index("group"), 2) == 0


def next_half(n_ref, h_ref):
    h_ref[...] = jnp.where(on_core0(), n_ref[: R // 2, :], n_ref[R // 2 :, :])


def first_level_kernel(c_ref, own_ref, *refs):
    *y_refs, dep_ref, p_ref, m_ref, n_ref = refs
    grams = gram_pairs(y_refs, range(SPLIT // 2))

    def part(level):
        return packed(1, own_ref, level) + row_block(grams, level)

    p = reduce_level(1, c_ref, part(1), p_ref, m_ref)
    next_level(1, p, part, n_ref)


def level_kernel(k, c_ref, own_ref, got_ref, dep_ref, dep2_ref, p_ref, m_ref, n_ref=None, h_ref=None):
    def part(level):
        return packed(k, own_ref, level) + packed(k, got_ref, level)

    p = reduce_level(k, c_ref, part(k), p_ref, m_ref)
    next_level(k, p, part, n_ref)
    if h_ref is not None:
        next_half(n_ref, h_ref)


def halves_level_kernel(k, c_ref, own_ref, got_ref, other_ref, dep_ref, p_ref, m_ref, n_ref, h_ref=None):
    core0 = on_core0()

    def part(level):
        mine, theirs = packed(k, got_ref, level), packed(k, other_ref, level)
        got = [jnp.where(core0, mine, theirs), jnp.where(core0, theirs, mine)]
        return packed(k, own_ref, level) + jnp.concatenate(got, axis=0)

    p = reduce_level(k, c_ref, part(k), p_ref, m_ref)
    next_level(k, p, part, n_ref)
    if h_ref is not None:
        next_half(n_ref, h_ref)


def first_far_kernel(own_ref, *refs):
    *y_refs, p_ref, n_ref = refs
    first = SPLIT + 1
    grams = gram_pairs(y_refs, range(SPLIT // 2, LEVELS // 2))
    less = schur(1, p_ref[...], first, LEVELS)
    more = {level: row_block(grams, level) - row_block(less, level) for level in range(first, LEVELS + 1)}
    for level, value in pack(first, more).items():
        put(n_ref, first, level, packed(first, own_ref, level) + value)


def less_kernel(k, own_ref, p_ref, n_ref):
    first = SPLIT + 1
    less = schur(k, p_ref[...], first, LEVELS)
    for level, value in pack(first, {level: row_block(less, level) for level in range(first, LEVELS + 1)}).items():
        put(n_ref, first, level, packed(first, own_ref, level) - value)


def add_kernel(own_ref, got_ref, n_ref):
    n_ref[...] = own_ref[...] + got_ref[...]


def apply_level(k, w, p, minv):
    o = R * ((k - 1) % 2)
    cut = (start_of(k + 1) if k < LEVELS else LEVELS * R) - start_of(k)
    coef = mm_t(minv, p[:, cut:])[R - o : 2 * R - o, :]
    return w[:, cut:] - mm(w[:, o : o + R], coef)


def apply_kernel(k, w_ref, p_ref, m_ref, o_ref):
    o_ref[...] = apply_level(k, w_ref[...], p_ref[...], m_ref[...])


def apply_two_kernel(w_ref, p_ref, m_ref, p2_ref, m2_ref, o_ref):
    two = 2 * R
    coef = mm_t(m_ref[...], p_ref[...])[R:, :]
    coef2 = mm_t(m2_ref[...], p2_ref[:, two:])[:R, :]
    coef = jnp.concatenate([coef[:, two:] - mm(coef[:, R:two], coef2), coef2], axis=0)
    o_ref[...] = w_ref[:, two:] - mm(w_ref[:, :two], coef)


def last_kernel(k, c_ref, own_ref, got_ref, w_ref, o_ref):
    o = R * ((k - 1) % 2)
    rows = own_ref[...] + got_ref[...]
    minv = factor(k, c_ref, rows)[:, R - o : 2 * R - o]
    left = lax.dot_general(
        w_ref[:, o : o + R], minv, (((1,), (1,)), ((), ())), precision=HI, preferred_element_type=F32
    )
    o_ref[...] = w_ref[:, 128:] - mm(left, mm(minv, rows[:, 128:]))


def call(kernel, outs, *args, hbm=(), scratch=(), sems=0, flops=10_000_000):
    vm = pl.BlockSpec(memory_space=pltpu.VMEM)
    hb = pl.BlockSpec(memory_space=pl.ANY)
    shapes = [jax.ShapeDtypeStruct(s, F32) for s in outs]
    extra = [pltpu.SemaphoreType.DMA((sems,))] if sems else []
    return pl.pallas_call(
        kernel,
        out_shape=shapes,
        in_specs=[hb if i in hbm else vm for i in range(len(args))],
        out_specs=[vm] * len(shapes),
        scratch_shapes=[pltpu.VMEM(s, F32) for s in scratch] + extra,
        compiler_params=pltpu.CompilerParams(vmem_limit_bytes=16 << 20),
        cost_estimate=pl.CostEstimate(flops=flops, bytes_accessed=1_000_000, transcendentals=0),
    )(*args)


def exchange(value, level):
    axis = "inner" if level <= 4 else "group"
    mask = {1: 1, 2: 3, 3: 4, 4: 12, 5: 1, 6: 2, 7: 4, 8: 12}[level]
    return lax.ppermute(value, axis, [(s, s ^ mask) for s in range(lax.axis_size(axis))])


def per_device(leaf_blocks, bases, targets, coupling):
    leaf_blocks, bases, targets = (
        pltpu.with_memory_space_constraint(a, pltpu.HBM) for a in (leaf_blocks, bases, targets)
    )
    ys, zs, ms, got_y = [], [], [], []
    for j in range(4):
        outs = [(R, WIDTH), (R, M - lanes_from(j)), (R, 128)]
        if j == 0:
            y, z, m, rest = call(
                leaf_kernel, outs + [(M - R, M + WIDTH)], leaf_blocks, bases, targets,
                hbm=(0, 1, 2), scratch=[(R, M + WIDTH)], sems=6,
            )
        else:
            kernel = lambda *refs, j=j: leaf_next_kernel(j, *refs)
            y, z, m = call(kernel, outs, rest, *ys, *zs)
        ys.append(y)
        zs.append(z)
        ms.append(m)
        got_y.append(exchange(y, 1))
    far_shape = (R, offsets(SPLIT + 1)[1])
    near, far = call(gram_kernel, [(R, offsets(1)[1]), far_shape], *ys, *got_y[:3])
    (w,) = call(back_kernel, [(M, WIDTH)], *ys, *zs, *ms)
    got = far_got = None
    dep = w
    for k in range(1, LEVELS):
        outs = [(R, width_of(k)), (R, 128)]
        if k != SPLIT:
            outs.append((R, offsets(k + 1)[1]))
        if k + 1 in HALVED:
            outs.append((R // 2, offsets(k + 1)[1]))
        if k == 1:
            p, minv, near = call(first_level_kernel, outs, coupling, near, *got_y[3:], dep, hbm=(3,))
            more = [near]
        elif k in HALVED:
            kernel = lambda *refs, k=k: halves_level_kernel(k, *refs)
            p, minv, *more = call(kernel, outs, coupling, near, got, other, dep, hbm=(4,))
        else:
            kernel = lambda *refs, k=k: level_kernel(k, *refs)
            p, minv, *more = call(kernel, outs, coupling, near, got, dep, far, hbm=(3, 4))
        near = more[0] if more else None
        if k < SPLIT:
            got = exchange(near, k + 1)
        if k == 1:
            (far,) = call(first_far_kernel, [far_shape], far, *got_y[3:], p)
        elif k <= SPLIT:
            kernel = lambda *refs, k=k: less_kernel(k, *refs)
            (far,) = call(kernel, [far_shape], far, p)
            (far,) = call(add_kernel, [far_shape], far, far_got)
        if k < SPLIT:
            far_got = exchange(far, k + 1)
        if k == SPLIT:
            near = far
        if k + 1 in HALVED:
            got = exchange(more[1], k + 1)
            other = exchange(got, SPLIT + 1)
        elif k >= SPLIT:
            got = exchange(near, k + 1)
        if k == LEVELS - 1:
            kernel = lambda *refs, k=k: apply_kernel(k, *refs)
            (w,) = call(kernel, [(M, width_of(k + 1))], w, p, minv)
        elif k % 2 == 0:
            (w,) = call(apply_two_kernel, [(M, width_of(k + 1))], w, *before, p, minv)
        before = (p, minv)
        if k != SPLIT:
            dep = w
    kernel = lambda *refs: last_kernel(LEVELS, *refs)
    return call(kernel, [(M, NRHS)], coupling, near, got, w)[0]


def solution(mesh):
    in_specs = (
        P(("group", "inner"), None),
        P(("group", "inner"), None),
        P(("group", "inner"), None),
        P(),
    )
    out_specs = P(("group", "inner"), None)
    return jax.shard_map(per_device, mesh=mesh, in_specs=in_specs, out_specs=out_specs, check_vma=False)
```

```python
import jax
import jax.numpy as jnp
from jax import lax
from jax.experimental import pallas as pl
from jax.experimental.pallas import tpu as pltpu
from jax.sharding import PartitionSpec as P


M = 256
R = 64
LEVELS = 8
NRHS = 128
WIDTH = LEVELS * R + NRHS
BLOCKS = (8, 8, 16, 16, 16)
SPLIT = 4
HALVED = (6, 7)
F32 = jnp.float32
HI = lax.Precision.HIGHEST


def start_of(level):
    return 128 * ((level - 1) // 2)


def width_of(level):
    return WIDTH - start_of(level)


def shared(first):
    return {2: (2, 4), 5: (6, 8), 6: (6, 8)}.get(first, (0, 0))


def last_of(first):
    return SPLIT if first <= SPLIT else LEVELS


def offsets(first):
    out, at = {}, 0
    for level in range(first, last_of(first) + 1):
        out[level] = at
        at += width_in(first, level)
    return out, at


def width_in(first, level):
    return width_of(level) - (128 if level == shared(first)[1] else 0)


def mm(a, b):
    return lax.dot_general(a, b, (((1,), (0,)), ((), ())), precision=HI, preferred_element_type=F32)


def mm_t(a, b):
    return lax.dot_general(a, b, (((0,), (0,)), ((), ())), precision=HI, preferred_element_type=F32)


def chol_inverse(block, at):
    sub = lax.broadcasted_iota(jnp.int32, (8, 128), 0)
    lane = lax.broadcasted_iota(jnp.int32, (8, 128), 1)
    mine = (lane >= at) & (lane < at + R)
    groups = R // 8
    tiles, pivots = [], [None] * groups
    for g in range(groups):
        eye = jnp.where(lane == sub + (8 * g + R - at), 1.0, 0.0)
        tiles.append(jnp.where(mine, block[8 * g : 8 * g + 8, :], eye))

    def spread(tile, s):
        return jnp.broadcast_to(tile[s : s + 1, :], (8, 128))

    first = 0
    for size in BLOCKS:
        last = first + size
        cols = {}
        for r in range(first, last):
            for g in range(r // 8, groups):
                cols[r, g] = jnp.take_along_axis(tiles[g], jnp.full((8, 128), at + r, jnp.int32), axis=1)
        for i in range(first, last, 2):
            gi, s = i // 8, i % 8
            a, b = spread(cols[i, gi], s), spread(cols[i, gi], s + 1)
            c = spread(cols[i + 1, gi], s + 1)
            inv_a = 1.0 / a
            inv_c = a * (1.0 / (a * c - b * b))
            ratio = b * inv_a
            low = {g: cols[i, g] for g in range(gi, groups)}
            low2 = {g: cols[i + 1, g] - low[g] * ratio for g in range(gi, groups)}
            for r in range(i + 2, last):
                h = r // 8
                mult = spread(low[h], r % 8) * inv_a
                mult2 = spread(low2[h], r % 8) * inv_c
                for g in range(h, groups):
                    cols[r, g] = (cols[r, g] - low[g] * mult) - low2[g] * mult2
            pair = jnp.where(sub == s, a, c - b * ratio)
            pivots[gi] = pair if s == 0 else jnp.where(sub >= s, pair, pivots[gi])
            row = spread(tiles[gi], s)
            row2 = (spread(tiles[gi], s + 1) - row * ratio) * inv_c
            row = row * inv_a
            low[gi] = jnp.where(sub > s, low[gi], 0.0)
            low2[gi] = jnp.where(sub > s + 1, low2[gi], 0.0)
            for g in range(gi, groups):
                tiles[g] = (tiles[g] - low[g] * row) - low2[g] * row2
        first = last
    out = [jnp.where(mine, 0.0, tiles[g] * lax.rsqrt(pivots[g])) for g in range(groups)]
    return jnp.concatenate(out, axis=0)


def lanes_from(j):
    return 128 * (R * j // 128)


def panel_out(rows, j, y_ref, z_ref, m_ref):
    split = M - lanes_from(j)
    minv = chol_inverse(rows[:, :128], R * j - lanes_from(j))
    m_ref[...] = minv
    panel = mm(minv, jnp.concatenate([rows, rows], axis=0))
    z_ref[...] = panel[:, :split]
    y_ref[...] = panel[:, split:]


def leaf_kernel(d_any, b_any, t_any, y_ref, z_ref, m_ref, rest_ref, head, sem):
    at = M + LEVELS * R
    parts = ((d_any, 0, M), (b_any, M, at), (t_any, at, M + WIDTH))
    copies = []
    for n, (rows, dest) in enumerate((((0, R), head), ((R, M), rest_ref))):
        for i, (src, lo, hi) in enumerate(parts):
            copies.append(
                pltpu.make_async_copy(src.at[rows[0] : rows[1], :], dest.at[:, lo:hi], sem.at[3 * n + i])
            )
    for copy in copies:
        copy.start()
    for copy in copies[:3]:
        copy.wait()
    panel_out(head[...], 0, y_ref, z_ref, m_ref)
    for copy in copies[3:]:
        copy.wait()


def leaf_next_kernel(j, rest_ref, *refs):
    ys, zs, outs = refs[:j], refs[j : 2 * j], refs[2 * j :]
    base = lanes_from(j)
    before = jnp.concatenate(
        [jnp.concatenate([zs[i][:, base - lanes_from(i) :], ys[i][...]], axis=1) for i in range(j)], axis=0
    )
    c0 = R * j - base
    rows = rest_ref[R * (j - 1) : R * j, base:] - mm_t(before[:, c0 : c0 + R], before)
    panel_out(rows, j, *outs)


def back_kernel(*refs):
    ys, zs, ms, w_ref = refs[:4], refs[4:8], refs[8:12], refs[12]
    for j in range(3, -1, -1):
        o = R - (R * j - lanes_from(j))
        rhs = ys[j][...]
        if j < 3:
            z = zs[j][:, R * (j + 1) - lanes_from(j) :]
            rhs = rhs - mm(z, w_ref[R * (j + 1) :, :])
        w_ref[R * j : R * j + R, :] = mm_t(ms[j][...], rhs)[o : o + R, :]


def gram_pair(y, pair):
    st = 128 * pair
    return mm_t(y[:, st : st + 128], y[:, st:])


def row_block(grams, level):
    h = R * ((level - 1) % 2)
    return grams[(level - 1) // 2][h : h + R, :]


def pack(first, blocks):
    host, guest = shared(first)
    out = dict(blocks)
    if host:
        lane = lax.broadcasted_iota(jnp.int32, (R, 128), 1)
        moved = pltpu.roll(blocks[guest][:, :128], R, 1)
        tile = jnp.where(lane < R, moved, blocks[host][:, :128])
        out[host] = jnp.concatenate([tile, blocks[host][:, 128:]], axis=1)
        out[guest] = blocks[guest][:, 128:]
    return out


def packed(first, value, level):
    o = offsets(first)[0][level]
    if isinstance(value, tuple):
        if level == first:
            return value[0][...]
        value, o = value[1], o - width_in(first, first)
    return value[:, o : o + width_in(first, level)]


def unpack(first, value, level):
    host, guest = shared(first)
    if level != guest:
        return value(level)
    return jnp.concatenate([pltpu.roll(value(host)[:, :128], R, 1), value(level)], axis=1)


def put(ref, first, level, value):
    o = offsets(first)[0][level]
    if isinstance(ref, tuple):
        if level == first:
            ref[0][...] = value
            return
        ref, o = ref[1], o - width_in(first, first)
    ref[:, o : o + width_in(first, level)] = value


def gram_pairs(y_refs, pairs):
    y = jnp.concatenate([y_ref[...] for y_ref in y_refs], axis=0)
    return {pair: gram_pair(y, pair) for pair in pairs}


def gram_kernel(*refs):
    *y_refs, near_ref, far_ref = refs
    grams = gram_pairs(y_refs, range(4))
    for level in range(1, SPLIT + 1):
        put(near_ref, 1, level, row_block(grams, level))
    first = SPLIT + 1
    blocks = pack(first, {level: row_block(grams, level) for level in range(first, LEVELS + 1)})
    for level, value in blocks.items():
        put(far_ref, first, level, value)


def factor(k, coupling_ref, rows):
    o = R * ((k - 1) % 2)
    ids0 = lax.broadcasted_iota(jnp.int32, (R, 128), 0)
    ids1 = lax.broadcasted_iota(jnp.int32, (R, 128), 1)
    weights = 1.0 / coupling_ref[k - 1 : k, :]
    weights = jnp.concatenate([weights, weights], axis=1)
    cap = rows[:, :128] + jnp.where(ids0 + o == ids1, jnp.broadcast_to(weights, (R, 128)), 0.0)
    return chol_inverse(cap, o)


def reduce_level(k, coupling_ref, rows, p_ref, m_ref):
    minv = factor(k, coupling_ref, rows)
    m_ref[...] = minv
    p = mm(minv, jnp.concatenate([rows, rows], axis=0))
    p_ref[...] = p
    return p


def schur(k, p, first, last):
    sk = start_of(k)
    grams = {}
    for pair in range((first - 1) // 2, (last + 1) // 2):
        st = 128 * pair
        grams[pair] = mm_t(p[:, st - sk : st - sk + 128], p[:, st - sk :])
    return grams


def next_level(k, p, trailing, n_ref):
    first, last = k + 1, last_of(k)
    if k >= last:
        return
    grams = schur(k, p, first, last)
    less = {level: row_block(grams, level) for level in range(first, last + 1)}
    if shared(first)[0] and shared(first) == shared(k):
        less = pack(first, less)
        blocks = {level: trailing(level) - less[level] for level in less}
    else:
        blocks = pack(first, {level: unpack(k, trailing, level) - less[level] for level in less})
    for level, value in blocks.items():
        put(n_ref, first, level, value)


def on_core0():
    return lax.rem(lax.axis_index("group"), 2) == 0


def next_half(n_ref, h_ref):
    h_ref[...] = jnp.where(on_core0(), n_ref[: R // 2, :], n_ref[R // 2 :, :])


def first_level_kernel(c_ref, own_ref, *refs):
    *y_refs, dep_ref, p_ref, m_ref, n_ref, n2_ref = refs
    grams = gram_pairs(y_refs, range(SPLIT // 2))

    def part(level):
        return packed(1, own_ref, level) + row_block(grams, level)

    p = reduce_level(1, c_ref, part(1), p_ref, m_ref)
    next_level(1, p, part, (n_ref, n2_ref))


def level_kernel(k, c_ref, own_ref, got_ref, dep_ref, dep2_ref, p_ref, m_ref, n_ref=None, h_ref=None):
    def part(level):
        return packed(k, own_ref, level) + packed(k, got_ref, level)

    p = reduce_level(k, c_ref, part(k), p_ref, m_ref)
    next_level(k, p, part, n_ref)
    if h_ref is not None:
        next_half(n_ref, h_ref)


def head_kernel(k, c_ref, own_ref, got_ref, dep_ref, dep2_ref, p_ref, m_ref):
    reduce_level(k, c_ref, own_ref[...] + got_ref[...], p_ref, m_ref)


def tail_kernel(k, own_ref, own2_ref, got_ref, got2_ref, p_ref, *n_refs):
    def part(level):
        return packed(k, (own_ref, own2_ref), level) + packed(k, (got_ref, got2_ref), level)

    next_level(k, p_ref[...], part, n_refs if len(n_refs) > 1 else n_refs[0])


def halves_level_kernel(k, c_ref, own_ref, got_ref, other_ref, dep_ref, p_ref, m_ref, n_ref, h_ref=None):
    core0 = on_core0()

    def part(level):
        mine, theirs = packed(k, got_ref, level), packed(k, other_ref, level)
        got = [jnp.where(core0, mine, theirs), jnp.where(core0, theirs, mine)]
        return packed(k, own_ref, level) + jnp.concatenate(got, axis=0)

    p = reduce_level(k, c_ref, part(k), p_ref, m_ref)
    next_level(k, p, part, n_ref)
    if h_ref is not None:
        next_half(n_ref, h_ref)


def first_far_kernel(own_ref, *refs):
    *y_refs, p_ref, n_ref = refs
    first = SPLIT + 1
    grams = gram_pairs(y_refs, range(SPLIT // 2, LEVELS // 2))
    less = schur(1, p_ref[...], first, LEVELS)
    more = {level: row_block(grams, level) - row_block(less, level) for level in range(first, LEVELS + 1)}
    for level, value in pack(first, more).items():
        put(n_ref, first, level, packed(first, own_ref, level) + value)


def less_kernel(k, own_ref, p_ref, n_ref):
    first = SPLIT + 1
    less = schur(k, p_ref[...], first, LEVELS)
    for level, value in pack(first, {level: row_block(less, level) for level in range(first, LEVELS + 1)}).items():
        put(n_ref, first, level, packed(first, own_ref, level) - value)


def add_kernel(own_ref, got_ref, n_ref):
    n_ref[...] = own_ref[...] + got_ref[...]


def apply_level(k, w, p, minv):
    o = R * ((k - 1) % 2)
    cut = (start_of(k + 1) if k < LEVELS else LEVELS * R) - start_of(k)
    coef = mm_t(minv, p[:, cut:])[R - o : 2 * R - o, :]
    return w[:, cut:] - mm(w[:, o : o + R], coef)


def apply_kernel(k, w_ref, p_ref, m_ref, o_ref):
    o_ref[...] = apply_level(k, w_ref[...], p_ref[...], m_ref[...])


def apply_two_kernel(w_ref, p_ref, m_ref, p2_ref, m2_ref, o_ref):
    two = 2 * R
    coef = mm_t(m_ref[...], p_ref[...])[R:, :]
    coef2 = mm_t(m2_ref[...], p2_ref[:, two:])[:R, :]
    coef = jnp.concatenate([coef[:, two:] - mm(coef[:, R:two], coef2), coef2], axis=0)
    o_ref[...] = w_ref[:, two:] - mm(w_ref[:, :two], coef)


def last_kernel(k, c_ref, own_ref, got_ref, w_ref, o_ref):
    o = R * ((k - 1) % 2)
    rows = own_ref[...] + got_ref[...]
    minv = factor(k, c_ref, rows)[:, R - o : 2 * R - o]
    left = lax.dot_general(
        w_ref[:, o : o + R], minv, (((1,), (1,)), ((), ())), precision=HI, preferred_element_type=F32
    )
    o_ref[...] = w_ref[:, 128:] - mm(left, mm(minv, rows[:, 128:]))


def call(kernel, outs, *args, hbm=(), scratch=(), sems=0, flops=10_000_000):
    vm = pl.BlockSpec(memory_space=pltpu.VMEM)
    hb = pl.BlockSpec(memory_space=pl.ANY)
    shapes = [jax.ShapeDtypeStruct(s, F32) for s in outs]
    extra = [pltpu.SemaphoreType.DMA((sems,))] if sems else []
    return pl.pallas_call(
        kernel,
        out_shape=shapes,
        in_specs=[hb if i in hbm else vm for i in range(len(args))],
        out_specs=[vm] * len(shapes),
        scratch_shapes=[pltpu.VMEM(s, F32) for s in scratch] + extra,
        compiler_params=pltpu.CompilerParams(vmem_limit_bytes=16 << 20),
        cost_estimate=pl.CostEstimate(flops=flops, bytes_accessed=1_000_000, transcendentals=0),
    )(*args)


def exchange(value, level):
    axis = "inner" if level <= 4 else "group"
    mask = {1: 1, 2: 3, 3: 4, 4: 12, 5: 1, 6: 2, 7: 4, 8: 12}[level]
    return lax.ppermute(value, axis, [(s, s ^ mask) for s in range(lax.axis_size(axis))])


def per_device(leaf_blocks, bases, targets, coupling):
    leaf_blocks, bases, targets = (
        pltpu.with_memory_space_constraint(a, pltpu.HBM) for a in (leaf_blocks, bases, targets)
    )
    ys, zs, ms, got_y = [], [], [], []
    for j in range(4):
        outs = [(R, WIDTH), (R, M - lanes_from(j)), (R, 128)]
        if j == 0:
            y, z, m, rest = call(
                leaf_kernel, outs + [(M - R, M + WIDTH)], leaf_blocks, bases, targets,
                hbm=(0, 1, 2), scratch=[(R, M + WIDTH)], sems=6,
            )
        else:
            kernel = lambda *refs, j=j: leaf_next_kernel(j, *refs)
            y, z, m = call(kernel, outs, rest, *ys, *zs)
        ys.append(y)
        zs.append(z)
        ms.append(m)
        got_y.append(exchange(y, 1))
    far_shape = (R, offsets(SPLIT + 1)[1])
    near, far = call(gram_kernel, [(R, offsets(1)[1]), far_shape], *ys, *got_y[:3])
    (w,) = call(back_kernel, [(M, WIDTH)], *ys, *zs, *ms)
    got = far_got = None
    dep = w
    for k in range(1, LEVELS):
        outs = [(R, width_of(k)), (R, 128)]
        following = []
        if k != SPLIT:
            head, total = width_in(k + 1, k + 1), offsets(k + 1)[1]
            following = [(R, head), (R, total - head)] if k + 1 < SPLIT else [(R, total)]
        if k + 1 in HALVED:
            following.append((R // 2, offsets(k + 1)[1]))
        if k == 1:
            p, minv, *near = call(first_level_kernel, outs + following, coupling, near, *got_y[3:], dep, hbm=(3,))
        elif k < SPLIT:
            kernel = lambda *refs, k=k: head_kernel(k, *refs)
            p, minv = call(kernel, outs, coupling, near[0], got[0], dep, far, hbm=(3, 4))
            kernel = lambda *refs, k=k: tail_kernel(k, *refs)
            near = call(kernel, following, *near, *got, p)
        elif k in HALVED:
            kernel = lambda *refs, k=k: halves_level_kernel(k, *refs)
            p, minv, *near = call(kernel, outs + following, coupling, near[0], got, other, dep, hbm=(4,))
        else:
            kernel = lambda *refs, k=k: level_kernel(k, *refs)
            p, minv, *near = call(kernel, outs + following, coupling, near[0], got, dep, far, hbm=(3, 4))
        if k + 1 < SPLIT:
            got = [exchange(near[0], k + 1), exchange(near[1], k + 1)]
        elif k + 1 == SPLIT:
            got = exchange(near[0], k + 1)
        if k == 1:
            (far,) = call(first_far_kernel, [far_shape], far, *got_y[3:], p)
        elif k <= SPLIT:
            kernel = lambda *refs, k=k: less_kernel(k, *refs)
            (far,) = call(kernel, [far_shape], far, p)
            (far,) = call(add_kernel, [far_shape], far, far_got)
        if k < SPLIT:
            far_got = exchange(far, k + 1)
        if k == SPLIT:
            near = [far]
        if k + 1 in HALVED:
            got = exchange(near[1], k + 1)
            other = exchange(got, SPLIT + 1)
        elif k >= SPLIT:
            got = exchange(near[0], k + 1)
        if k == LEVELS - 1:
            kernel = lambda *refs, k=k: apply_kernel(k, *refs)
            (w,) = call(kernel, [(M, width_of(k + 1))], w, p, minv)
        elif k % 2 == 0:
            (w,) = call(apply_two_kernel, [(M, width_of(k + 1))], w, *before, p, minv)
        before = (p, minv)
        if k > SPLIT:
            dep = w
    kernel = lambda *refs: last_kernel(LEVELS, *refs)
    return call(kernel, [(M, NRHS)], coupling, near[0], got, w)[0]


def solution(mesh):
    in_specs = (
        P(("group", "inner"), None),
        P(("group", "inner"), None),
        P(("group", "inner"), None),
        P(),
    )
    out_specs = P(("group", "inner"), None)
    return jax.shard_map(per_device, mesh=mesh, in_specs=in_specs, out_specs=out_specs, check_vma=False)
```

```python
import jax
import jax.numpy as jnp
from jax import lax
from jax.experimental import pallas as pl
from jax.experimental.pallas import tpu as pltpu
from jax.sharding import PartitionSpec as P


M = 256
R = 64
LEVELS = 8
NRHS = 128
WIDTH = LEVELS * R + NRHS
BLOCKS = (8, 8, 16, 16, 16)
SPLIT = 4
HALVED = (6, 7)
F32 = jnp.float32
HI = lax.Precision.HIGHEST


def start_of(level):
    return 128 * ((level - 1) // 2)


def width_of(level):
    return WIDTH - start_of(level)


def shared(first):
    return {2: (2, 4), 5: (6, 8), 6: (6, 8)}.get(first, (0, 0))


def last_of(first):
    return SPLIT if first <= SPLIT else LEVELS


def offsets(first):
    out, at = {}, 0
    for level in range(first, last_of(first) + 1):
        out[level] = at
        at += width_in(first, level)
    return out, at


def width_in(first, level):
    return width_of(level) - (128 if level == shared(first)[1] else 0)


def mm(a, b):
    return lax.dot_general(a, b, (((1,), (0,)), ((), ())), precision=HI, preferred_element_type=F32)


def mm_t(a, b):
    return lax.dot_general(a, b, (((0,), (0,)), ((), ())), precision=HI, preferred_element_type=F32)


def chol_inverse(block, at):
    sub = lax.broadcasted_iota(jnp.int32, (8, 128), 0)
    lane = lax.broadcasted_iota(jnp.int32, (8, 128), 1)
    mine = (lane >= at) & (lane < at + R)
    groups = R // 8
    tiles, pivots = [], [None] * groups
    for g in range(groups):
        eye = jnp.where(lane == sub + (8 * g + R - at), 1.0, 0.0)
        tiles.append(jnp.where(mine, block[8 * g : 8 * g + 8, :], eye))

    def spread(tile, s):
        return jnp.broadcast_to(tile[s : s + 1, :], (8, 128))

    first = 0
    for size in BLOCKS:
        last = first + size
        cols = {}
        for r in range(first, last):
            for g in range(r // 8, groups):
                cols[r, g] = jnp.take_along_axis(tiles[g], jnp.full((8, 128), at + r, jnp.int32), axis=1)
        for i in range(first, last, 2):
            gi, s = i // 8, i % 8
            a, b = spread(cols[i, gi], s), spread(cols[i, gi], s + 1)
            c = spread(cols[i + 1, gi], s + 1)
            inv_a = 1.0 / a
            inv_c = a * (1.0 / (a * c - b * b))
            ratio = b * inv_a
            low = {g: cols[i, g] for g in range(gi, groups)}
            low2 = {g: cols[i + 1, g] - low[g] * ratio for g in range(gi, groups)}
            for r in range(i + 2, last):
                h = r // 8
                mult = spread(low[h], r % 8) * inv_a
                mult2 = spread(low2[h], r % 8) * inv_c
                for g in range(h, groups):
                    cols[r, g] = (cols[r, g] - low[g] * mult) - low2[g] * mult2
            pair = jnp.where(sub == s, a, c - b * ratio)
            pivots[gi] = pair if s == 0 else jnp.where(sub >= s, pair, pivots[gi])
            row = spread(tiles[gi], s)
            row2 = (spread(tiles[gi], s + 1) - row * ratio) * inv_c
            row = row * inv_a
            low[gi] = jnp.where(sub > s, low[gi], 0.0)
            low2[gi] = jnp.where(sub > s + 1, low2[gi], 0.0)
            for g in range(gi, groups):
                tiles[g] = (tiles[g] - low[g] * row) - low2[g] * row2
        first = last
    out = [jnp.where(mine, 0.0, tiles[g] * lax.rsqrt(pivots[g])) for g in range(groups)]
    return jnp.concatenate(out, axis=0)


def lanes_from(j):
    return 128 * (R * j // 128)


def panel_out(rows, j, y_ref, z_ref, m_ref):
    split = M - lanes_from(j)
    minv = chol_inverse(rows[:, :128], R * j - lanes_from(j))
    m_ref[...] = minv
    panel = mm(minv, jnp.concatenate([rows, rows], axis=0))
    z_ref[...] = panel[:, :split]
    y_ref[...] = panel[:, split:]


def leaf_kernel(d_any, b_any, t_any, y_ref, z_ref, m_ref, rest_ref, head, sem):
    at = M + LEVELS * R
    parts = ((d_any, 0, M), (b_any, M, at), (t_any, at, M + WIDTH))
    copies = []
    for n, (rows, dest) in enumerate((((0, R), head), ((R, M), rest_ref))):
        for i, (src, lo, hi) in enumerate(parts):
            copies.append(
                pltpu.make_async_copy(src.at[rows[0] : rows[1], :], dest.at[:, lo:hi], sem.at[3 * n + i])
            )
    for copy in copies:
        copy.start()
    for copy in copies[:3]:
        copy.wait()
    panel_out(head[...], 0, y_ref, z_ref, m_ref)
    for copy in copies[3:]:
        copy.wait()


def leaf_next_kernel(j, rest_ref, *refs):
    ys, zs, outs = refs[:j], refs[j : 2 * j], refs[2 * j :]
    base = lanes_from(j)
    before = jnp.concatenate(
        [jnp.concatenate([zs[i][:, base - lanes_from(i) :], ys[i][...]], axis=1) for i in range(j)], axis=0
    )
    c0 = R * j - base
    rows = rest_ref[R * (j - 1) : R * j, base:] - mm_t(before[:, c0 : c0 + R], before)
    panel_out(rows, j, *outs)


def back_kernel(*refs):
    ys, zs, ms, w_ref = refs[:4], refs[4:8], refs[8:12], refs[12]
    for j in range(3, -1, -1):
        o = R - (R * j - lanes_from(j))
        rhs = ys[j][...]
        if j < 3:
            z = zs[j][:, R * (j + 1) - lanes_from(j) :]
            rhs = rhs - mm(z, w_ref[R * (j + 1) :, :])
        w_ref[R * j : R * j + R, :] = mm_t(ms[j][...], rhs)[o : o + R, :]


def gram_pair(y, pair):
    st = 128 * pair
    return mm_t(y[:, st : st + 128], y[:, st:])


def row_block(grams, level):
    h = R * ((level - 1) % 2)
    return grams[(level - 1) // 2][h : h + R, :]


def pack(first, blocks):
    host, guest = shared(first)
    out = dict(blocks)
    if host:
        lane = lax.broadcasted_iota(jnp.int32, (R, 128), 1)
        moved = pltpu.roll(blocks[guest][:, :128], R, 1)
        tile = jnp.where(lane < R, moved, blocks[host][:, :128])
        out[host] = jnp.concatenate([tile, blocks[host][:, 128:]], axis=1)
        out[guest] = blocks[guest][:, 128:]
    return out


def packed(first, value, level):
    o = offsets(first)[0][level]
    if isinstance(value, tuple):
        if level == first:
            return value[0][...]
        value, o = value[1], o - width_in(first, first)
    return value[:, o : o + width_in(first, level)]


def unpack(first, value, level):
    host, guest = shared(first)
    if level != guest:
        return value(level)
    return jnp.concatenate([pltpu.roll(value(host)[:, :128], R, 1), value(level)], axis=1)


def put(ref, first, level, value):
    o = offsets(first)[0][level]
    if isinstance(ref, tuple):
        if level == first:
            ref[0][...] = value
            return
        ref, o = ref[1], o - width_in(first, first)
    ref[:, o : o + width_in(first, level)] = value


def gram_pairs(y_refs, pairs):
    y = jnp.concatenate([y_ref[...] for y_ref in y_refs], axis=0)
    return {pair: gram_pair(y, pair) for pair in pairs}


def gram_kernel(*refs):
    *y_refs, near_ref, far_ref = refs
    grams = gram_pairs(y_refs, range(4))
    for level in range(1, SPLIT + 1):
        put(near_ref, 1, level, row_block(grams, level))
    first = SPLIT + 1
    blocks = pack(first, {level: row_block(grams, level) for level in range(first, LEVELS + 1)})
    for level, value in blocks.items():
        put(far_ref, first, level, value)


def factor(k, coupling_ref, rows):
    o = R * ((k - 1) % 2)
    ids0 = lax.broadcasted_iota(jnp.int32, (R, 128), 0)
    ids1 = lax.broadcasted_iota(jnp.int32, (R, 128), 1)
    weights = 1.0 / coupling_ref[k - 1 : k, :]
    weights = jnp.concatenate([weights, weights], axis=1)
    cap = rows[:, :128] + jnp.where(ids0 + o == ids1, jnp.broadcast_to(weights, (R, 128)), 0.0)
    return chol_inverse(cap, o)


def reduce_level(k, coupling_ref, rows, p_ref, m_ref):
    minv = factor(k, coupling_ref, rows)
    m_ref[...] = minv
    p = mm(minv, jnp.concatenate([rows, rows], axis=0))
    p_ref[...] = p
    return p


def schur(k, p, first, last):
    sk = start_of(k)
    grams = {}
    for pair in range((first - 1) // 2, (last + 1) // 2):
        st = 128 * pair
        grams[pair] = mm_t(p[:, st - sk : st - sk + 128], p[:, st - sk :])
    return grams


def next_level(k, p, trailing, n_ref):
    first, last = k + 1, last_of(k)
    if k >= last:
        return
    grams = schur(k, p, first, last)
    less = {level: row_block(grams, level) for level in range(first, last + 1)}
    if shared(first)[0] and shared(first) == shared(k):
        less = pack(first, less)
        blocks = {level: trailing(level) - less[level] for level in less}
    else:
        blocks = pack(first, {level: unpack(k, trailing, level) - less[level] for level in less})
    for level, value in blocks.items():
        put(n_ref, first, level, value)


def on_core0():
    return lax.rem(lax.axis_index("group"), 2) == 0


def next_half(n_ref, h_ref):
    h_ref[...] = jnp.where(on_core0(), n_ref[: R // 2, :], n_ref[R // 2 :, :])


def first_level_kernel(c_ref, own_ref, *refs):
    *y_refs, dep_ref, p_ref, m_ref, n_ref, n2_ref = refs
    grams = gram_pairs(y_refs, range(SPLIT // 2))

    def part(level):
        return packed(1, own_ref, level) + row_block(grams, level)

    p = reduce_level(1, c_ref, part(1), p_ref, m_ref)
    next_level(1, p, part, (n_ref, n2_ref))


def level_kernel(k, c_ref, own_ref, got_ref, dep_ref, dep2_ref, p_ref, m_ref, n_ref=None, h_ref=None):
    def part(level):
        return packed(k, own_ref, level) + packed(k, got_ref, level)

    p = reduce_level(k, c_ref, part(k), p_ref, m_ref)
    next_level(k, p, part, n_ref)
    if h_ref is not None:
        next_half(n_ref, h_ref)


def head_kernel(k, c_ref, own_ref, got_ref, dep_ref, dep2_ref, p_ref, m_ref):
    reduce_level(k, c_ref, own_ref[...] + got_ref[...], p_ref, m_ref)


def tail_kernel(k, own_ref, own2_ref, got_ref, got2_ref, p_ref, *n_refs):
    def part(level):
        return packed(k, (own_ref, own2_ref), level) + packed(k, (got_ref, got2_ref), level)

    next_level(k, p_ref[...], part, n_refs if len(n_refs) > 1 else n_refs[0])


def halves_level_kernel(k, c_ref, own_ref, got_ref, other_ref, dep_ref, p_ref, m_ref, n_ref, h_ref=None):
    core0 = on_core0()

    def part(level):
        mine, theirs = packed(k, got_ref, level), packed(k, other_ref, level)
        got = [jnp.where(core0, mine, theirs), jnp.where(core0, theirs, mine)]
        return packed(k, own_ref, level) + jnp.concatenate(got, axis=0)

    p = reduce_level(k, c_ref, part(k), p_ref, m_ref)
    next_level(k, p, part, n_ref)
    if h_ref is not None:
        next_half(n_ref, h_ref)


def first_far_kernel(own_ref, *refs):
    *y_refs, p_ref, n_ref = refs
    first = SPLIT + 1
    grams = gram_pairs(y_refs, range(SPLIT // 2, LEVELS // 2))
    less = schur(1, p_ref[...], first, LEVELS)
    more = {level: row_block(grams, level) - row_block(less, level) for level in range(first, LEVELS + 1)}
    for level, value in pack(first, more).items():
        put(n_ref, first, level, packed(first, own_ref, level) + value)


def less_kernel(k, own_ref, p_ref, n_ref):
    first = SPLIT + 1
    less = schur(k, p_ref[...], first, LEVELS)
    for level, value in pack(first, {level: row_block(less, level) for level in range(first, LEVELS + 1)}).items():
        put(n_ref, first, level, packed(first, own_ref, level) - value)


def add_kernel(own_ref, got_ref, n_ref):
    n_ref[...] = own_ref[...] + got_ref[...]


def apply_level(k, w, p, minv):
    o = R * ((k - 1) % 2)
    cut = (start_of(k + 1) if k < LEVELS else LEVELS * R) - start_of(k)
    coef = mm_t(minv, p[:, cut:])[R - o : 2 * R - o, :]
    return w[:, cut:] - mm(w[:, o : o + R], coef)


def apply_kernel(k, w_ref, p_ref, m_ref, o_ref):
    o_ref[...] = apply_level(k, w_ref[...], p_ref[...], m_ref[...])


def apply_two_kernel(w_ref, p_ref, m_ref, p2_ref, m2_ref, o_ref):
    two = 2 * R
    coef = mm_t(m_ref[...], p_ref[...])[R:, :]
    coef2 = mm_t(m2_ref[...], p2_ref[:, two:])[:R, :]
    coef = jnp.concatenate([coef[:, two:] - mm(coef[:, R:two], coef2), coef2], axis=0)
    o_ref[...] = w_ref[:, two:] - mm(w_ref[:, :two], coef)


def last_kernel(k, c_ref, own_ref, got_ref, w_ref, o_ref):
    o = R * ((k - 1) % 2)
    rows = own_ref[...] + got_ref[...]
    minv = factor(k, c_ref, rows)[:, R - o : 2 * R - o]
    left = lax.dot_general(
        w_ref[:, o : o + R], minv, (((1,), (1,)), ((), ())), precision=HI, preferred_element_type=F32
    )
    o_ref[...] = w_ref[:, 128:] - mm(left, mm(minv, rows[:, 128:]))


def call(kernel, outs, *args, hbm=(), scratch=(), sems=0, flops=10_000_000):
    vm = pl.BlockSpec(memory_space=pltpu.VMEM)
    hb = pl.BlockSpec(memory_space=pl.ANY)
    shapes = [jax.ShapeDtypeStruct(s, F32) for s in outs]
    extra = [pltpu.SemaphoreType.DMA((sems,))] if sems else []
    return pl.pallas_call(
        kernel,
        out_shape=shapes,
        in_specs=[hb if i in hbm else vm for i in range(len(args))],
        out_specs=[vm] * len(shapes),
        scratch_shapes=[pltpu.VMEM(s, F32) for s in scratch] + extra,
        compiler_params=pltpu.CompilerParams(vmem_limit_bytes=16 << 20),
        cost_estimate=pl.CostEstimate(flops=flops, bytes_accessed=1_000_000, transcendentals=0),
    )(*args)


def exchange(value, level):
    axis = "inner" if level <= 4 else "group"
    mask = {1: 1, 2: 3, 3: 4, 4: 12, 5: 1, 6: 2, 7: 4, 8: 12}[level]
    return lax.ppermute(value, axis, [(s, s ^ mask) for s in range(lax.axis_size(axis))])


def per_device(leaf_blocks, bases, targets, coupling):
    leaf_blocks, bases, targets = (
        pltpu.with_memory_space_constraint(a, pltpu.HBM) for a in (leaf_blocks, bases, targets)
    )
    ys, zs, ms, got_y = [], [], [], []
    for j in range(4):
        outs = [(R, WIDTH), (R, M - lanes_from(j)), (R, 128)]
        if j == 0:
            y, z, m, rest = call(
                leaf_kernel, outs + [(M - R, M + WIDTH)], leaf_blocks, bases, targets,
                hbm=(0, 1, 2), scratch=[(R, M + WIDTH)], sems=6,
            )
        else:
            kernel = lambda *refs, j=j: leaf_next_kernel(j, *refs)
            y, z, m = call(kernel, outs, rest, *ys, *zs)
        ys.append(y)
        zs.append(z)
        ms.append(m)
        got_y.append(exchange(y, 1))
    far_shape = (R, offsets(SPLIT + 1)[1])
    near, far = call(gram_kernel, [(R, offsets(1)[1]), far_shape], *ys, *got_y[:2])
    (w,) = call(back_kernel, [(M, WIDTH)], *ys, *zs, *ms)
    got = far_got = None
    dep = w
    for k in range(1, LEVELS):
        outs = [(R, width_of(k)), (R, 128)]
        following = []
        if k != SPLIT:
            head, total = width_in(k + 1, k + 1), offsets(k + 1)[1]
            following = [(R, head), (R, total - head)] if k + 1 < SPLIT else [(R, total)]
        if k + 1 in HALVED:
            following.append((R // 2, offsets(k + 1)[1]))
        if k == 1:
            p, minv, *near = call(first_level_kernel, outs + following, coupling, near, *got_y[2:], dep, hbm=(4,))
        elif k < SPLIT:
            kernel = lambda *refs, k=k: head_kernel(k, *refs)
            p, minv = call(kernel, outs, coupling, near[0], got[0], dep, far, hbm=(3, 4))
            kernel = lambda *refs, k=k: tail_kernel(k, *refs)
            near = call(kernel, following, *near, *got, p)
        elif k in HALVED:
            kernel = lambda *refs, k=k: halves_level_kernel(k, *refs)
            p, minv, *near = call(kernel, outs + following, coupling, near[0], got, other, dep, hbm=(4,))
        else:
            kernel = lambda *refs, k=k: level_kernel(k, *refs)
            p, minv, *near = call(kernel, outs + following, coupling, near[0], got, dep, far, hbm=(3, 4))
        if k + 1 < SPLIT:
            got = [exchange(near[0], k + 1), exchange(near[1], k + 1)]
        elif k + 1 == SPLIT:
            got = exchange(near[0], k + 1)
        if k == 1:
            (far,) = call(first_far_kernel, [far_shape], far, *got_y[2:], p)
        elif k <= SPLIT:
            kernel = lambda *refs, k=k: less_kernel(k, *refs)
            (far,) = call(kernel, [far_shape], far, p)
            (far,) = call(add_kernel, [far_shape], far, far_got)
        if k < SPLIT:
            far_got = exchange(far, k + 1)
        if k == SPLIT:
            near = [far]
        if k + 1 in HALVED:
            got = exchange(near[1], k + 1)
            other = exchange(got, SPLIT + 1)
        elif k >= SPLIT:
            got = exchange(near[0], k + 1)
        if k == LEVELS - 1:
            kernel = lambda *refs, k=k: apply_kernel(k, *refs)
            (w,) = call(kernel, [(M, width_of(k + 1))], w, p, minv)
        elif k % 2 == 0:
            (w,) = call(apply_two_kernel, [(M, width_of(k + 1))], w, *before, p, minv)
        before = (p, minv)
        if k > SPLIT:
            dep = w
    kernel = lambda *refs: last_kernel(LEVELS, *refs)
    return call(kernel, [(M, NRHS)], coupling, near[0], got, w)[0]


def solution(mesh):
    in_specs = (
        P(("group", "inner"), None),
        P(("group", "inner"), None),
        P(("group", "inner"), None),
        P(),
    )
    out_specs = P(("group", "inner"), None)
    return jax.shard_map(per_device, mesh=mesh, in_specs=in_specs, out_specs=out_specs, check_vma=False)
```

```python
import jax
import jax.numpy as jnp
from jax import lax
from jax.experimental import pallas as pl
from jax.experimental.pallas import tpu as pltpu
from jax.sharding import PartitionSpec as P


M = 256
R = 64
LEVELS = 8
NRHS = 128
WIDTH = LEVELS * R + NRHS
BLOCKS = (8, 8, 16, 16, 16)
SPLIT = 4
HALVED = (6, 7)
F32 = jnp.float32
HI = lax.Precision.HIGHEST


def start_of(level):
    return 128 * ((level - 1) // 2)


def width_of(level):
    return WIDTH - start_of(level)


def shared(first):
    return {2: (2, 4), 5: (6, 8), 6: (6, 8)}.get(first, (0, 0))


def last_of(first):
    return SPLIT if first <= SPLIT else LEVELS


def offsets(first):
    out, at = {}, 0
    for level in range(first, last_of(first) + 1):
        out[level] = at
        at += width_in(first, level)
    return out, at


def width_in(first, level):
    return width_of(level) - (128 if level == shared(first)[1] else 0)


def mm(a, b):
    return lax.dot_general(a, b, (((1,), (0,)), ((), ())), precision=HI, preferred_element_type=F32)


def mm_t(a, b):
    return lax.dot_general(a, b, (((0,), (0,)), ((), ())), precision=HI, preferred_element_type=F32)


def chol_inverse(block, at):
    sub = lax.broadcasted_iota(jnp.int32, (8, 128), 0)
    lane = lax.broadcasted_iota(jnp.int32, (8, 128), 1)
    mine = (lane >= at) & (lane < at + R)
    groups = R // 8
    tiles, pivots = [], [None] * groups
    for g in range(groups):
        eye = jnp.where(lane == sub + (8 * g + R - at), 1.0, 0.0)
        tiles.append(jnp.where(mine, block[8 * g : 8 * g + 8, :], eye))

    def spread(tile, s):
        return jnp.broadcast_to(tile[s : s + 1, :], (8, 128))

    first = 0
    for size in BLOCKS:
        last = first + size
        cols = {}
        for r in range(first, last):
            for g in range(r // 8, groups):
                cols[r, g] = jnp.take_along_axis(tiles[g], jnp.full((8, 128), at + r, jnp.int32), axis=1)
        for i in range(first, last, 2):
            gi, s = i // 8, i % 8
            a, b = spread(cols[i, gi], s), spread(cols[i, gi], s + 1)
            c = spread(cols[i + 1, gi], s + 1)
            inv_a = 1.0 / a
            inv_c = a * (1.0 / (a * c - b * b))
            ratio = b * inv_a
            low = {g: cols[i, g] for g in range(gi, groups)}
            low2 = {g: cols[i + 1, g] - low[g] * ratio for g in range(gi, groups)}
            for r in range(i + 2, last):
                h = r // 8
                mult = spread(low[h], r % 8) * inv_a
                mult2 = spread(low2[h], r % 8) * inv_c
                for g in range(h, groups):
                    cols[r, g] = (cols[r, g] - low[g] * mult) - low2[g] * mult2
            pair = jnp.where(sub == s, a, c - b * ratio)
            pivots[gi] = pair if s == 0 else jnp.where(sub >= s, pair, pivots[gi])
            row = spread(tiles[gi], s)
            row2 = (spread(tiles[gi], s + 1) - row * ratio) * inv_c
            row = row * inv_a
            low[gi] = jnp.where(sub > s, low[gi], 0.0)
            low2[gi] = jnp.where(sub > s + 1, low2[gi], 0.0)
            for g in range(gi, groups):
                tiles[g] = (tiles[g] - low[g] * row) - low2[g] * row2
        first = last
    out = [jnp.where(mine, 0.0, tiles[g] * lax.rsqrt(pivots[g])) for g in range(groups)]
    return jnp.concatenate(out, axis=0)


def lanes_from(j):
    return 128 * (R * j // 128)


def panel_out(rows, j, y_ref, z_ref, m_ref, minv=None):
    split = M - lanes_from(j)
    if minv is None:
        minv = chol_inverse(rows[:, :128], R * j - lanes_from(j))
    m_ref[...] = minv
    panel = mm(minv, jnp.concatenate([rows, rows], axis=0))
    z_ref[...] = panel[:, :split]
    y_ref[...] = panel[:, split:]


def leaf_kernel(d_any, b_any, t_any, y_ref, z_ref, m_ref, rest_ref, head, sem):
    at = M + LEVELS * R
    parts = ((d_any, 0, M), (b_any, M, at), (t_any, at, M + WIDTH))
    copies = []
    for n, (rows, dest) in enumerate((((0, R), head), ((R, M), rest_ref))):
        for i, (src, lo, hi) in enumerate(parts):
            copies.append(
                pltpu.make_async_copy(src.at[rows[0] : rows[1], :], dest.at[:, lo:hi], sem.at[3 * n + i])
            )
    for copy in copies:
        copy.start()
    copies[0].wait()
    minv = chol_inverse(head[:, :128], 0)
    copies[1].wait()
    copies[2].wait()
    panel_out(head[...], 0, y_ref, z_ref, m_ref, minv)
    for copy in copies[3:]:
        copy.wait()


def leaf_next_kernel(j, rest_ref, *refs):
    ys, zs, outs = refs[:j], refs[j : 2 * j], refs[2 * j :]
    base = lanes_from(j)
    before = jnp.concatenate(
        [jnp.concatenate([zs[i][:, base - lanes_from(i) :], ys[i][...]], axis=1) for i in range(j)], axis=0
    )
    c0 = R * j - base
    rows = rest_ref[R * (j - 1) : R * j, base:] - mm_t(before[:, c0 : c0 + R], before)
    panel_out(rows, j, *outs)


def back_kernel(*refs):
    ys, zs, ms, w_ref = refs[:4], refs[4:8], refs[8:12], refs[12]
    for j in range(3, -1, -1):
        o = R - (R * j - lanes_from(j))
        rhs = ys[j][...]
        if j < 3:
            z = zs[j][:, R * (j + 1) - lanes_from(j) :]
            rhs = rhs - mm(z, w_ref[R * (j + 1) :, :])
        w_ref[R * j : R * j + R, :] = mm_t(ms[j][...], rhs)[o : o + R, :]


def gram_pair(y, pair):
    st = 128 * pair
    return mm_t(y[:, st : st + 128], y[:, st:])


def row_block(grams, level):
    h = R * ((level - 1) % 2)
    return grams[(level - 1) // 2][h : h + R, :]


def pack(first, blocks):
    host, guest = shared(first)
    out = dict(blocks)
    if host:
        lane = lax.broadcasted_iota(jnp.int32, (R, 128), 1)
        moved = pltpu.roll(blocks[guest][:, :128], R, 1)
        tile = jnp.where(lane < R, moved, blocks[host][:, :128])
        out[host] = jnp.concatenate([tile, blocks[host][:, 128:]], axis=1)
        out[guest] = blocks[guest][:, 128:]
    return out


def packed(first, value, level):
    o = offsets(first)[0][level]
    if isinstance(value, tuple):
        if level == first:
            return value[0][...]
        value, o = value[1], o - width_in(first, first)
    return value[:, o : o + width_in(first, level)]


def unpack(first, value, level):
    host, guest = shared(first)
    if level != guest:
        return value(level)
    return jnp.concatenate([pltpu.roll(value(host)[:, :128], R, 1), value(level)], axis=1)


def put(ref, first, level, value):
    o = offsets(first)[0][level]
    if isinstance(ref, tuple):
        if level == first:
            ref[0][...] = value
            return
        ref, o = ref[1], o - width_in(first, first)
    ref[:, o : o + width_in(first, level)] = value


def gram_pairs(y_refs, pairs):
    y = jnp.concatenate([y_ref[...] for y_ref in y_refs], axis=0)
    return {pair: gram_pair(y, pair) for pair in pairs}


def gram_kernel(*refs):
    *y_refs, near_ref, far_ref = refs
    grams = gram_pairs(y_refs, range(4))
    for level in range(1, SPLIT + 1):
        put(near_ref, 1, level, row_block(grams, level))
    first = SPLIT + 1
    blocks = pack(first, {level: row_block(grams, level) for level in range(first, LEVELS + 1)})
    for level, value in blocks.items():
        put(far_ref, first, level, value)


def factor(k, coupling_ref, rows):
    o = R * ((k - 1) % 2)
    ids0 = lax.broadcasted_iota(jnp.int32, (R, 128), 0)
    ids1 = lax.broadcasted_iota(jnp.int32, (R, 128), 1)
    weights = 1.0 / coupling_ref[k - 1 : k, :]
    weights = jnp.concatenate([weights, weights], axis=1)
    cap = rows[:, :128] + jnp.where(ids0 + o == ids1, jnp.broadcast_to(weights, (R, 128)), 0.0)
    return chol_inverse(cap, o)


def reduce_level(k, coupling_ref, rows, p_ref, m_ref):
    minv = factor(k, coupling_ref, rows)
    m_ref[...] = minv
    p = mm(minv, jnp.concatenate([rows, rows], axis=0))
    p_ref[...] = p
    return p


def schur(k, p, first, last):
    sk = start_of(k)
    grams = {}
    for pair in range((first - 1) // 2, (last + 1) // 2):
        st = 128 * pair
        grams[pair] = mm_t(p[:, st - sk : st - sk + 128], p[:, st - sk :])
    return grams


def next_level(k, p, trailing, n_ref):
    first, last = k + 1, last_of(k)
    if k >= last:
        return
    grams = schur(k, p, first, last)
    less = {level: row_block(grams, level) for level in range(first, last + 1)}
    if shared(first)[0] and shared(first) == shared(k):
        less = pack(first, less)
        blocks = {level: trailing(level) - less[level] for level in less}
    else:
        blocks = pack(first, {level: unpack(k, trailing, level) - less[level] for level in less})
    for level, value in blocks.items():
        put(n_ref, first, level, value)


def on_core0():
    return lax.rem(lax.axis_index("group"), 2) == 0


def next_half(n_ref, h_ref):
    h_ref[...] = jnp.where(on_core0(), n_ref[: R // 2, :], n_ref[R // 2 :, :])


def first_level_kernel(c_ref, own_ref, *refs):
    *y_refs, dep_ref, p_ref, m_ref, n_ref, n2_ref = refs
    grams = gram_pairs(y_refs, range(SPLIT // 2))

    def part(level):
        return packed(1, own_ref, level) + row_block(grams, level)

    p = reduce_level(1, c_ref, part(1), p_ref, m_ref)
    next_level(1, p, part, (n_ref, n2_ref))


def level_kernel(k, c_ref, own_ref, got_ref, dep_ref, dep2_ref, p_ref, m_ref, n_ref=None, h_ref=None):
    def part(level):
        return packed(k, own_ref, level) + packed(k, got_ref, level)

    p = reduce_level(k, c_ref, part(k), p_ref, m_ref)
    next_level(k, p, part, n_ref)
    if h_ref is not None:
        next_half(n_ref, h_ref)


def head_kernel(k, c_ref, own_ref, got_ref, dep_ref, dep2_ref, p_ref, m_ref):
    reduce_level(k, c_ref, own_ref[...] + got_ref[...], p_ref, m_ref)


def tail_kernel(k, own_ref, own2_ref, got_ref, got2_ref, p_ref, *n_refs):
    def part(level):
        return packed(k, (own_ref, own2_ref), level) + packed(k, (got_ref, got2_ref), level)

    next_level(k, p_ref[...], part, n_refs if len(n_refs) > 1 else n_refs[0])


def halves_level_kernel(k, c_ref, own_ref, got_ref, other_ref, dep_ref, p_ref, m_ref, n_ref, h_ref=None):
    core0 = on_core0()

    def part(level):
        mine, theirs = packed(k, got_ref, level), packed(k, other_ref, level)
        got = [jnp.where(core0, mine, theirs), jnp.where(core0, theirs, mine)]
        return packed(k, own_ref, level) + jnp.concatenate(got, axis=0)

    p = reduce_level(k, c_ref, part(k), p_ref, m_ref)
    next_level(k, p, part, n_ref)
    if h_ref is not None:
        next_half(n_ref, h_ref)


def first_far_kernel(own_ref, *refs):
    *y_refs, p_ref, n_ref = refs
    first = SPLIT + 1
    grams = gram_pairs(y_refs, range(SPLIT // 2, LEVELS // 2))
    less = schur(1, p_ref[...], first, LEVELS)
    more = {level: row_block(grams, level) - row_block(less, level) for level in range(first, LEVELS + 1)}
    for level, value in pack(first, more).items():
        put(n_ref, first, level, packed(first, own_ref, level) + value)


def less_kernel(k, own_ref, p_ref, n_ref):
    first = SPLIT + 1
    less = schur(k, p_ref[...], first, LEVELS)
    for level, value in pack(first, {level: row_block(less, level) for level in range(first, LEVELS + 1)}).items():
        put(n_ref, first, level, packed(first, own_ref, level) - value)


def add_kernel(own_ref, got_ref, n_ref):
    n_ref[...] = own_ref[...] + got_ref[...]


def apply_level(k, w, p, minv):
    o = R * ((k - 1) % 2)
    cut = (start_of(k + 1) if k < LEVELS else LEVELS * R) - start_of(k)
    coef = mm_t(minv, p[:, cut:])[R - o : 2 * R - o, :]
    return w[:, cut:] - mm(w[:, o : o + R], coef)


def apply_kernel(k, w_ref, p_ref, m_ref, o_ref):
    o_ref[...] = apply_level(k, w_ref[...], p_ref[...], m_ref[...])


def apply_two_kernel(w_ref, p_ref, m_ref, p2_ref, m2_ref, o_ref):
    two = 2 * R
    coef = mm_t(m_ref[...], p_ref[...])[R:, :]
    coef2 = mm_t(m2_ref[...], p2_ref[:, two:])[:R, :]
    coef = jnp.concatenate([coef[:, two:] - mm(coef[:, R:two], coef2), coef2], axis=0)
    o_ref[...] = w_ref[:, two:] - mm(w_ref[:, :two], coef)


def last_kernel(k, c_ref, own_ref, got_ref, w_ref, o_ref):
    o = R * ((k - 1) % 2)
    rows = own_ref[...] + got_ref[...]
    minv = factor(k, c_ref, rows)[:, R - o : 2 * R - o]
    left = lax.dot_general(
        w_ref[:, o : o + R], minv, (((1,), (1,)), ((), ())), precision=HI, preferred_element_type=F32
    )
    o_ref[...] = w_ref[:, 128:] - mm(left, mm(minv, rows[:, 128:]))


def call(kernel, outs, *args, hbm=(), scratch=(), sems=0, flops=10_000_000):
    vm = pl.BlockSpec(memory_space=pltpu.VMEM)
    hb = pl.BlockSpec(memory_space=pl.ANY)
    shapes = [jax.ShapeDtypeStruct(s, F32) for s in outs]
    extra = [pltpu.SemaphoreType.DMA((sems,))] if sems else []
    return pl.pallas_call(
        kernel,
        out_shape=shapes,
        in_specs=[hb if i in hbm else vm for i in range(len(args))],
        out_specs=[vm] * len(shapes),
        scratch_shapes=[pltpu.VMEM(s, F32) for s in scratch] + extra,
        compiler_params=pltpu.CompilerParams(vmem_limit_bytes=16 << 20),
        cost_estimate=pl.CostEstimate(flops=flops, bytes_accessed=1_000_000, transcendentals=0),
    )(*args)


def exchange(value, level):
    axis = "inner" if level <= 4 else "group"
    mask = {1: 1, 2: 3, 3: 4, 4: 12, 5: 1, 6: 2, 7: 4, 8: 12}[level]
    return lax.ppermute(value, axis, [(s, s ^ mask) for s in range(lax.axis_size(axis))])


def per_device(leaf_blocks, bases, targets, coupling):
    leaf_blocks, bases, targets = (
        pltpu.with_memory_space_constraint(a, pltpu.HBM) for a in (leaf_blocks, bases, targets)
    )
    ys, zs, ms, got_y = [], [], [], []
    for j in range(4):
        outs = [(R, WIDTH), (R, M - lanes_from(j)), (R, 128)]
        if j == 0:
            y, z, m, rest = call(
                leaf_kernel, outs + [(M - R, M + WIDTH)], leaf_blocks, bases, targets,
                hbm=(0, 1, 2), scratch=[(R, M + WIDTH)], sems=6,
            )
        else:
            kernel = lambda *refs, j=j: leaf_next_kernel(j, *refs)
            y, z, m = call(kernel, outs, rest, *ys, *zs)
        ys.append(y)
        zs.append(z)
        ms.append(m)
        got_y.append(exchange(y, 1))
    far_shape = (R, offsets(SPLIT + 1)[1])
    near, far = call(gram_kernel, [(R, offsets(1)[1]), far_shape], *ys, *got_y[:2])
    (w,) = call(back_kernel, [(M, WIDTH)], *ys, *zs, *ms)
    got = far_got = None
    dep = w
    for k in range(1, LEVELS):
        outs = [(R, width_of(k)), (R, 128)]
        following = []
        if k != SPLIT:
            head, total = width_in(k + 1, k + 1), offsets(k + 1)[1]
            following = [(R, head), (R, total - head)] if k + 1 < SPLIT else [(R, total)]
        if k + 1 in HALVED:
            following.append((R // 2, offsets(k + 1)[1]))
        if k == 1:
            p, minv, *near = call(first_level_kernel, outs + following, coupling, near, *got_y[2:], dep, hbm=(4,))
        elif k < SPLIT:
            kernel = lambda *refs, k=k: head_kernel(k, *refs)
            p, minv = call(kernel, outs, coupling, near[0], got[0], dep, far, hbm=(3, 4))
            kernel = lambda *refs, k=k: tail_kernel(k, *refs)
            near = call(kernel, following, *near, *got, p)
        elif k in HALVED:
            kernel = lambda *refs, k=k: halves_level_kernel(k, *refs)
            p, minv, *near = call(kernel, outs + following, coupling, near[0], got, other, dep, hbm=(4,))
        else:
            kernel = lambda *refs, k=k: level_kernel(k, *refs)
            p, minv, *near = call(kernel, outs + following, coupling, near[0], got, dep, far, hbm=(3, 4))
        if k + 1 < SPLIT:
            got = [exchange(near[0], k + 1), exchange(near[1], k + 1)]
        elif k + 1 == SPLIT:
            got = exchange(near[0], k + 1)
        if k == 1:
            (far,) = call(first_far_kernel, [far_shape], far, *got_y[2:], p)
        elif k <= SPLIT:
            kernel = lambda *refs, k=k: less_kernel(k, *refs)
            (far,) = call(kernel, [far_shape], far, p)
            (far,) = call(add_kernel, [far_shape], far, far_got)
        if k < SPLIT:
            far_got = exchange(far, k + 1)
        if k == SPLIT:
            near = [far]
        if k + 1 in HALVED:
            got = exchange(near[1], k + 1)
            other = exchange(got, SPLIT + 1)
        elif k >= SPLIT:
            got = exchange(near[0], k + 1)
        if k == LEVELS - 1:
            kernel = lambda *refs, k=k: apply_kernel(k, *refs)
            (w,) = call(kernel, [(M, width_of(k + 1))], w, p, minv)
        elif k % 2 == 0:
            (w,) = call(apply_two_kernel, [(M, width_of(k + 1))], w, *before, p, minv)
        before = (p, minv)
        if k > SPLIT:
            dep = w
    kernel = lambda *refs: last_kernel(LEVELS, *refs)
    return call(kernel, [(M, NRHS)], coupling, near[0], got, w)[0]


def solution(mesh):
    in_specs = (
        P(("group", "inner"), None),
        P(("group", "inner"), None),
        P(("group", "inner"), None),
        P(),
    )
    out_specs = P(("group", "inner"), None)
    return jax.shard_map(per_device, mesh=mesh, in_specs=in_specs, out_specs=out_specs, check_vma=False)
```
